32 devices in a mesh: stack: 2 (over x), scene: 16 (over z, y, core).
Axes of the slice: x: 2, y: 2, z: 4, core: 2. Of those that a mesh axis runs over, the one named last changes fastest.
Arguments:
- raw_echoes: bfloat16 [4096, 2, 4, 512], P('scene', None, 'stack'), parts along dimension 2, may hold values from -6 to 6
- azimuth_phase: float32 [8192, 512], P('stack', 'scene'), parts along dimension 0, may hold values from -3.140625 to 3.140625
- band_offset: int32 [1024], P(('stack', 'scene')), parts along dimension 0, may hold values from 0 to 8, as said below
- partners: int32 [2, 2], P('stack'), parts along dimension 0, may hold values from 0 to 0, as said below
Outputs:
- goldstein: bfloat16 [4, 1024, 2, 512], P('stack', None, None, 'scene'), parts along dimension 0
The draws below stay inside these ranges and needn't reach their ends.
There are 2 independent parts, one for each index of `stack`. The reference program is written for one: setup_inputs(seed, part) draws one part's arguments, and reference() takes and returns one part's arrays. A program takes and returns all parts, laid end to end along the dimension named above; each array names one. Nothing has to cross between parts.
Inputs may be any that keep to these rules, and one draw needn't show every extreme that they name: `partners`: row i names two dates that precede date i + 1, each from 0 to i, possibly equal; the last row's first entry is 0. `band_offset`: both 0 and 8 occur among the range bins.
All inputs are finite; a program needn't handle non-finite values.
Results may differ from the reference program's by a relative error of at most 0.023.
Values may be sent and summed in bfloat16 or wider, within the bound.
A program may use at most 128 MiB of HBM per device.

```python
import math
import jax
import jax.numpy as jnp
from jax import lax

AZ = 4096
SPLIT = 64
DATES = 2
LOOKS = 4
PATCH = 64
SHIFT = 8
RG = 512
PAIRS = 2


def draw_band_offset(key, part):
    first_key, second_key = jax.random.split(jax.random.fold_in(key, 11), 2)
    values = jax.random.randint(first_key, (RG,), 0, SHIFT + 1)
    spots = jax.random.permutation(second_key, RG)
    places = jnp.arange(RG, dtype=jnp.int32)
    values = jnp.where(places == spots[0], SHIFT, values)
    values = jnp.where(places == spots[1], 0, values)
    return values.astype(jnp.int32)


def draw_partners(key, part):
    noise = jax.random.randint(jax.random.fold_in(key, 23), (DATES - 1, 2), 0, 1 << 20)
    rows_index = jnp.arange(DATES - 1, dtype=jnp.int32)[:, None]
    cols_index = jnp.arange(2, dtype=jnp.int32)[None, :]
    picks = noise % (rows_index + 1)
    picks = jnp.where((rows_index == DATES - 2) & (cols_index == 0), DATES - 2, picks)
    return picks.astype(jnp.int32)


def levels(stream_key, extent, shards, least, largest):
    gain, own = 1.0, jax.random.fold_in(stream_key, 6)
    for dim, shards_of in shards:
        draws = jnp.exp(jax.random.uniform(jax.random.fold_in(own, dim), (shards_of,), jnp.float32, least / len(shards), largest / len(shards)))
        gain = gain * jnp.repeat(draws, extent[dim] // shards_of).reshape([-1 if axis == dim else 1 for axis in range(len(extent))])
    return gain


def centred(rng, shape, deviation, limit, shards=(), kind=jnp.bfloat16):
    factor_of = levels(rng, shape, shards, -0.22, 0.18) if shards else 1.0
    entries = jax.random.normal(rng, shape, jnp.float32) * deviation * factor_of
    return jnp.minimum(jnp.maximum(entries, -limit), limit).astype(kind)


def setup_inputs(seed: int = 0, part: int = 0) -> dict:
    seeds = jax.random.split(jax.random.key(seed), 5)
    own_keys = jax.random.split(jax.random.fold_in(seeds[4], part), 5)
    raw_echoes = centred(own_keys[0], (AZ, 2, DATES, RG), 1.0, 6.0, ((0, 16),))
    azimuth_phase = jnp.clip(jax.random.uniform(own_keys[1], (AZ, RG), jnp.float32, -3.140625, 3.140625), -3.140625, 3.140625)
    band_offset = draw_band_offset(jax.random.fold_in(jax.random.fold_in(seeds[4], part), 71), part)
    partners = draw_partners(jax.random.fold_in(jax.random.fold_in(seeds[4], part), 71), part)
    return {"raw_echoes": raw_echoes, "azimuth_phase": azimuth_phase, "band_offset": band_offset, "partners": partners}


epsilon = 1e-06

def dft_tables(size):
    position = jnp.arange(size, dtype=jnp.int32)
    phase_angle = (position[:, None] * position[None, :] % size).astype(jnp.float32) * (2.0 * math.pi / size)
    return (jnp.cos(phase_angle).astype(jnp.bfloat16), jnp.sin(phase_angle).astype(jnp.bfloat16))

def twiddles(size):
    position = jnp.arange(size, dtype=jnp.int32)
    phase_angle = (position[:, None] * position[None, :] % (size * size)).astype(jnp.float32) * (2.0 * math.pi / (size * size))
    return (jnp.cos(phase_angle), jnp.sin(phase_angle))

def dft_segment(cos_table, sin_table, data, pattern, direction):
    values = data.astype(jnp.float32)
    cos_part = jnp.einsum(pattern, cos_table.astype(jnp.float32), values, precision=lax.Precision.HIGHEST)
    sin_part = jnp.einsum(pattern, sin_table.astype(jnp.float32), values, precision=lax.Precision.HIGHEST)
    real_part = cos_part[:, :, 0] + direction * sin_part[:, :, 1]
    imag_part = cos_part[:, :, 1] - direction * sin_part[:, :, 0]
    return (real_part, imag_part)

def apply_twiddle(real_part, imag_part, direction):
    twist_cos, twist_sin = twiddles(SPLIT)
    tail_shape = (1,) * (real_part.ndim - 2)
    twist_cos = twist_cos.reshape(twist_cos.shape + tail_shape)
    twist_sin = twist_sin.reshape(twist_sin.shape + tail_shape)
    real_out = real_part * twist_cos + direction * imag_part * twist_sin
    imag_out = imag_part * twist_cos - direction * real_part * twist_sin
    return jnp.stack([real_out, imag_out], axis=2).astype(jnp.bfloat16)

def forward_azimuth(signal):
    cos_table, sin_table = dft_tables(SPLIT)
    grid_view = signal.reshape((SPLIT, SPLIT) + signal.shape[1:])
    real_part, imag_part = dft_segment(cos_table, sin_table, grid_view, 'kp,pqcdr->kqcdr', 1.0)
    segmented = apply_twiddle(real_part, imag_part, 1.0)
    real_part, imag_part = dft_segment(cos_table, sin_table, segmented, 'mq,kqcdr->kmcdr', 1.0)
    result = jnp.stack([real_part, imag_part], axis=2) * (1.0 / SPLIT)
    return result.astype(jnp.bfloat16).reshape(signal.shape)

def inverse_azimuth(spectrum):
    cos_table, sin_table = dft_tables(SPLIT)
    grid_view = spectrum.reshape((SPLIT, SPLIT) + spectrum.shape[1:])
    real_part, imag_part = dft_segment(cos_table, sin_table, grid_view, 'qm,kmcdr->kqcdr', -1.0)
    segmented = apply_twiddle(real_part, imag_part, -1.0)
    real_part, imag_part = dft_segment(cos_table, sin_table, segmented, 'pk,kqcdr->pqcdr', -1.0)
    result = jnp.stack([real_part, imag_part], axis=2) * (1.0 / SPLIT)
    return result.astype(jnp.bfloat16).reshape(spectrum.shape)

def doppler_order(phase_table):
    total_rows = phase_table.shape[0]
    return phase_table.reshape(SPLIT, SPLIT, phase_table.shape[1]).transpose(1, 0, 2).reshape(total_rows, phase_table.shape[1])

def migrate(doppler, band, phase_flat):
    total_rows = doppler.shape[0]
    strip_width = doppler.shape[3] - 2 * SHIFT
    flat_index = jnp.arange(total_rows, dtype=jnp.int32)
    natural = flat_index // SPLIT + SPLIT * (flat_index % SPLIT)
    signed = jnp.where(natural < total_rows // 2, natural, natural - total_rows).astype(jnp.float32)
    doppler_ratio = (signed / (total_rows / 2.0)) ** 2
    offset = band.astype(jnp.float32)[None, :] * (doppler_ratio[:, None] - 0.5)
    real_sum = jnp.zeros((total_rows,) + doppler.shape[2:3] + (strip_width,), jnp.float32)
    imag_sum = jnp.zeros((total_rows,) + doppler.shape[2:3] + (strip_width,), jnp.float32)
    for tap_index in range(2 * SHIFT):
        distance = tap_index - SHIFT - offset
        weight = jnp.where(jnp.abs(distance) < SHIFT / 2.0, jnp.sinc(distance) * jnp.cos(math.pi * distance / SHIFT) ** 2, 0.0)
        window = doppler[:, :, :, tap_index:tap_index + strip_width].astype(jnp.float32)
        real_sum = real_sum + weight[:, None, :] * window[:, 0]
        imag_sum = imag_sum + weight[:, None, :] * window[:, 1]
    cos_phase = jnp.cos(phase_flat)[:, None, :]
    sin_phase = jnp.sin(phase_flat)[:, None, :]
    real_out = real_sum * cos_phase - imag_sum * sin_phase
    imag_out = imag_sum * cos_phase + real_sum * sin_phase
    return jnp.stack([real_out, imag_out], axis=1).astype(jnp.bfloat16)

def interfere(leading, trailing):
    leading = leading.astype(jnp.float32)
    trailing = trailing.astype(jnp.float32)
    real_part = leading[:, 0] * trailing[:, 0] + leading[:, 1] * trailing[:, 1]
    imag_part = leading[:, 1] * trailing[:, 0] - leading[:, 0] * trailing[:, 1]
    product = jnp.stack([real_part, imag_part], axis=1)
    looked = product.reshape((product.shape[0] // LOOKS, LOOKS) + product.shape[1:]).mean(axis=1)
    return looked.astype(jnp.bfloat16)

def goldstein(pair_block):
    stride = PATCH // 2
    quarter = PATCH // 4
    padded = jnp.pad(pair_block, ((quarter, quarter), (0, 0), (0, 0)))
    rows_in = padded.shape[0] // stride
    cols_in = padded.shape[2] // stride
    tile_grid = padded.reshape(rows_in, stride, 2, cols_in, stride)
    tile_grid = jnp.concatenate([tile_grid[:-1], tile_grid[1:]], axis=1)
    tile_grid = jnp.concatenate([tile_grid[:, :, :, :-1], tile_grid[:, :, :, 1:]], axis=4)
    cos_table, sin_table = dft_tables(PATCH)
    real_part, imag_part = dft_segment(cos_table, sin_table, tile_grid, 'ku,iucjv->ikcjv', 1.0)
    segmented = jnp.stack([real_part, imag_part], axis=2).astype(jnp.bfloat16)
    real_part, imag_part = dft_segment(cos_table, sin_table, segmented, 'lv,ikcjv->ikcjl', 1.0)
    real_part = real_part * (1.0 / PATCH)
    imag_part = imag_part * (1.0 / PATCH)
    magnitude = jnp.sqrt(real_part * real_part + imag_part * imag_part + epsilon)
    row_sum = magnitude + jnp.roll(magnitude, 1, axis=1) + jnp.roll(magnitude, -1, axis=1)
    smooth = (row_sum + jnp.roll(row_sum, 1, axis=3) + jnp.roll(row_sum, -1, axis=3)) / 9.0
    mean_level = lax.optimization_barrier(jnp.mean(smooth, axis=(1, 3), keepdims=True))
    filter_gain = smooth / (mean_level + epsilon)
    spectrum = jnp.stack([real_part * filter_gain, imag_part * filter_gain], axis=2).astype(jnp.bfloat16)
    central_cos = cos_table[quarter:quarter + stride]
    central_sin = sin_table[quarter:quarter + stride]
    real_part, imag_part = dft_segment(central_cos, central_sin, spectrum, 'uk,ikcjl->iucjl', -1.0)
    segmented = jnp.stack([real_part, imag_part], axis=2).astype(jnp.bfloat16)
    real_part, imag_part = dft_segment(central_cos, central_sin, segmented, 'vl,iucjl->iucjv', -1.0)
    result = jnp.stack([real_part, imag_part], axis=2) * (1.0 / PATCH)
    return result.reshape(pair_block.shape[0], 2, -1).astype(jnp.bfloat16)

def reference(raw_echoes, azimuth_phase, band_offset, partners):
    date_count = raw_echoes.shape[2]
    phase_flat = doppler_order(azimuth_phase)
    quarter = PATCH // 4

    def focus_date(position):
        signal = lax.dynamic_index_in_dim(raw_echoes, position, 2, keepdims=True)
        padded = jnp.pad(signal, ((0, 0), (0, 0), (0, 0), (SHIFT, SHIFT)))
        doppler = forward_azimuth(padded)
        compressed = migrate(doppler, band_offset, phase_flat)
        return inverse_azimuth(compressed)[:, :, 0]
    focused = lax.map(focus_date, jnp.arange(date_count, dtype=jnp.int32))
    later_dates = jnp.repeat(jnp.arange(1, date_count, dtype=jnp.int32), 2)
    earlier_dates = partners.reshape(-1).astype(jnp.int32)

    def one_pair(position):
        leading = lax.dynamic_index_in_dim(focused, later_dates[position], 0, keepdims=False)
        trailing = lax.dynamic_index_in_dim(focused, earlier_dates[position], 0, keepdims=False)
        looked = interfere(leading, trailing)
        pair_block = jnp.pad(looked, ((0, 0), (0, 0), (quarter, quarter)))
        return goldstein(pair_block)
    return lax.map(one_pair, jnp.arange(PAIRS, dtype=jnp.int32))
```

```python
import math

import jax
import jax.numpy as jnp
import numpy as np
from jax import lax
from jax.experimental import pallas as pl
from jax.experimental.pallas import tpu as pltpu
from jax.sharding import PartitionSpec as P

SPLIT = 64
LOOKS = 4
PATCH = 64
SHIFT = 8
TAPS = 2 * SHIFT - 1
EPSILON = 1e-06
STRIP = 32
GROUPS = STRIP // 2
LANES = 2 * SPLIT
CHUNKS = STRIP // 4
HALO_CHUNKS = CHUNKS // 2
HALF = STRIP // 2
EARLY = 12
TABLES = 13
VMEM_LIMIT = 40 * 1024 * 1024


def base_tables():
    k = np.arange(64)
    angle = 2.0 * np.pi * ((k[:, None] * k[None, :]) % 64) / 64.0
    return np.cos(angle), np.sin(angle)


def twiddle_tables():
    k = np.arange(SPLIT)
    angle = 2.0 * np.pi * ((k[:, None] * k[None, :]) % (SPLIT * SPLIT)) / (SPLIT * SPLIT)
    return (
        np.tile(np.cos(angle), (1, 2)).astype(np.float32),
        np.tile(np.sin(angle), (1, 2)).astype(np.float32),
    )


def bf16(table):
    return jnp.asarray(np.asarray(table, np.float32), jnp.bfloat16)


def left_table(direction):
    c, s = base_tables()
    return np.block([[c, direction * s], [-direction * s, c]])


def right_table(direction):
    c, s = base_tables()
    eye = np.eye(2)
    return np.block(
        [
            [np.kron(eye, c), np.kron(eye, -direction * s)],
            [np.kron(eye, direction * s), np.kron(eye, c)],
        ]
    )


def look_table():
    table = np.zeros((4, 2, 2, SPLIT, 2, 4, 2, SPLIT // LOOKS))
    for g in range(4):
        for c in range(2):
            for rb in range(2):
                for q in range(SPLIT):
                    table[g, c, rb, q, rb, g, c, q // LOOKS] = 1.0 / LOOKS
    return table.reshape(4 * 2 * 2 * SPLIT, 2 * 4 * 2 * SPLIT // LOOKS)


def patch_azimuth_table():
    c, s = base_tables()
    table = np.zeros((4, 4, 2, 16, 4, 2, 64))
    for p in range(4):
        part_c, part_s = c[16 * p : 16 * p + 16], s[16 * p : 16 * p + 16]
        for r in range(4):
            table[p, r, 0, :, r, 0] = part_c
            table[p, r, 1, :, r, 0] = part_s
            table[p, r, 0, :, r, 1] = -part_s
            table[p, r, 1, :, r, 1] = part_c
    return table.reshape(512, 512)


def patch_range_table():
    c, s = base_tables()
    return np.concatenate([c, s], axis=1)


def back_azimuth_table():
    c, s = base_tables()
    c, s = c[:, 16:48], s[:, 16:48]
    table = np.zeros((4, 2, 64, 2, 4, 32))
    for i in range(4):
        table[i, 0, :, 0, i] = c
        table[i, 1, :, 0, i] = -s
        table[i, 0, :, 1, i] = s
        table[i, 1, :, 1, i] = c
    return table.reshape(512, 256)


def back_range_table():
    c, s = base_tables()
    c, s = c[16:48], s[16:48]
    return np.block([[c, -s], [s, c]])


def dot(a, b):
    return jnp.dot(a, b, preferred_element_type=jnp.float32)


def lane_order():
    lane = np.arange(SPLIT)
    return 2 * (lane % (SPLIT // 2)) + lane // (SPLIT // 2)


def spectrum_side(table, axis):
    order = np.concatenate([SPLIT * half + lane_order() for half in range(4)])
    return np.take(table, order, axis=axis)


def cos_sin(angle):
    h = 0.5 * angle
    h2 = h * h
    sin_h = 1.0 / 6227020800.0
    for fact in (-39916800.0, 362880.0, -5040.0, 120.0, -6.0, 1.0):
        sin_h = sin_h * h2 + 1.0 / fact
    sin_h = sin_h * h
    cos_h = 1.0 / 479001600.0
    for fact in (-3628800.0, 40320.0, -720.0, 24.0, -2.0, 1.0):
        cos_h = cos_h * h2 + 1.0 / fact
    return 1.0 - 2.0 * sin_h * sin_h, 2.0 * sin_h * cos_h


def make_weights(g, band_ref, lines_ref, weight_ref, cos_ref, sin_ref):
    shape = (SPLIT, LANES)
    lane = lax.broadcasted_iota(jnp.int32, shape, 1)
    row = lax.broadcasted_iota(jnp.int32, shape, 0)
    half = SPLIT // 2
    k = row + SPLIT * (2 * (lane & (half - 1)) + ((lane & half) // half))
    total = SPLIT * SPLIT
    f = jnp.where(k < total // 2, k, k - total).astype(jnp.float32)
    ratio = f * (2.0 / total)
    band = jnp.where(lane < SPLIT, band_ref[g], band_ref[g + GROUPS]).astype(jnp.float32)
    s = band * (ratio * ratio - 0.5)
    n = jnp.floor(s + 0.5)
    y = s - n
    y2 = y * y
    pi = math.pi
    poly = -(pi**11) / 39916800.0
    for power, fact in ((9, 362880.0), (7, -5040.0), (5, 120.0), (3, -6.0), (1, 1.0)):
        poly = poly * y2 + (pi**power) / fact
    odd = n.astype(jnp.int32) & 1
    lobe = jnp.where(odd == 1, 1.0, -1.0) * (y * poly) * (1.0 / pi)
    cos_s, sin_s = cos_sin(s * (pi / 4.0))
    cos_s, sin_s = 0.5 * cos_s, 0.5 * sin_s
    for tap in range(TAPS):
        m = tap + 1 - SHIFT
        x = m - s
        sign = 1.0 if m % 2 == 0 else -1.0
        safe = jnp.where(x == 0.0, 1.0, x)
        sinc = jnp.where(x == 0.0, 1.0, (sign * lobe) / safe)
        window = 0.5 + math.cos(pi * m / 4.0) * cos_s + math.sin(pi * m / 4.0) * sin_s
        weight_ref[g, tap] = jnp.where(jnp.abs(x) < SHIFT / 2.0, sinc * window, 0.0)
    first = lines_ref[pl.ds(g, SPLIT // 2, stride=STRIP)]
    second = lines_ref[pl.ds(g + GROUPS, SPLIT // 2, stride=STRIP)]
    pieces = [first, pltpu.roll(first, SPLIT, 1), second, pltpu.roll(second, SPLIT, 1)]
    angle = jnp.concatenate(pieces, axis=0).T[:SPLIT]
    cos_ref[g], sin_ref[g] = cos_sin(angle)


def arrived_lines(wide_ref, i, sources, local, low):
    rows = []
    for c in range(2):
        for pair in range(wide_ref.shape[1]):
            one = wide_ref[c, pair, pl.ds(i, sources, stride=HALF)]
            two = wide_ref[c, pair, pl.ds(i + SHIFT, sources, stride=HALF)]
            rows.append(jnp.where(low[:sources], one, pltpu.roll(two, SPLIT, 1)))
            if local > 1:
                rows.append(jnp.where(low[:sources], pltpu.roll(one, SPLIT, 1), two))
    return jnp.concatenate(rows, axis=0).astype(jnp.bfloat16)


def scene_kernel(
    band_ref, packed_ref, phase_ref,
    left_ref, right_ref, back_right_ref, back_left_ref, tc_ref, ts_ref, look_ref,
    azimuth_ref, range_ref, back_azimuth_ref, back_range_ref,
    out_ref,
    raw_ref, spread_ref, recv_ref, lines_ref, wide_ref, weight_ref, cos_ref, sin_ref, ext_ref,
    rim_ref, up_ref, down_ref, before_ref, after_ref, focused_ref,
    own_ref, own_before_ref, own_after_ref, line_ref, grid_ref,
    send_sem, recv_sem, local_sem, edge_send, edge_recv, look_send, look_recv,
    loads,
):
    scene = lax.axis_size("scene")
    me = lax.axis_index("scene")
    dates = raw_ref.shape[0]
    lines_held = raw_ref.shape[5]
    local = lines_held // SPLIT
    low = lax.broadcasted_iota(jnp.int32, (SPLIT, LANES), 1) < SPLIT
    patches = SPLIT // 2

    barrier = pltpu.get_barrier_semaphore()

    def greet(o, carry):
        pl.semaphore_signal(
            barrier, inc=1, device_id={"scene": lax.rem(me + o, scene)},
            device_id_type=pl.DeviceIdType.MESH,
        )
        return carry

    lax.fori_loop(1, scene, greet, 0)
    for load in loads:
        load.start()
    loads[0].wait()
    height = packed_ref.shape[0]
    piece = height // 8

    def spread(i, carry):
        rows = pl.ds(pl.multiple_of(i * piece, piece), piece)
        spread_ref[rows] = packed_ref[rows].astype(jnp.float32)
        return carry

    lax.fori_loop(0, 8, spread, 0)
    owners = LANES // STRIP
    tiles = scene // owners
    stride = 2 * tiles * dates

    def turn(d):
        def body(tile, carry):
            for c in range(2):
                start = (c * tiles + tile) * dates + d
                bins = spread_ref[pl.ds(start, lines_held, stride=stride)].T
                for n in range(owners):
                    own = bins[n * STRIP : (n + 1) * STRIP]
                    rim = jnp.concatenate([own[:SHIFT], own[STRIP - SHIFT :]], axis=0)
                    core = own[SHIFT : STRIP - SHIFT]
                    raw_ref[d, 0, tile * owners + n, c] = rim.astype(jnp.bfloat16)
                    raw_ref[d, 1, tile * owners + n, c] = core.astype(jnp.bfloat16)
            return carry

        lax.fori_loop(0, tiles, body, 0)

    turn(0)
    pl.semaphore_wait(barrier, scene - 1)

    def far(i):
        half = (i + 1) // 2
        return scene // 2 + half * (1 - 2 * lax.rem(i, 2))

    def piece_of(ref, k, owner):
        return ref.at[0, :, owner] if k == 0 else ref.at[1, k - 1, owner]

    def strip_copy(k, o):
        peer = lax.rem(me + o, scene)
        return pltpu.make_async_remote_copy(
            src_ref=piece_of(raw_ref, k, peer),
            dst_ref=piece_of(recv_ref, k, me),
            send_sem=send_sem.at[k, o],
            recv_sem=recv_sem.at[k, o],
            device_id={"scene": peer},
            device_id_type=pl.DeviceIdType.MESH,
        )

    def own_copy(k):
        return pltpu.make_async_copy(
            piece_of(raw_ref, k, me), piece_of(recv_ref, k, me), local_sem.at[k]
        )

    def send_all(k):
        def send(i, carry):
            strip_copy(k, far(i)).start()
            return carry

        lax.fori_loop(0, scene - 1, send, 0)
        own_copy(k).start()

    def arrive_all(k):
        def arrive(o, carry):
            strip_copy(k, o).wait_recv()
            return carry

        lax.fori_loop(1, scene, arrive, 0)
        own_copy(k).wait()

    send_all(0)
    for d in range(1, dates):
        turn(d)

    for load in loads[1:]:
        load.wait()

    for part in range(SPLIT // 2):
        lines_ref[pl.ds(part * STRIP, STRIP)] = phase_ref[:, part * LANES : (part + 1) * LANES]

    def weigh(g, carry):
        make_weights(g, band_ref, lines_ref, weight_ref, cos_ref, sin_ref)
        return carry

    lax.fori_loop(0, EARLY, weigh, 0)
    send_all(1)
    lax.fori_loop(EARLY, GROUPS, weigh, 0)

    @pl.when(me == 0)
    def _():
        before_ref[...] = jnp.zeros(before_ref.shape, before_ref.dtype)
        own_before_ref[...] = jnp.zeros(own_before_ref.shape, own_before_ref.dtype)

    @pl.when(me == scene - 1)
    def _():
        after_ref[...] = jnp.zeros(after_ref.shape, after_ref.dtype)
        own_after_ref[...] = jnp.zeros(own_after_ref.shape, own_after_ref.dtype)

    line_ref[...] = jnp.zeros(line_ref.shape, jnp.float32)

    def neighbour(source, target, send, recv, step):
        return pltpu.make_async_remote_copy(
            src_ref=source, dst_ref=target, send_sem=send, recv_sem=recv,
            device_id={"scene": me + step}, device_id_type=pl.DeviceIdType.MESH,
        )

    def edge_copies(d):
        return (
            neighbour(up_ref.at[d], before_ref.at[d], edge_send.at[d, 0], edge_recv.at[d, 0], 1),
            neighbour(down_ref.at[d], after_ref.at[d], edge_send.at[d, 1], edge_recv.at[d, 1], -1),
        )

    def look_copies(big):
        return (
            neighbour(
                own_ref.at[HALO_CHUNKS + big], own_before_ref.at[big],
                look_send.at[big, 0], look_recv.at[big, 0], 1,
            ),
            neighbour(
                own_ref.at[big], own_after_ref.at[big],
                look_send.at[big, 1], look_recv.at[big, 1], -1,
            ),
        )

    def start_pair(copies):
        @pl.when(me < scene - 1)
        def _():
            copies[0].start()

        @pl.when(me > 0)
        def _():
            copies[1].start()

    def wait_pair(copies):
        @pl.when(me > 0)
        def _():
            copies[0].wait_recv()
            copies[1].wait_send()

        @pl.when(me < scene - 1)
        def _():
            copies[1].wait_recv()
            copies[0].wait_send()

    def widen(d, part):
        def body(source, carry):
            start = pl.multiple_of(source * HALF, HALF)
            for c in range(2):
                strip = recv_ref[d, part, source, c].astype(jnp.float32)
                for pair in range(wide_ref.shape[1]):
                    kept = strip[:, pair * LANES : (pair + 1) * LANES]
                    wide_ref[c, pair, pl.ds(start, HALF), : kept.shape[1]] = kept
            return carry

        lax.fori_loop(0, scene, body, 0)

    def transform(i):
        lines = arrived_lines(wide_ref, i, scene, local, low)
        first = dot(left_ref[...], lines)
        re, im = first[:SPLIT], first[SPLIT:]
        tc, ts = tc_ref[...], ts_ref[...]
        segment = jnp.concatenate([re * tc + im * ts, im * tc - re * ts], axis=1)
        second = dot(segment.astype(jnp.bfloat16), right_ref[...]) * (1.0 / SPLIT)
        second = second.astype(jnp.bfloat16).astype(jnp.float32)
        return second[:, :LANES], second[:, LANES:]

    def forward_rim(d):
        widen(d, 0)

        def body(i, carry):
            re, im = transform(i)
            re_turned, im_turned = pltpu.roll(re, SPLIT, 1), pltpu.roll(im, SPLIT, 1)
            rim_ref[d, 0, i] = re
            rim_ref[d, 1, i] = im
            down_ref[d, i] = jnp.where(low, re, im_turned).astype(jnp.bfloat16)
            up_ref[d, i] = jnp.where(low, re_turned, im).astype(jnp.bfloat16)
            return carry

        lax.fori_loop(0, SHIFT, body, 0, unroll=8)
        start_pair(edge_copies(d))

    def forward_core(d):
        widen(d, 1)
        wait_pair(edge_copies(d))

        def body(i, carry):
            before = before_ref[d, i].astype(jnp.float32)
            after = after_ref[d, i].astype(jnp.float32)
            befores = (before, pltpu.roll(before, SPLIT, 1))
            afters = (pltpu.roll(after, SPLIT, 1), after)
            for c, core in enumerate(transform(i)):
                turned = pltpu.roll(core, SPLIT, 1)
                rim = rim_ref[d, c, i]
                ext_ref[c, i] = jnp.where(low, befores[c], turned)
                ext_ref[c, SHIFT + i] = jnp.where(low, rim, core)
                ext_ref[c, 2 * SHIFT + i] = jnp.where(low, core, rim)
                ext_ref[c, 3 * SHIFT + i] = jnp.where(low, turned, afters[c])
            return carry

        lax.fori_loop(0, SHIFT, body, 0, unroll=8)

    def focus(g):
        re_sum = jnp.zeros((SPLIT, LANES), jnp.float32)
        im_sum = jnp.zeros((SPLIT, LANES), jnp.float32)
        for tap in range(TAPS):
            weight = weight_ref[g, tap]
            re_sum += weight * ext_ref[0, g + tap + 1]
            im_sum += weight * ext_ref[1, g + tap + 1]
        cos_phase, sin_phase = cos_ref[g], sin_ref[g]
        compressed = jnp.concatenate(
            [re_sum * cos_phase - im_sum * sin_phase, im_sum * cos_phase + re_sum * sin_phase],
            axis=1,
        ).astype(jnp.bfloat16)
        first = dot(compressed, back_right_ref[...])
        re, im = first[:, :LANES], first[:, LANES:]
        tc, ts = tc_ref[...], ts_ref[...]
        segment = jnp.concatenate([re * tc - im * ts, im * tc + re * ts], axis=0)
        second = dot(back_left_ref[...], segment.astype(jnp.bfloat16)) * (1.0 / SPLIT)
        return second.astype(jnp.bfloat16)

    def focus_first(g, carry):
        focused_ref[g] = focus(g)
        return carry

    def focus_last(big, carry):
        highs, rests = [], []
        for j in range(4):
            g = 4 * big + j
            leading, trailing = focus(g).astype(jnp.float32), focused_ref[g].astype(jnp.float32)
            lr, li = leading[:SPLIT], leading[SPLIT:]
            tr, ti = trailing[:SPLIT], trailing[SPLIT:]
            product = jnp.concatenate([lr * tr + li * ti, li * tr - lr * ti], axis=1)
            high = product.astype(jnp.bfloat16)
            highs.append(high)
            rests.append((product - high.astype(jnp.float32)).astype(jnp.bfloat16))
        high, rest = jnp.concatenate(highs, axis=1), jnp.concatenate(rests, axis=1)
        looked = dot(high, look_ref[...]) + dot(rest, look_ref[...])
        own_ref[big] = looked[:, :LANES].astype(jnp.bfloat16)
        own_ref[HALO_CHUNKS + big] = looked[:, LANES:].astype(jnp.bfloat16)
        start_pair(look_copies(big))
        return carry

    arrive_all(0)
    forward_rim(0)
    send_all(2)
    arrive_all(1)
    forward_rim(1)
    forward_core(0)
    lax.fori_loop(0, GROUPS, focus_first, 0, unroll=8)
    arrive_all(2)
    forward_core(1)
    lax.fori_loop(0, GROUPS // 4, focus_last, 0, unroll=2)

    def lines_of(first_chunk, count):
        def forward_lines(step, carry):
            rows = []
            for j in range(4):
                chunk = first_chunk + 4 * step + j
                rows.append(
                    jnp.concatenate(
                        [line_ref[chunk, pl.ds(p, patches, stride=2)] for p in range(4)], axis=1
                    )
                )
            lines = jnp.concatenate(rows, axis=0).astype(jnp.bfloat16)
            result = dot(lines, azimuth_ref[...]).astype(jnp.bfloat16).astype(jnp.float32)
            for j in range(4):
                for r in range(4):
                    start = ((first_chunk + 4 * step + j) * 4 + r) * patches
                    grid_ref[pl.ds(pl.multiple_of(start, patches), patches)] = result[
                        j * patches : (j + 1) * patches, r * LANES : (r + 1) * LANES
                    ]
            return carry

        lax.fori_loop(0, count // 4, forward_lines, 0)

    for j in range(CHUNKS):
        line_ref[HALO_CHUNKS + j, pl.ds(1, SPLIT)] = own_ref[j].astype(jnp.float32)
    lines_of(HALO_CHUNKS, CHUNKS)
    for big in range(HALO_CHUNKS):
        wait_pair(look_copies(big))
    for j in range(HALO_CHUNKS):
        line_ref[j, pl.ds(1, SPLIT)] = own_before_ref[j].astype(jnp.float32)
        line_ref[HALO_CHUNKS + CHUNKS + j, pl.ds(1, SPLIT)] = own_after_ref[j].astype(jnp.float32)
    lines_of(0, HALO_CHUNKS)
    lines_of(HALO_CHUNKS + CHUNKS, HALO_CHUNKS)
    sign = jnp.where(low, 1.0, -1.0)

    def filter_patches(step, carry):
        tiles = []
        for j in range(4):
            tile = grid_ref[pl.ds(4 * step + j, PATCH, stride=patches)]
            swapped = pltpu.roll(tile, PATCH, 1) * sign
            tiles.append(jnp.concatenate([tile, swapped], axis=0).astype(jnp.bfloat16))
        spectra = dot(range_ref[...], jnp.concatenate(tiles, axis=1)) * (1.0 / PATCH)
        kept = []
        for j in range(4):
            spectrum = spectra[:, j * LANES : (j + 1) * LANES]
            power = spectrum * spectrum
            magnitude = jnp.sqrt(power + pltpu.roll(power, PATCH, 1) + EPSILON)
            row_sum = (
                magnitude
                + pltpu.roll(magnitude, 1, 0)
                + pltpu.roll(magnitude, PATCH - 1, 0)
            )
            smooth = (row_sum + pltpu.roll(row_sum, 1, 1) + pltpu.roll(row_sum, LANES - 1, 1)) * (
                1.0 / 9.0
            )
            level = jnp.sum(jnp.sum(magnitude, axis=0, keepdims=True), axis=1, keepdims=True)
            level = level * (1.0 / (PATCH * LANES)) + EPSILON
            kept.append((spectrum * (smooth / level)).astype(jnp.bfloat16))
        back = dot(jnp.concatenate(kept, axis=1), back_azimuth_ref[...]).astype(jnp.bfloat16)
        stacked = jnp.concatenate([back[:, :LANES], back[:, LANES:]], axis=0)
        result = (dot(back_range_ref[...], stacked) * (1.0 / PATCH)).astype(jnp.bfloat16)
        start = pl.multiple_of(step * LANES, LANES)
        out_ref[:, pl.ds(start, LANES)] = result
        return carry

    lax.fori_loop(0, patches // 4, filter_patches, 0, unroll=4)

    for k in range(dates + 1):

        def sent(o, carry):
            strip_copy(k, o).wait_send()
            return carry

        lax.fori_loop(1, scene, sent, 0)


def loading_kernel(band_ref, *refs):
    held, out_ref, kept, load_sem = refs[:TABLES], refs[TABLES], refs[TABLES + 1 : -1], refs[-1]
    loads = [
        pltpu.make_async_copy(source, target, load_sem.at[i])
        for i, (source, target) in enumerate(zip(held, kept[:TABLES]))
    ]
    scene_kernel(band_ref, *kept[:TABLES], out_ref, *kept[TABLES:], loads)


def run_scene(raw, band, phase, left, scene, shape):
    dates, width = shape[1], shape[3]
    looks = SPLIT * SPLIT // LOOKS
    tc, ts = twiddle_tables()
    vmem = pl.BlockSpec(memory_space=pltpu.VMEM)
    plane = (GROUPS, SPLIT, LANES)
    edge = pltpu.VMEM((dates, SHIFT, SPLIT, LANES), jnp.bfloat16)
    looked_edge = pltpu.VMEM((HALO_CHUNKS, SPLIT, LANES), jnp.bfloat16)
    dma = pltpu.SemaphoreType.DMA
    tables = (
        raw, phase, bf16(left), bf16(spectrum_side(right_table(1.0), 1)),
        bf16(spectrum_side(right_table(-1.0), 0)), bf16(left_table(-1.0)),
        jnp.asarray(tc), jnp.asarray(ts), bf16(look_table()),
        bf16(patch_azimuth_table()), bf16(patch_range_table()),
        bf16(back_azimuth_table()), bf16(back_range_table()),
    )
    return pl.pallas_call(
        loading_kernel,
        in_specs=[pl.BlockSpec(memory_space=pltpu.SMEM)]
        + [pl.BlockSpec(memory_space=pl.ANY)] * TABLES,
        out_specs=vmem,
        out_shape=pltpu.VMEM((2 * STRIP, looks), jnp.bfloat16),
        scratch_shapes=[pltpu.VMEM(table.shape, table.dtype) for table in tables]
        + [
            pltpu.VMEM((dates, 2, scene, 2, HALF, width), jnp.bfloat16),
            pltpu.VMEM(raw.shape, jnp.float32),
            pltpu.VMEM((dates, 2, scene, 2, HALF, width), jnp.bfloat16),
            pltpu.VMEM((STRIP * SPLIT // 2, LANES), jnp.float32),
            pltpu.VMEM((2, pl.cdiv(width, LANES), scene * HALF, LANES), jnp.float32),
            pltpu.VMEM((GROUPS, TAPS, SPLIT, LANES), jnp.float32),
            pltpu.VMEM(plane, jnp.float32),
            pltpu.VMEM(plane, jnp.float32),
            pltpu.VMEM((2, GROUPS + 2 * SHIFT, SPLIT, LANES), jnp.float32),
            pltpu.VMEM((dates, 2, SHIFT, SPLIT, LANES), jnp.float32),
            edge, edge, edge, edge,
            pltpu.VMEM((GROUPS, 2 * SPLIT, LANES), jnp.bfloat16),
            pltpu.VMEM((CHUNKS, SPLIT, LANES), jnp.bfloat16),
            looked_edge,
            looked_edge,
            pltpu.VMEM((2 * CHUNKS, SPLIT + 8, LANES), jnp.float32),
            pltpu.VMEM((PATCH * SPLIT // 2, LANES), jnp.float32),
            dma((dates + 1, scene)), dma((dates + 1, scene)), dma((dates + 1,)),
            dma((dates, 2)), dma((dates, 2)),
            dma((HALO_CHUNKS, 2)), dma((HALO_CHUNKS, 2)), dma((TABLES,)),
        ],
        compiler_params=pltpu.CompilerParams(
            vmem_limit_bytes=VMEM_LIMIT, collective_id=0, has_side_effects=True
        ),
        name="scene",
    )(*[pltpu.with_memory_space_constraint(t, pltpu.HBM) for t in (band, *tables)])


def on_device(raw_echoes, azimuth_phase, band_offset, partners):
    scene = lax.axis_size("scene")
    dates = raw_echoes.shape[2]
    local = raw_echoes.shape[0] // SPLIT
    pairs = partners.size
    assert dates == 2 and raw_echoes.shape[3] == scene * STRIP
    left = left_table(1.0).reshape(2 * SPLIT, 2, scene, local)
    left = left.transpose(0, 1, 3, 2).reshape(2 * SPLIT, 2 * SPLIT)
    lines, bins = raw_echoes.shape[0], raw_echoes.shape[3]
    raw = raw_echoes.reshape(lines, 2, dates, bins // LANES, LANES)
    raw = raw.transpose(0, 1, 3, 2, 4).reshape(-1, LANES)
    phase = azimuth_phase.T
    result = run_scene(
        raw, band_offset, phase, left, scene, (2, dates, bins, lines)
    )
    result = jnp.broadcast_to(result, (pairs,) + result.shape)
    return result.reshape(pairs, 2, STRIP, -1).transpose(0, 3, 1, 2)


def solution(mesh):
    return jax.shard_map(
        on_device,
        mesh=mesh,
        in_specs=(
            P("scene", None, "stack", None),
            P("stack", "scene"),
            P(("stack", "scene")),
            P("stack", None),
        ),
        out_specs=P("stack", None, None, "scene"),
        check_vma=False,
    )
```

```python
import math

import jax
import jax.numpy as jnp
import numpy as np
from jax import lax
from jax.experimental import pallas as pl
from jax.experimental.pallas import tpu as pltpu
from jax.sharding import PartitionSpec as P

SPLIT = 64
LOOKS = 4
PATCH = 64
SHIFT = 8
TAPS = 2 * SHIFT - 1
EPSILON = 1e-06
STRIP = 32
GROUPS = STRIP // 2
LANES = 2 * SPLIT
CHUNKS = STRIP // 4
HALO_CHUNKS = CHUNKS // 2
HALF = STRIP // 2
BATCH = 8
STEPS = 4
TABLES = 13
VMEM_LIMIT = 40 * 1024 * 1024


def base_tables():
    k = np.arange(64)
    angle = 2.0 * np.pi * ((k[:, None] * k[None, :]) % 64) / 64.0
    return np.cos(angle), np.sin(angle)


def twiddle_tables():
    k = np.arange(SPLIT)
    angle = 2.0 * np.pi * ((k[:, None] * k[None, :]) % (SPLIT * SPLIT)) / (SPLIT * SPLIT)
    return (
        np.tile(np.cos(angle), (1, 2)).astype(np.float32),
        np.tile(np.sin(angle), (1, 2)).astype(np.float32),
    )


def bf16(table):
    return jnp.asarray(np.asarray(table, np.float32), jnp.bfloat16)


def left_table(direction):
    c, s = base_tables()
    return np.block([[c, direction * s], [-direction * s, c]])


def right_table(direction):
    c, s = base_tables()
    eye = np.eye(2)
    return np.block(
        [
            [np.kron(eye, c), np.kron(eye, -direction * s)],
            [np.kron(eye, direction * s), np.kron(eye, c)],
        ]
    )


def look_table():
    table = np.zeros((4, 2, 2, SPLIT, 2, 4, 2, SPLIT // LOOKS))
    for g in range(4):
        for c in range(2):
            for rb in range(2):
                for q in range(SPLIT):
                    table[g, c, rb, q, rb, g, c, q // LOOKS] = 1.0 / LOOKS
    return table.reshape(4 * 2 * 2 * SPLIT, 2 * 4 * 2 * SPLIT // LOOKS)


def patch_azimuth_table():
    c, s = base_tables()
    table = np.zeros((4, 4, 2, 16, 4, 2, 64))
    for p in range(4):
        part_c, part_s = c[16 * p : 16 * p + 16], s[16 * p : 16 * p + 16]
        for r in range(4):
            table[p, r, 0, :, r, 0] = part_c
            table[p, r, 1, :, r, 0] = part_s
            table[p, r, 0, :, r, 1] = -part_s
            table[p, r, 1, :, r, 1] = part_c
    return table.reshape(512, 512)


def patch_range_table():
    c, s = base_tables()
    return np.block([[c, s], [-s, c]])


def back_azimuth_table():
    c, s = base_tables()
    c, s = c[:, 16:48], s[:, 16:48]
    table = np.zeros((2, 4, 64, 2, 4, 32))
    for i in range(4):
        table[0, i, :, 0, i] = c
        table[1, i, :, 0, i] = -s
        table[0, i, :, 1, i] = s
        table[1, i, :, 1, i] = c
    return table.reshape(512, 256)


def back_range_table():
    c, s = base_tables()
    c, s = c[16:48], s[16:48]
    return np.block([[c, -s], [s, c]])


def dot(a, b):
    return jnp.dot(a, b, preferred_element_type=jnp.float32)


def lane_order():
    lane = np.arange(SPLIT)
    return 2 * (lane % (SPLIT // 2)) + lane // (SPLIT // 2)


def spectrum_side(table, axis):
    order = np.concatenate([SPLIT * half + lane_order() for half in range(4)])
    return np.take(table, order, axis=axis)


def cos_sin(angle):
    h = 0.5 * angle
    h2 = h * h
    sin_h = 1.0 / 6227020800.0
    for fact in (-39916800.0, 362880.0, -5040.0, 120.0, -6.0, 1.0):
        sin_h = sin_h * h2 + 1.0 / fact
    sin_h = sin_h * h
    cos_h = 1.0 / 479001600.0
    for fact in (-3628800.0, 40320.0, -720.0, 24.0, -2.0, 1.0):
        cos_h = cos_h * h2 + 1.0 / fact
    return 1.0 - 2.0 * sin_h * sin_h, 2.0 * sin_h * cos_h


def make_weights(g, band_ref, lines_ref, weight_ref, cos_ref, sin_ref):
    shape = (SPLIT, LANES)
    lane = lax.broadcasted_iota(jnp.int32, shape, 1)
    row = lax.broadcasted_iota(jnp.int32, shape, 0)
    half = SPLIT // 2
    k = row + SPLIT * (2 * (lane & (half - 1)) + ((lane & half) // half))
    total = SPLIT * SPLIT
    f = jnp.where(k < total // 2, k, k - total).astype(jnp.float32)
    ratio = f * (2.0 / total)
    band = jnp.where(lane < SPLIT, band_ref[g], band_ref[g + GROUPS]).astype(jnp.float32)
    s = band * (ratio * ratio - 0.5)
    n = jnp.floor(s + 0.5)
    y = s - n
    y2 = y * y
    pi = math.pi
    poly = -(pi**11) / 39916800.0
    for power, fact in ((9, 362880.0), (7, -5040.0), (5, 120.0), (3, -6.0), (1, 1.0)):
        poly = poly * y2 + (pi**power) / fact
    odd = n.astype(jnp.int32) & 1
    lobe = jnp.where(odd == 1, 1.0, -1.0) * (y * poly) * (1.0 / pi)
    cos_s, sin_s = cos_sin(s * (pi / 4.0))
    cos_s, sin_s = 0.5 * cos_s, 0.5 * sin_s
    for tap in range(TAPS):
        m = tap + 1 - SHIFT
        x = m - s
        sign = 1.0 if m % 2 == 0 else -1.0
        safe = jnp.where(x == 0.0, 1.0, x)
        sinc = jnp.where(x == 0.0, 1.0, (sign * lobe) / safe)
        window = 0.5 + math.cos(pi * m / 4.0) * cos_s + math.sin(pi * m / 4.0) * sin_s
        weight = jnp.where(jnp.abs(x) < SHIFT / 2.0, sinc * window, 0.0)
        weight_ref[g, tap] = jnp.concatenate([weight, weight], axis=1).astype(jnp.bfloat16)
    first = lines_ref[pl.ds(g, SPLIT // 2, stride=STRIP)]
    second = lines_ref[pl.ds(g + GROUPS, SPLIT // 2, stride=STRIP)]
    pieces = [first, pltpu.roll(first, SPLIT, 1), second, pltpu.roll(second, SPLIT, 1)]
    angle = jnp.concatenate(pieces, axis=0).T[:SPLIT]
    cos_ref[g], sin_ref[g] = cos_sin(angle)


def arrived_lines(wide_ref, i, sources, local, low):
    rows = []
    for c in range(2):
        for pair in range(wide_ref.shape[1]):
            one = wide_ref[c, pair, pl.ds(i, sources, stride=HALF)]
            two = wide_ref[c, pair, pl.ds(i + SHIFT, sources, stride=HALF)]
            rows.append(jnp.where(low[:sources], one, pltpu.roll(two, SPLIT, 1)))
            if local > 1:
                rows.append(jnp.where(low[:sources], pltpu.roll(one, SPLIT, 1), two))
    return jnp.concatenate(rows, axis=0).astype(jnp.bfloat16)


def scene_kernel(
    band_ref, packed_ref, phase_ref,
    left_ref, right_ref, back_right_ref, back_left_ref, tc_ref, ts_ref, look_ref,
    azimuth_ref, range_ref, back_azimuth_ref, back_range_ref,
    out_ref,
    raw_ref, spread_ref, recv_ref, lines_ref, wide_ref, weight_ref, cos_ref, sin_ref, ext_ref,
    rim_ref, up_ref, down_ref, before_ref, after_ref, focused_ref,
    own_ref, own_before_ref, own_after_ref, line_ref, grid_ref,
    send_sem, recv_sem, local_sem, edge_send, edge_recv, look_send, look_recv,
    loads,
):
    scene = lax.axis_size("scene")
    me = lax.axis_index("scene")
    dates = raw_ref.shape[0]
    lines_held = raw_ref.shape[5]
    local = lines_held // SPLIT
    low = lax.broadcasted_iota(jnp.int32, (SPLIT, LANES), 1) < SPLIT
    lows = jnp.concatenate([low, low], axis=1)
    patches = SPLIT // 2

    barrier = pltpu.get_barrier_semaphore()

    def greet(o, carry):
        pl.semaphore_signal(
            barrier, inc=1, device_id={"scene": lax.rem(me + o, scene)},
            device_id_type=pl.DeviceIdType.MESH,
        )
        return carry

    lax.fori_loop(1, scene, greet, 0)
    for load in loads:
        load.start()
    loads[0].wait()
    height = packed_ref.shape[0]
    piece = height // 8

    def spread(i, carry):
        rows = pl.ds(pl.multiple_of(i * piece, piece), piece)
        spread_ref[rows] = packed_ref[rows].astype(jnp.float32)
        return carry

    lax.fori_loop(0, 8, spread, 0)
    owners = LANES // STRIP
    tiles = scene // owners
    stride = 2 * tiles * dates

    def turn(d):
        def body(tile, carry):
            for c in range(2):
                start = (c * tiles + tile) * dates + d
                bins = spread_ref[pl.ds(start, lines_held, stride=stride)].T
                for n in range(owners):
                    own = bins[n * STRIP : (n + 1) * STRIP]
                    rim = jnp.concatenate([own[:SHIFT], own[STRIP - SHIFT :]], axis=0)
                    core = own[SHIFT : STRIP - SHIFT]
                    raw_ref[d, 0, tile * owners + n, c] = rim.astype(jnp.bfloat16)
                    raw_ref[d, 1, tile * owners + n, c] = core.astype(jnp.bfloat16)
            return carry

        lax.fori_loop(0, tiles, body, 0)

    turn(0)
    pl.semaphore_wait(barrier, scene - 1)

    def far(i):
        half = (i + 1) // 2
        return scene // 2 + half * (1 - 2 * lax.rem(i, 2))

    def piece_of(ref, k, owner):
        return ref.at[k // 2, k % 2, owner]

    def strip_copy(k, o):
        peer = lax.rem(me + o, scene)
        return pltpu.make_async_remote_copy(
            src_ref=piece_of(raw_ref, k, peer),
            dst_ref=piece_of(recv_ref, k, me),
            send_sem=send_sem.at[k, o],
            recv_sem=recv_sem.at[k, o],
            device_id={"scene": peer},
            device_id_type=pl.DeviceIdType.MESH,
        )

    def own_copy(k):
        return pltpu.make_async_copy(
            piece_of(raw_ref, k, me), piece_of(recv_ref, k, me), local_sem.at[k]
        )

    def send_all(k):
        def send(i, carry):
            strip_copy(k, far(i)).start()
            return carry

        lax.fori_loop(0, scene - 1, send, 0)
        own_copy(k).start()

    def arrive_all(k):
        def arrive(o, carry):
            strip_copy(k, o).wait_recv()
            return carry

        lax.fori_loop(1, scene, arrive, 0)
        own_copy(k).wait()

    send_all(0)
    for d in range(1, dates):
        turn(d)
        send_all(2 * d)

    for load in loads[1:]:
        load.wait()

    for part in range(SPLIT // 2):
        lines_ref[pl.ds(part * STRIP, STRIP)] = phase_ref[:, part * LANES : (part + 1) * LANES]

    def weigh(g, carry):
        make_weights(g, band_ref, lines_ref, weight_ref, cos_ref, sin_ref)
        return carry

    lax.fori_loop(0, GROUPS, weigh, 0)

    @pl.when(me == 0)
    def _():
        before_ref[...] = jnp.zeros(before_ref.shape, before_ref.dtype)
        own_before_ref[...] = jnp.zeros(own_before_ref.shape, own_before_ref.dtype)

    @pl.when(me == scene - 1)
    def _():
        after_ref[...] = jnp.zeros(after_ref.shape, after_ref.dtype)
        own_after_ref[...] = jnp.zeros(own_after_ref.shape, own_after_ref.dtype)

    line_ref[...] = jnp.zeros(line_ref.shape, jnp.float32)

    def neighbour(source, target, send, recv, step):
        return pltpu.make_async_remote_copy(
            src_ref=source, dst_ref=target, send_sem=send, recv_sem=recv,
            device_id={"scene": me + step}, device_id_type=pl.DeviceIdType.MESH,
        )

    def edge_copies(d):
        return (
            neighbour(
                up_ref.at[d, pl.ds(1, SHIFT - 1)], before_ref.at[d, pl.ds(1, SHIFT - 1)],
                edge_send.at[d, 0], edge_recv.at[d, 0], 1,
            ),
            neighbour(
                down_ref.at[d, pl.ds(0, SHIFT - 1)], after_ref.at[d, pl.ds(0, SHIFT - 1)],
                edge_send.at[d, 1], edge_recv.at[d, 1], -1,
            ),
        )

    def look_copies(big):
        return (
            neighbour(
                own_ref.at[HALO_CHUNKS + big], own_before_ref.at[big],
                look_send.at[big, 0], look_recv.at[big, 0], 1,
            ),
            neighbour(
                own_ref.at[big], own_after_ref.at[big],
                look_send.at[big, 1], look_recv.at[big, 1], -1,
            ),
        )

    def start_pair(copies):
        @pl.when(me < scene - 1)
        def _():
            copies[0].start()

        @pl.when(me > 0)
        def _():
            copies[1].start()

    def wait_pair(copies):
        @pl.when(me > 0)
        def _():
            copies[0].wait_recv()
            copies[1].wait_send()

        @pl.when(me < scene - 1)
        def _():
            copies[1].wait_recv()
            copies[0].wait_send()

    def widen(d, part):
        def body(source, carry):
            start = pl.multiple_of(source * HALF, HALF)
            for c in range(2):
                strip = recv_ref[d, part, source, c].astype(jnp.float32)
                for pair in range(wide_ref.shape[1]):
                    kept = strip[:, pair * LANES : (pair + 1) * LANES]
                    wide_ref[c, pair, pl.ds(start, HALF), : kept.shape[1]] = kept
            return carry

        lax.fori_loop(0, scene, body, 0)

    def transform(first, count):
        held = [arrived_lines(wide_ref, first + n, scene, local, low) for n in range(count)]
        mixed = dot(left_ref[...], jnp.concatenate(held, axis=1))
        tc, ts = tc_ref[...], ts_ref[...]
        segments = []
        for n in range(count):
            re, im = (mixed[k : k + SPLIT, n * LANES : (n + 1) * LANES] for k in (0, SPLIT))
            segments.append(jnp.concatenate([re * tc + im * ts, im * tc - re * ts], axis=1))
        stacked = jnp.concatenate(segments, axis=0).astype(jnp.bfloat16)
        spectra = dot(stacked, right_ref[...]) * (1.0 / SPLIT)
        return [spectra[n * SPLIT : (n + 1) * SPLIT] for n in range(count)]

    def turned(pair):
        parts = (pair[:, :LANES], pair[:, LANES:])
        return jnp.concatenate([pltpu.roll(part, SPLIT, 1) for part in parts], axis=1)

    def forward_rim(d):
        widen(d, 0)

        def body(step, carry):
            for n, rim in enumerate(transform(BATCH * step, BATCH)):
                i = BATCH * step + n
                flipped = turned(rim)
                rim_ref[d, i] = rim
                down = jnp.where(low, rim[:, :LANES], flipped[:, LANES:])
                up = jnp.where(low, flipped[:, :LANES], rim[:, LANES:])
                down_ref[d, i] = down.astype(jnp.bfloat16)
                up_ref[d, i] = up.astype(jnp.bfloat16)
            return carry

        lax.fori_loop(0, SHIFT // BATCH, body, 0, unroll=True)
        start_pair(edge_copies(d))

    def forward_core(d):
        widen(d, 1)
        wait_pair(edge_copies(d))

        def body(step, carry):
            for n, core in enumerate(transform(BATCH * step, BATCH)):
                i = BATCH * step + n
                before = before_ref[d, i].astype(jnp.float32)
                after = after_ref[d, i].astype(jnp.float32)
                before = jnp.concatenate([before, pltpu.roll(before, SPLIT, 1)], axis=1)
                after = jnp.concatenate([pltpu.roll(after, SPLIT, 1), after], axis=1)
                rim, flipped = rim_ref[d, i], turned(core)
                ext_ref[i] = jnp.where(lows, before, flipped).astype(jnp.bfloat16)
                ext_ref[SHIFT + i] = jnp.where(lows, rim, core).astype(jnp.bfloat16)
                ext_ref[2 * SHIFT + i] = jnp.where(lows, core, rim).astype(jnp.bfloat16)
                ext_ref[3 * SHIFT + i] = jnp.where(lows, flipped, after).astype(jnp.bfloat16)
            return carry

        lax.fori_loop(0, SHIFT // BATCH, body, 0, unroll=True)

    def migrate(big):
        totals = [[] for _ in range(4)]
        for top in range(0, SPLIT, 8):
            rows = slice(top, top + 8)
            data = [ext_ref[4 * big + n + 1, rows] for n in range(TAPS + 3)]
            for j in range(4):
                sums = []
                for first in range(2):
                    total = weight_ref[4 * big + j, first, rows] * data[j + first]
                    for tap in range(first + 2, TAPS, 2):
                        total += weight_ref[4 * big + j, tap, rows] * data[j + tap]
                    sums.append(total.astype(jnp.float32))
                totals[j].append(sums[0] + sums[1])
        return [jnp.concatenate(total, axis=0) for total in totals]

    def focus(big):
        compressed = []
        for j, migrated in enumerate(migrate(big)):
            re, im = migrated[:, :LANES], migrated[:, LANES:]
            cos_phase, sin_phase = cos_ref[4 * big + j], sin_ref[4 * big + j]
            parts = [re * cos_phase - im * sin_phase, im * cos_phase + re * sin_phase]
            compressed.append(jnp.concatenate(parts, axis=1).astype(jnp.bfloat16))
        first = dot(jnp.concatenate(compressed, axis=0), back_right_ref[...])
        tc, ts = tc_ref[...], ts_ref[...]
        segments = []
        for j in range(4):
            rows = first[j * SPLIT : (j + 1) * SPLIT]
            re, im = rows[:, :LANES], rows[:, LANES:]
            segments.append(jnp.concatenate([re * tc - im * ts, im * tc + re * ts], axis=0))
        stacked = jnp.concatenate(segments, axis=1).astype(jnp.bfloat16)
        second = (dot(back_left_ref[...], stacked) * (1.0 / SPLIT)).astype(jnp.bfloat16)
        return [second[:, j * LANES : (j + 1) * LANES] for j in range(4)]

    def focus_first(big, carry):
        for j, focused in enumerate(focus(big)):
            focused_ref[4 * big + j] = focused
        return carry

    def focus_last(step, carry):
        products = []
        for n in range(2):
            big = 2 * step + n
            pieces = []
            for j, focused in enumerate(focus(big)):
                leading = focused.astype(jnp.float32)
                trailing = focused_ref[4 * big + j].astype(jnp.float32)
                lr, li = leading[:SPLIT], leading[SPLIT:]
                tr, ti = trailing[:SPLIT], trailing[SPLIT:]
                product = jnp.concatenate([lr * tr + li * ti, li * tr - lr * ti], axis=1)
                pieces.append(product.astype(jnp.bfloat16))
            products.append(jnp.concatenate(pieces, axis=1))
        looked = dot(jnp.concatenate(products, axis=0), look_ref[...]).astype(jnp.bfloat16)
        for n in range(2):
            big, rows = 2 * step + n, slice(n * SPLIT, (n + 1) * SPLIT)
            own_ref[big] = looked[rows, :LANES]
            own_ref[HALO_CHUNKS + big] = looked[rows, LANES:]
            start_pair(look_copies(big))
        return carry

    send_all(1)
    for d in range(dates):
        arrive_all(2 * d)
        forward_rim(d)
    send_all(3)
    arrive_all(1)
    forward_core(0)
    lax.fori_loop(0, GROUPS // 4, focus_first, 0, unroll=2)
    arrive_all(3)
    forward_core(1)
    lax.fori_loop(0, GROUPS // 8, focus_last, 0)

    def lines_of(first_chunk, count):
        def forward_lines(step, carry):
            rows = []
            for j in range(4):
                chunk = first_chunk + 4 * step + j
                rows.append(
                    jnp.concatenate(
                        [line_ref[chunk, pl.ds(p, patches, stride=2)] for p in range(4)], axis=1
                    )
                )
            lines = jnp.concatenate(rows, axis=0).astype(jnp.bfloat16)
            result = dot(lines, azimuth_ref[...]).astype(jnp.bfloat16).astype(jnp.float32)
            for j in range(4):
                for r in range(4):
                    start = ((first_chunk + 4 * step + j) * 4 + r) * patches
                    grid_ref[pl.ds(pl.multiple_of(start, patches), patches)] = result[
                        j * patches : (j + 1) * patches, r * LANES : (r + 1) * LANES
                    ]
            return carry

        lax.fori_loop(0, count // 4, forward_lines, 0)

    for j in range(CHUNKS):
        line_ref[HALO_CHUNKS + j, pl.ds(1, SPLIT)] = own_ref[j].astype(jnp.float32)
    lines_of(HALO_CHUNKS, CHUNKS)
    for k in range(2 * dates):

        def sent(o, carry):
            strip_copy(k, o).wait_send()
            return carry

        lax.fori_loop(1, scene, sent, 0)

    for big in range(HALO_CHUNKS):
        wait_pair(look_copies(big))
    for j in range(HALO_CHUNKS):
        line_ref[j, pl.ds(1, SPLIT)] = own_before_ref[j].astype(jnp.float32)
        line_ref[HALO_CHUNKS + CHUNKS + j, pl.ds(1, SPLIT)] = own_after_ref[j].astype(jnp.float32)
    lines_of(0, HALO_CHUNKS)
    lines_of(HALO_CHUNKS + CHUNKS, HALO_CHUNKS)
    lane = lax.broadcasted_iota(jnp.int32, (PATCH, LANES), 1)
    opening, closing = lane % PATCH == 0, lane % PATCH == PATCH - 1

    def filter_patches(step, carry):
        stacks = []
        for pair in range(2 * STEPS):
            one = grid_ref[pl.ds(4 * STEPS * step + 2 * pair, PATCH, stride=patches)]
            two = grid_ref[pl.ds(4 * STEPS * step + 2 * pair + 1, PATCH, stride=patches)]
            re = jnp.where(low, one, pltpu.roll(two, PATCH, 1))
            im = jnp.where(low, pltpu.roll(one, PATCH, 1), two)
            stacks.append(jnp.concatenate([re, im], axis=0).astype(jnp.bfloat16))
        spectra = dot(range_ref[...], jnp.concatenate(stacks, axis=1)) * (1.0 / PATCH)
        kept_re, kept_im = [], []
        for pair in range(2 * STEPS):
            re = spectra[:PATCH, pair * LANES : (pair + 1) * LANES]
            im = spectra[PATCH:, pair * LANES : (pair + 1) * LANES]
            magnitude = jnp.sqrt(re * re + im * im + EPSILON)
            rows = magnitude + pltpu.roll(magnitude, 1, 0) + pltpu.roll(magnitude, PATCH - 1, 0)
            left = jnp.where(opening, pltpu.roll(rows, PATCH + 1, 1), pltpu.roll(rows, 1, 1))
            right = jnp.where(closing, pltpu.roll(rows, PATCH - 1, 1), pltpu.roll(rows, LANES - 1, 1))
            column = jnp.sum(magnitude, axis=0, keepdims=True)
            first = jnp.sum(jnp.where(low[:1], column, 0.0), axis=1, keepdims=True)
            second = jnp.sum(jnp.where(low[:1], 0.0, column), axis=1, keepdims=True)
            level = jnp.where(low[:1], first, second) * (1.0 / (PATCH * PATCH)) + EPSILON
            gain = (rows + left + right) * ((1.0 / 9.0) / level)
            kept_re.append((re * gain).astype(jnp.bfloat16))
            kept_im.append((im * gain).astype(jnp.bfloat16))
        kept = [
            jnp.concatenate(kept_re[2 * n : 2 * n + 2] + kept_im[2 * n : 2 * n + 2], axis=1)
            for n in range(STEPS)
        ]
        back = dot(jnp.concatenate(kept, axis=0), back_azimuth_ref[...]).astype(jnp.bfloat16)
        stacked = []
        for n in range(STEPS):
            rows = back[n * PATCH : (n + 1) * PATCH]
            stacked.append(jnp.concatenate([rows[:, :LANES], rows[:, LANES:]], axis=0))
        result = dot(back_range_ref[...], jnp.concatenate(stacked, axis=1)) * (1.0 / PATCH)
        width = STEPS * LANES
        start = pl.multiple_of(step * width, width)
        out_ref[:, pl.ds(start, width)] = result.astype(jnp.bfloat16)
        return carry

    lax.fori_loop(0, patches // (4 * STEPS), filter_patches, 0)


def loading_kernel(band_ref, *refs):
    held, out_ref, kept, load_sem = refs[:TABLES], refs[TABLES], refs[TABLES + 1 : -1], refs[-1]
    loads = [
        pltpu.make_async_copy(source, target, load_sem.at[i])
        for i, (source, target) in enumerate(zip(held, kept[:TABLES]))
    ]
    scene_kernel(band_ref, *kept[:TABLES], out_ref, *kept[TABLES:], loads)


def run_scene(raw, band, phase, left, scene, shape):
    dates, width = shape[1], shape[3]
    looks = SPLIT * SPLIT // LOOKS
    tc, ts = twiddle_tables()
    vmem = pl.BlockSpec(memory_space=pltpu.VMEM)
    plane = (GROUPS, SPLIT, LANES)
    edge = pltpu.VMEM((dates, SHIFT, SPLIT, LANES), jnp.bfloat16)
    looked_edge = pltpu.VMEM((HALO_CHUNKS, SPLIT, LANES), jnp.bfloat16)
    dma = pltpu.SemaphoreType.DMA
    tables = (
        raw, phase, bf16(left), bf16(spectrum_side(right_table(1.0), 1)),
        bf16(spectrum_side(right_table(-1.0), 0)), bf16(left_table(-1.0)),
        jnp.asarray(tc), jnp.asarray(ts), bf16(look_table()),
        bf16(patch_azimuth_table()), bf16(patch_range_table()),
        bf16(back_azimuth_table()), bf16(back_range_table()),
    )
    return pl.pallas_call(
        loading_kernel,
        in_specs=[pl.BlockSpec(memory_space=pltpu.SMEM)]
        + [pl.BlockSpec(memory_space=pl.ANY)] * TABLES,
        out_specs=vmem,
        out_shape=pltpu.VMEM((2 * STRIP, looks), jnp.bfloat16),
        scratch_shapes=[pltpu.VMEM(table.shape, table.dtype) for table in tables]
        + [
            pltpu.VMEM((dates, 2, scene, 2, HALF, width), jnp.bfloat16),
            pltpu.VMEM(raw.shape, jnp.float32),
            pltpu.VMEM((dates, 2, scene, 2, HALF, width), jnp.bfloat16),
            pltpu.VMEM((STRIP * SPLIT // 2, LANES), jnp.float32),
            pltpu.VMEM((2, pl.cdiv(width, LANES), scene * HALF, LANES), jnp.float32),
            pltpu.VMEM((GROUPS, TAPS, SPLIT, 2 * LANES), jnp.bfloat16),
            pltpu.VMEM(plane, jnp.float32),
            pltpu.VMEM(plane, jnp.float32),
            pltpu.VMEM((GROUPS + 2 * SHIFT, SPLIT, 2 * LANES), jnp.bfloat16),
            pltpu.VMEM((dates, SHIFT, SPLIT, 2 * LANES), jnp.float32),
            edge, edge, edge, edge,
            pltpu.VMEM((GROUPS, 2 * SPLIT, LANES), jnp.bfloat16),
            pltpu.VMEM((CHUNKS, SPLIT, LANES), jnp.bfloat16),
            looked_edge,
            looked_edge,
            pltpu.VMEM((2 * CHUNKS, SPLIT + 8, LANES), jnp.float32),
            pltpu.VMEM((PATCH * SPLIT // 2, LANES), jnp.float32),
            dma((2 * dates, scene)), dma((2 * dates, scene)), dma((2 * dates,)),
            dma((dates, 2)), dma((dates, 2)),
            dma((HALO_CHUNKS, 2)), dma((HALO_CHUNKS, 2)), dma((TABLES,)),
        ],
        compiler_params=pltpu.CompilerParams(
            vmem_limit_bytes=VMEM_LIMIT, collective_id=0, has_side_effects=True
        ),
        name="scene",
    )(*[pltpu.with_memory_space_constraint(t, pltpu.HBM) for t in (band, *tables)])


def on_device(raw_echoes, azimuth_phase, band_offset, partners):
    scene = lax.axis_size("scene")
    dates = raw_echoes.shape[2]
    local = raw_echoes.shape[0] // SPLIT
    pairs = partners.size
    assert dates == 2 and raw_echoes.shape[3] == scene * STRIP
    left = left_table(1.0).reshape(2 * SPLIT, 2, scene, local)
    left = left.transpose(0, 1, 3, 2).reshape(2 * SPLIT, 2 * SPLIT)
    lines, bins = raw_echoes.shape[0], raw_echoes.shape[3]
    raw = raw_echoes.reshape(lines, 2, dates, bins // LANES, LANES)
    raw = raw.transpose(0, 1, 3, 2, 4).reshape(-1, LANES)
    phase = azimuth_phase.T
    result = run_scene(
        raw, band_offset, phase, left, scene, (2, dates, bins, lines)
    )
    result = jnp.broadcast_to(result, (pairs,) + result.shape)
    return result.reshape(pairs, 2, STRIP, -1).transpose(0, 3, 1, 2)


def solution(mesh):
    return jax.shard_map(
        on_device,
        mesh=mesh,
        in_specs=(
            P("scene", None, "stack", None),
            P("stack", "scene"),
            P(("stack", "scene")),
            P("stack", None),
        ),
        out_specs=P("stack", None, None, "scene"),
        check_vma=False,
    )
```

```python
import math

import jax
import jax.numpy as jnp
import numpy as np
from jax import lax
from jax.experimental import pallas as pl
from jax.experimental.pallas import tpu as pltpu
from jax.sharding import PartitionSpec as P

SPLIT = 64
LOOKS = 4
PATCH = 64
SHIFT = 8
TAPS = 2 * SHIFT - 1
EPSILON = 1e-06
STRIP = 32
GROUPS = STRIP // 2
LANES = 2 * SPLIT
CHUNKS = STRIP // 4
HALO_CHUNKS = CHUNKS // 2
HALF = STRIP // 2
BATCH = 8
STEPS = 4
TABLES = 5
SLABS = 4
VMEM_LIMIT = 40 * 1024 * 1024


def base_tables():
    k = np.arange(64)
    angle = 2.0 * np.pi * ((k[:, None] * k[None, :]) % 64) / 64.0
    return np.cos(angle), np.sin(angle)


def twiddle_tables():
    k = np.arange(SPLIT)
    angle = 2.0 * np.pi * ((k[:, None] * k[None, :]) % (SPLIT * SPLIT)) / (SPLIT * SPLIT)
    return (
        np.tile(np.cos(angle), (1, 2)).astype(np.float32),
        np.tile(np.sin(angle), (1, 2)).astype(np.float32),
    )


def bf16(table):
    return jnp.asarray(np.asarray(table, np.float32), jnp.bfloat16)


def left_table(direction):
    c, s = base_tables()
    return np.block([[c, direction * s], [-direction * s, c]])


def right_table(direction):
    c, s = base_tables()
    eye = np.eye(2)
    return np.block(
        [
            [np.kron(eye, c), np.kron(eye, -direction * s)],
            [np.kron(eye, direction * s), np.kron(eye, c)],
        ]
    )


def look_table():
    table = np.zeros((4, 2, 2, SPLIT, 2, 4, 2, SPLIT // LOOKS))
    for g in range(4):
        for c in range(2):
            for rb in range(2):
                for q in range(SPLIT):
                    table[g, c, rb, q, rb, g, c, q // LOOKS] = 1.0 / LOOKS
    return table.reshape(4 * 2 * 2 * SPLIT, 2 * 4 * 2 * SPLIT // LOOKS)


def patch_azimuth_table():
    c, s = base_tables()
    table = np.zeros((4, 4, 2, 16, 4, 2, 64))
    for p in range(4):
        part_c, part_s = c[16 * p : 16 * p + 16], s[16 * p : 16 * p + 16]
        for r in range(4):
            table[p, r, 0, :, r, 0] = part_c
            table[p, r, 1, :, r, 0] = part_s
            table[p, r, 0, :, r, 1] = -part_s
            table[p, r, 1, :, r, 1] = part_c
    return table.reshape(512, 512)


def patch_range_table():
    c, s = base_tables()
    return np.block([[c, s], [-s, c]])


def back_azimuth_table():
    c, s = base_tables()
    c, s = c[:, 16:48], s[:, 16:48]
    table = np.zeros((2, 4, 64, 2, 4, 32))
    for i in range(4):
        table[0, i, :, 0, i] = c
        table[1, i, :, 0, i] = -s
        table[0, i, :, 1, i] = s
        table[1, i, :, 1, i] = c
    return table.reshape(512, 256)


def back_range_table():
    c, s = base_tables()
    c, s = c[16:48], s[16:48]
    return np.block([[c, -s], [s, c]])


def dot(a, b):
    return jnp.dot(a, b, preferred_element_type=jnp.float32)


def lane_order():
    lane = np.arange(SPLIT)
    return 2 * (lane % (SPLIT // 2)) + lane // (SPLIT // 2)


def spectrum_side(table, axis):
    order = np.concatenate([SPLIT * half + lane_order() for half in range(4)])
    return np.take(table, order, axis=axis)


def cos_sin(angle):
    h = 0.5 * angle
    h2 = h * h
    sin_h = 1.0 / 6227020800.0
    for fact in (-39916800.0, 362880.0, -5040.0, 120.0, -6.0, 1.0):
        sin_h = sin_h * h2 + 1.0 / fact
    sin_h = sin_h * h
    cos_h = 1.0 / 479001600.0
    for fact in (-3628800.0, 40320.0, -720.0, 24.0, -2.0, 1.0):
        cos_h = cos_h * h2 + 1.0 / fact
    return 1.0 - 2.0 * sin_h * sin_h, 2.0 * sin_h * cos_h


def make_weights(g, band_ref, lines_ref, weight_ref, cos_ref, sin_ref):
    shape = (SPLIT, LANES)
    lane = lax.broadcasted_iota(jnp.int32, shape, 1)
    row = lax.broadcasted_iota(jnp.int32, shape, 0)
    half = SPLIT // 2
    k = row + SPLIT * (2 * (lane & (half - 1)) + ((lane & half) // half))
    total = SPLIT * SPLIT
    f = jnp.where(k < total // 2, k, k - total).astype(jnp.float32)
    ratio = f * (2.0 / total)
    band = jnp.where(lane < SPLIT, band_ref[g], band_ref[g + GROUPS]).astype(jnp.float32)
    s = band * (ratio * ratio - 0.5)
    n = jnp.floor(s + 0.5)
    y = s - n
    y2 = y * y
    pi = math.pi
    poly = -(pi**11) / 39916800.0
    for power, fact in ((9, 362880.0), (7, -5040.0), (5, 120.0), (3, -6.0), (1, 1.0)):
        poly = poly * y2 + (pi**power) / fact
    odd = n.astype(jnp.int32) & 1
    lobe = jnp.where(odd == 1, 1.0, -1.0) * (y * poly) * (1.0 / pi)
    cos_s, sin_s = cos_sin(s * (pi / 4.0))
    cos_s, sin_s = 0.5 * cos_s, 0.5 * sin_s
    for tap in range(TAPS):
        m = tap + 1 - SHIFT
        x = m - s
        sign = 1.0 if m % 2 == 0 else -1.0
        safe = jnp.where(x == 0.0, 1.0, x)
        sinc = jnp.where(x == 0.0, 1.0, (sign * lobe) / safe)
        window = 0.5 + math.cos(pi * m / 4.0) * cos_s + math.sin(pi * m / 4.0) * sin_s
        weight = jnp.where(jnp.abs(x) < SHIFT / 2.0, sinc * window, 0.0)
        weight_ref[g, tap] = jnp.concatenate([weight, weight], axis=1).astype(jnp.bfloat16)
    first = lines_ref[pl.ds(g, SPLIT // 2, stride=STRIP)]
    second = lines_ref[pl.ds(g + GROUPS, SPLIT // 2, stride=STRIP)]
    pieces = [first, pltpu.roll(first, SPLIT, 1), second, pltpu.roll(second, SPLIT, 1)]
    angle = jnp.concatenate(pieces, axis=0).T[:SPLIT]
    cos_ref[g], sin_ref[g] = cos_sin(angle)


def arrived_lines(wide_ref, i, sources, local, low):
    rows = []
    for c in range(2):
        for pair in range(wide_ref.shape[1]):
            one = wide_ref[c, pair, pl.ds(i, sources, stride=HALF)]
            two = wide_ref[c, pair, pl.ds(i + SHIFT, sources, stride=HALF)]
            rows.append(jnp.where(low[:sources], one, pltpu.roll(two, SPLIT, 1)))
            if local > 1:
                rows.append(jnp.where(low[:sources], pltpu.roll(one, SPLIT, 1), two))
    return jnp.concatenate(rows, axis=0).astype(jnp.bfloat16)


def scene_kernel(
    packed_ref, band_ref, phase_ref, table_ref, twiddle_ref,
    out_ref,
    raw_ref, spread_ref, recv_ref, lines_ref, wide_ref, weight_ref, cos_ref, sin_ref, ext_ref,
    rim_ref, up_ref, down_ref, before_ref, after_ref, focused_ref,
    own_ref, own_before_ref, own_after_ref, line_ref, grid_ref,
    send_sem, recv_sem, edge_send, edge_recv, look_send, look_recv,
    slabs, loads,
):
    scene = lax.axis_size("scene")
    me = lax.axis_index("scene")
    dates = raw_ref.shape[0]
    lines_held = raw_ref.shape[5]
    local = lines_held // SPLIT
    low = lax.broadcasted_iota(jnp.int32, (SPLIT, LANES), 1) < SPLIT
    lows = jnp.concatenate([low, low], axis=1)
    patches = SPLIT // 2

    left_ref, back_left_ref, range_ref, back_range_ref = (
        table_ref.at[rows, columns] for rows, columns in (
            (pl.ds(0, LANES), pl.ds(0, LANES)), (pl.ds(0, LANES), pl.ds(LANES, LANES)),
            (pl.ds(LANES, LANES), pl.ds(0, LANES)), (pl.ds(LANES, PATCH), pl.ds(LANES, LANES)),
        )
    )
    wide = 2 * LANES
    starts = np.cumsum([wide, wide, wide, 4 * wide, 2 * wide, 2 * wide]).tolist()
    right_ref, back_right_ref, look_ref, azimuth_one_ref, azimuth_two_ref, back_azimuth_ref = (
        table_ref.at[pl.ds(start, rows)]
        for start, rows in zip(starts, (wide, wide, 4 * wide, 2 * wide, 2 * wide, 2 * wide))
    )
    tc_ref, ts_ref = twiddle_ref.at[pl.ds(0, SPLIT)], twiddle_ref.at[pl.ds(SPLIT, SPLIT)]

    barrier = pltpu.get_barrier_semaphore()

    def greet(o, carry):
        pl.semaphore_signal(
            barrier, inc=1, device_id={"scene": lax.rem(me + o, scene)},
            device_id_type=pl.DeviceIdType.MESH,
        )
        return carry

    lax.fori_loop(1, scene, greet, 0)
    for load in slabs + loads:
        load.start()
    piece = packed_ref.shape[0] // (2 * SLABS)
    for n, slab in enumerate(slabs):
        slab.wait()
        for half in range(2):
            rows = pl.ds((2 * n + half) * piece, piece)
            spread_ref[rows] = packed_ref[rows].astype(jnp.float32)
    owners = LANES // STRIP
    tiles = scene // owners
    stride = 2 * tiles * dates

    def piece_of(ref, k, owner):
        return ref.at[k // 2, k % 2, owner]

    def strip_copy(k, peer):
        return pltpu.make_async_remote_copy(
            src_ref=piece_of(raw_ref, k, peer),
            dst_ref=piece_of(recv_ref, k, me),
            send_sem=send_sem.at[k],
            recv_sem=recv_sem.at[k],
            device_id={"scene": peer},
            device_id_type=pl.DeviceIdType.MESH,
        )

    def own_copy(k):
        return pltpu.make_async_copy(
            piece_of(raw_ref, k, me), piece_of(recv_ref, k, me), recv_sem.at[k]
        )

    def turn(d, tile):
        for c in range(2):
            start = (c * tiles + tile) * dates + d
            bins = spread_ref[pl.ds(start, lines_held, stride=stride)].T
            for n in range(owners):
                own = bins[n * STRIP : (n + 1) * STRIP]
                rim = jnp.concatenate([own[:SHIFT], own[STRIP - SHIFT :]], axis=0)
                core = own[SHIFT : STRIP - SHIFT]
                raw_ref[d, 0, tile * owners + n, c] = rim.astype(jnp.bfloat16)
                raw_ref[d, 1, tile * owners + n, c] = core.astype(jnp.bfloat16)

    def turn_and_send(d):
        def body(i, carry):
            tile = lax.rem(me // owners + tiles // 2 + i, tiles)
            turn(d, tile)

            @pl.when(i == 0)
            def _():
                if d == 0:
                    pl.semaphore_wait(barrier, scene - 1)

            for n in range(owners):
                peer = tile * owners + n

                @pl.when(peer != me)
                def _():
                    strip_copy(2 * d, peer).start()

            return carry

        lax.fori_loop(0, tiles, body, 0)
        own_copy(2 * d).start()

    def far(i):
        half = (i + 1) // 2
        return scene // 2 + half * (1 - 2 * lax.rem(i, 2))

    def send_all(k):
        def send(i, carry):
            strip_copy(k, lax.rem(me + far(i), scene)).start()
            return carry

        lax.fori_loop(0, scene - 1, send, 0)
        own_copy(k).start()

    def arrive_all(k):
        held = recv_ref.at[k // 2, k % 2]
        pltpu.make_async_copy(held, held, recv_sem.at[k]).wait()

    def sent_all(k):
        held = raw_ref.at[k // 2, k % 2, pl.ds(0, scene - 1)]
        pltpu.make_async_copy(held, held, send_sem.at[k]).wait()

    for d in range(dates):
        turn_and_send(d)

    for load in loads:
        load.wait()

    for part in range(SPLIT // 2):
        lines_ref[pl.ds(part * STRIP, STRIP)] = phase_ref[:, part * LANES : (part + 1) * LANES]

    def weigh(g, carry):
        make_weights(g, band_ref, lines_ref, weight_ref, cos_ref, sin_ref)
        return carry

    lax.fori_loop(0, GROUPS, weigh, 0)

    @pl.when(me == 0)
    def _():
        before_ref[...] = jnp.zeros(before_ref.shape, before_ref.dtype)
        own_before_ref[...] = jnp.zeros(own_before_ref.shape, own_before_ref.dtype)

    @pl.when(me == scene - 1)
    def _():
        after_ref[...] = jnp.zeros(after_ref.shape, after_ref.dtype)
        own_after_ref[...] = jnp.zeros(own_after_ref.shape, own_after_ref.dtype)

    line_ref[...] = jnp.zeros(line_ref.shape, jnp.float32)

    def neighbour(source, target, send, recv, step):
        return pltpu.make_async_remote_copy(
            src_ref=source, dst_ref=target, send_sem=send, recv_sem=recv,
            device_id={"scene": me + step}, device_id_type=pl.DeviceIdType.MESH,
        )

    def edge_copies(d):
        return (
            neighbour(
                up_ref.at[d, pl.ds(1, SHIFT - 1)], before_ref.at[d, pl.ds(1, SHIFT - 1)],
                edge_send.at[d, 0], edge_recv.at[d, 0], 1,
            ),
            neighbour(
                down_ref.at[d, pl.ds(0, SHIFT - 1)], after_ref.at[d, pl.ds(0, SHIFT - 1)],
                edge_send.at[d, 1], edge_recv.at[d, 1], -1,
            ),
        )

    def look_copies(big):
        return (
            neighbour(
                own_ref.at[HALO_CHUNKS + big], own_before_ref.at[big],
                look_send.at[0], look_recv.at[0], 1,
            ),
            neighbour(
                own_ref.at[big], own_after_ref.at[big],
                look_send.at[1], look_recv.at[1], -1,
            ),
        )

    def start_pair(copies):
        @pl.when(me < scene - 1)
        def _():
            copies[0].start()

        @pl.when(me > 0)
        def _():
            copies[1].start()

    def wait_pair(copies):
        @pl.when(me > 0)
        def _():
            copies[0].wait_recv()
            copies[1].wait_send()

        @pl.when(me < scene - 1)
        def _():
            copies[1].wait_recv()
            copies[0].wait_send()

    def widen(d, part):
        def body(source, carry):
            start = pl.multiple_of(source * HALF, HALF)
            for c in range(2):
                strip = recv_ref[d, part, source, c].astype(jnp.float32)
                for pair in range(wide_ref.shape[1]):
                    kept = strip[:, pair * LANES : (pair + 1) * LANES]
                    wide_ref[c, pair, pl.ds(start, HALF), : kept.shape[1]] = kept
            return carry

        lax.fori_loop(0, scene, body, 0)

    def transform(first, count):
        held = [arrived_lines(wide_ref, first + n, scene, local, low) for n in range(count)]
        mixed = dot(left_ref[...], jnp.concatenate(held, axis=1))
        tc, ts = tc_ref[...], ts_ref[...]
        segments = []
        for n in range(count):
            re, im = (mixed[k : k + SPLIT, n * LANES : (n + 1) * LANES] for k in (0, SPLIT))
            segments.append(jnp.concatenate([re * tc + im * ts, im * tc - re * ts], axis=1))
        stacked = jnp.concatenate(segments, axis=0).astype(jnp.bfloat16)
        spectra = dot(stacked, right_ref[...])
        return [spectra[n * SPLIT : (n + 1) * SPLIT] for n in range(count)]

    def turned(pair):
        parts = (pair[:, :LANES], pair[:, LANES:])
        return jnp.concatenate([pltpu.roll(part, SPLIT, 1) for part in parts], axis=1)

    def forward_rim(d):
        widen(d, 0)

        def body(step, carry):
            for n, rim in enumerate(transform(BATCH * step, BATCH)):
                i = BATCH * step + n
                flipped = turned(rim)
                rim_ref[d, i] = rim
                down = jnp.where(low, rim[:, :LANES], flipped[:, LANES:])
                up = jnp.where(low, flipped[:, :LANES], rim[:, LANES:])
                down_ref[d, i] = down.astype(jnp.bfloat16)
                up_ref[d, i] = up.astype(jnp.bfloat16)
            return carry

        lax.fori_loop(0, SHIFT // BATCH, body, 0, unroll=True)
        start_pair(edge_copies(d))

    def forward_core(d):
        widen(d, 1)
        wait_pair(edge_copies(d))

        def body(step, carry):
            for n, core in enumerate(transform(BATCH * step, BATCH)):
                i = BATCH * step + n
                before = before_ref[d, i].astype(jnp.float32)
                after = after_ref[d, i].astype(jnp.float32)
                before = jnp.concatenate([before, pltpu.roll(before, SPLIT, 1)], axis=1)
                after = jnp.concatenate([pltpu.roll(after, SPLIT, 1), after], axis=1)
                rim, flipped = rim_ref[d, i], turned(core)
                ext_ref[i] = jnp.where(lows, before, flipped).astype(jnp.bfloat16)
                ext_ref[SHIFT + i] = jnp.where(lows, rim, core).astype(jnp.bfloat16)
                ext_ref[2 * SHIFT + i] = jnp.where(lows, core, rim).astype(jnp.bfloat16)
                ext_ref[3 * SHIFT + i] = jnp.where(lows, flipped, after).astype(jnp.bfloat16)
            return carry

        lax.fori_loop(0, SHIFT // BATCH, body, 0, unroll=True)

    def migrate(big):
        totals = [[] for _ in range(4)]
        for top in range(0, SPLIT, 8):
            rows = slice(top, top + 8)
            data = [ext_ref[4 * big + n + 1, rows] for n in range(TAPS + 3)]
            for j in range(4):
                sums = []
                for first in range(2):
                    total = weight_ref[4 * big + j, first, rows] * data[j + first]
                    for tap in range(first + 2, TAPS, 2):
                        total += weight_ref[4 * big + j, tap, rows] * data[j + tap]
                    sums.append(total.astype(jnp.float32))
                totals[j].append(sums[0] + sums[1])
        return [jnp.concatenate(total, axis=0) for total in totals]

    def focus(big):
        compressed = []
        for j, migrated in enumerate(migrate(big)):
            re, im = migrated[:, :LANES], migrated[:, LANES:]
            cos_phase, sin_phase = cos_ref[4 * big + j], sin_ref[4 * big + j]
            parts = [re * cos_phase - im * sin_phase, im * cos_phase + re * sin_phase]
            compressed.append(jnp.concatenate(parts, axis=1).astype(jnp.bfloat16))
        first = dot(jnp.concatenate(compressed, axis=0), back_right_ref[...])
        tc, ts = tc_ref[...], ts_ref[...]
        segments = []
        for j in range(4):
            rows = first[j * SPLIT : (j + 1) * SPLIT]
            re, im = rows[:, :LANES], rows[:, LANES:]
            segments.append(jnp.concatenate([re * tc - im * ts, im * tc + re * ts], axis=0))
        stacked = jnp.concatenate(segments, axis=1).astype(jnp.bfloat16)
        second = dot(back_left_ref[...], stacked).astype(jnp.bfloat16)
        return [second[:, j * LANES : (j + 1) * LANES] for j in range(4)]

    def focus_first(big, carry):
        for j, focused in enumerate(focus(big)):
            focused_ref[4 * big + j] = focused
        return carry

    def focus_last(step, carry):
        products = []
        for n in range(2):
            big = 2 * step + n
            pieces = []
            for j, focused in enumerate(focus(big)):
                leading = focused.astype(jnp.float32)
                trailing = focused_ref[4 * big + j].astype(jnp.float32)
                lr, li = leading[:SPLIT], leading[SPLIT:]
                tr, ti = trailing[:SPLIT], trailing[SPLIT:]
                product = jnp.concatenate([lr * tr + li * ti, li * tr - lr * ti], axis=1)
                pieces.append(product.astype(jnp.bfloat16))
            products.append(jnp.concatenate(pieces, axis=1))
        looked = dot(jnp.concatenate(products, axis=0), look_ref[...]).astype(jnp.bfloat16)
        for n in range(2):
            big, rows = 2 * step + n, slice(n * SPLIT, (n + 1) * SPLIT)
            own_ref[big] = looked[rows, :LANES]
            own_ref[HALO_CHUNKS + big] = looked[rows, LANES:]
            start_pair(look_copies(big))
        return carry

    send_all(1)
    for d in range(dates):
        arrive_all(2 * d)
        forward_rim(d)
    send_all(3)
    arrive_all(1)
    forward_core(0)
    lax.fori_loop(0, GROUPS // 4, focus_first, 0, unroll=2)
    arrive_all(3)
    forward_core(1)
    lax.fori_loop(0, GROUPS // 8, focus_last, 0)

    def lines_of(first_chunk, count):
        def forward_lines(step, carry):
            rows = []
            for j in range(4):
                chunk = first_chunk + 4 * step + j
                rows.append(
                    jnp.concatenate(
                        [line_ref[chunk, pl.ds(p, patches, stride=2)] for p in range(4)], axis=1
                    )
                )
            lines = jnp.concatenate(rows, axis=0).astype(jnp.bfloat16)
            results = [dot(lines, ref[...]) for ref in (azimuth_one_ref, azimuth_two_ref)]
            for j in range(4):
                for r in range(4):
                    start = ((first_chunk + 4 * step + j) * 4 + r) * patches
                    part = results[r // 2][j * patches : (j + 1) * patches]
                    part = part[:, (r % 2) * LANES : (r % 2 + 1) * LANES]
                    grid_ref[pl.ds(pl.multiple_of(start, patches), patches)] = part
            return carry

        lax.fori_loop(0, count // 4, forward_lines, 0)

    for j in range(CHUNKS):
        line_ref[HALO_CHUNKS + j, pl.ds(1, SPLIT)] = own_ref[j].astype(jnp.float32)
    lines_of(HALO_CHUNKS, CHUNKS)
    for k in range(2 * dates):
        sent_all(k)
    wait_pair(
        (
            neighbour(own_before_ref, own_before_ref, look_send.at[0], look_recv.at[0], 1),
            neighbour(own_after_ref, own_after_ref, look_send.at[1], look_recv.at[1], -1),
        )
    )
    for j in range(HALO_CHUNKS):
        line_ref[j, pl.ds(1, SPLIT)] = own_before_ref[j].astype(jnp.float32)
        line_ref[HALO_CHUNKS + CHUNKS + j, pl.ds(1, SPLIT)] = own_after_ref[j].astype(jnp.float32)
    lines_of(0, HALO_CHUNKS)
    lines_of(HALO_CHUNKS + CHUNKS, HALO_CHUNKS)
    lane = lax.broadcasted_iota(jnp.int32, (PATCH, LANES), 1)
    opening, closing = lane % PATCH == 0, lane % PATCH == PATCH - 1

    def filter_patches(step, carry):
        stacks = []
        for pair in range(2 * STEPS):
            one = grid_ref[pl.ds(4 * STEPS * step + 2 * pair, PATCH, stride=patches)]
            two = grid_ref[pl.ds(4 * STEPS * step + 2 * pair + 1, PATCH, stride=patches)]
            re = jnp.where(low, one, pltpu.roll(two, PATCH, 1))
            im = jnp.where(low, pltpu.roll(one, PATCH, 1), two)
            stacks.append(jnp.concatenate([re, im], axis=0).astype(jnp.bfloat16))
        spectra = dot(range_ref[...], jnp.concatenate(stacks, axis=1))
        kept_re, kept_im = [], []
        for pair in range(2 * STEPS):
            re = spectra[:PATCH, pair * LANES : (pair + 1) * LANES]
            im = spectra[PATCH:, pair * LANES : (pair + 1) * LANES]
            magnitude = jnp.sqrt(re * re + im * im + EPSILON)
            rows = magnitude + pltpu.roll(magnitude, 1, 0) + pltpu.roll(magnitude, PATCH - 1, 0)
            left = jnp.where(opening, pltpu.roll(rows, PATCH + 1, 1), pltpu.roll(rows, 1, 1))
            right = jnp.where(closing, pltpu.roll(rows, PATCH - 1, 1), pltpu.roll(rows, LANES - 1, 1))
            column = jnp.sum(magnitude, axis=0, keepdims=True)
            first = jnp.sum(jnp.where(low[:1], column, 0.0), axis=1, keepdims=True)
            second = jnp.sum(jnp.where(low[:1], 0.0, column), axis=1, keepdims=True)
            level = jnp.where(low[:1], first, second) * (1.0 / (PATCH * PATCH)) + EPSILON
            gain = (rows + left + right) * ((1.0 / 9.0) / level)
            kept_re.append((re * gain).astype(jnp.bfloat16))
            kept_im.append((im * gain).astype(jnp.bfloat16))
        kept = [
            jnp.concatenate(kept_re[2 * n : 2 * n + 2] + kept_im[2 * n : 2 * n + 2], axis=1)
            for n in range(STEPS)
        ]
        back = dot(jnp.concatenate(kept, axis=0), back_azimuth_ref[...]).astype(jnp.bfloat16)
        stacked = []
        for n in range(STEPS):
            rows = back[n * PATCH : (n + 1) * PATCH]
            stacked.append(jnp.concatenate([rows[:, :LANES], rows[:, LANES:]], axis=0))
        result = dot(back_range_ref[...], jnp.concatenate(stacked, axis=1))
        width = STEPS * LANES
        start = pl.multiple_of(step * width, width)
        out_ref[:, pl.ds(start, width)] = result.astype(jnp.bfloat16)
        return carry

    lax.fori_loop(0, patches // (4 * STEPS), filter_patches, 0)


def loading_kernel(*refs):
    held, out_ref, kept, load_sem = refs[:TABLES], refs[TABLES], refs[TABLES + 1 : -1], refs[-1]
    rows = held[0].shape[0] // SLABS
    slabs = [
        pltpu.make_async_copy(
            held[0].at[pl.ds(n * rows, rows)], kept[0].at[pl.ds(n * rows, rows)], load_sem.at[n]
        )
        for n in range(SLABS)
    ]
    loads = [
        pltpu.make_async_copy(held[i], kept[i], load_sem.at[SLABS - 1 + i])
        for i in range(1, TABLES)
    ]
    scene_kernel(*kept[:TABLES], out_ref, *kept[TABLES:], slabs, loads)


def table_stack(left):
    unit = 1.0 / SPLIT
    back_range = np.zeros((LANES, LANES))
    back_range[:PATCH] = back_range_table() * unit
    azimuth = patch_azimuth_table()
    return np.concatenate(
        [
            np.concatenate([left, left_table(-1.0) * unit], axis=1),
            np.concatenate([patch_range_table() * unit, back_range], axis=1),
            spectrum_side(right_table(1.0), 1) * unit,
            spectrum_side(right_table(-1.0), 0),
            look_table(),
            azimuth[:, : 2 * LANES],
            azimuth[:, 2 * LANES :],
            back_azimuth_table(),
        ]
    )


def run_scene(raw, band, phase, left, scene, shape):
    dates, width = shape[1], shape[3]
    looks = SPLIT * SPLIT // LOOKS
    vmem = pl.BlockSpec(memory_space=pltpu.VMEM)
    plane = (GROUPS, SPLIT, LANES)
    edge = pltpu.VMEM((dates, SHIFT, SPLIT, LANES), jnp.bfloat16)
    looked_edge = pltpu.VMEM((HALO_CHUNKS, SPLIT, LANES), jnp.bfloat16)
    dma = pltpu.SemaphoreType.DMA
    twiddles = np.concatenate(twiddle_tables())
    tables = (raw, band, phase, bf16(table_stack(left)), jnp.asarray(twiddles))
    return pl.pallas_call(
        loading_kernel,
        in_specs=[pl.BlockSpec(memory_space=pl.ANY)] * TABLES,
        out_specs=vmem,
        out_shape=pltpu.VMEM((2 * STRIP, looks), jnp.bfloat16),
        scratch_shapes=[
            (pltpu.SMEM if table is band else pltpu.VMEM)(table.shape, table.dtype)
            for table in tables
        ]
        + [
            pltpu.VMEM((dates, 2, scene, 2, HALF, width), jnp.bfloat16),
            pltpu.VMEM(raw.shape, jnp.float32),
            pltpu.VMEM((dates, 2, scene, 2, HALF, width), jnp.bfloat16),
            pltpu.VMEM((STRIP * SPLIT // 2, LANES), jnp.float32),
            pltpu.VMEM((2, pl.cdiv(width, LANES), scene * HALF, LANES), jnp.float32),
            pltpu.VMEM((GROUPS, TAPS, SPLIT, 2 * LANES), jnp.bfloat16),
            pltpu.VMEM(plane, jnp.float32),
            pltpu.VMEM(plane, jnp.float32),
            pltpu.VMEM((GROUPS + 2 * SHIFT, SPLIT, 2 * LANES), jnp.bfloat16),
            pltpu.VMEM((dates, SHIFT, SPLIT, 2 * LANES), jnp.float32),
            edge, edge, edge, edge,
            pltpu.VMEM((GROUPS, 2 * SPLIT, LANES), jnp.bfloat16),
            pltpu.VMEM((CHUNKS, SPLIT, LANES), jnp.bfloat16),
            looked_edge,
            looked_edge,
            pltpu.VMEM((2 * CHUNKS, SPLIT + 8, LANES), jnp.float32),
            pltpu.VMEM((PATCH * SPLIT // 2, LANES), jnp.float32),
            dma((2 * dates,)), dma((2 * dates,)),
            dma((dates, 2)), dma((dates, 2)), dma((2,)), dma((2,)), dma((SLABS - 1 + TABLES,)),
        ],
        compiler_params=pltpu.CompilerParams(
            vmem_limit_bytes=VMEM_LIMIT, collective_id=0, has_side_effects=True
        ),
        name="scene",
    )(*[pltpu.with_memory_space_constraint(t, pltpu.HBM) for t in tables])


def on_device(raw_echoes, azimuth_phase, band_offset, partners):
    scene = lax.axis_size("scene")
    dates = raw_echoes.shape[2]
    local = raw_echoes.shape[0] // SPLIT
    pairs = partners.size
    assert dates == 2 and raw_echoes.shape[3] == scene * STRIP
    left = left_table(1.0).reshape(2 * SPLIT, 2, scene, local)
    left = left.transpose(0, 1, 3, 2).reshape(2 * SPLIT, 2 * SPLIT)
    lines, bins = raw_echoes.shape[0], raw_echoes.shape[3]
    raw = raw_echoes.reshape(lines, 2, dates, bins // LANES, LANES)
    raw = raw.transpose(0, 1, 3, 2, 4).reshape(-1, LANES)
    phase = azimuth_phase.T
    result = run_scene(
        raw, band_offset, phase, left, scene, (2, dates, bins, lines)
    )
    result = jnp.broadcast_to(result, (pairs,) + result.shape)
    return result.reshape(pairs, 2, STRIP, -1).transpose(0, 3, 1, 2)


def solution(mesh):
    return jax.shard_map(
        on_device,
        mesh=mesh,
        in_specs=(
            P("scene", None, "stack", None),
            P("stack", "scene"),
            P(("stack", "scene")),
            P("stack", None),
        ),
        out_specs=P("stack", None, None, "scene"),
        check_vma=False,
    )
```

```python
import math

import jax
import jax.numpy as jnp
import numpy as np
from jax import lax
from jax.experimental import pallas as pl
from jax.experimental.pallas import tpu as pltpu
from jax.sharding import PartitionSpec as P

SPLIT = 64
LOOKS = 4
PATCH = 64
SHIFT = 8
TAPS = 2 * SHIFT - 1
EPSILON = 1e-06
STRIP = 32
GROUPS = STRIP // 2
LANES = 2 * SPLIT
CHUNKS = STRIP // 4
HALO_CHUNKS = CHUNKS // 2
HALF = STRIP // 2
BATCH = 8
STEPS = 8
TABLES = 5
SLABS = 4
VMEM_LIMIT = 40 * 1024 * 1024


def base_tables():
    k = np.arange(64)
    angle = 2.0 * np.pi * ((k[:, None] * k[None, :]) % 64) / 64.0
    return np.cos(angle), np.sin(angle)


def twiddle_tables():
    k = np.arange(SPLIT)
    angle = 2.0 * np.pi * ((k[:, None] * k[None, :]) % (SPLIT * SPLIT)) / (SPLIT * SPLIT)
    return (
        np.tile(np.cos(angle), (1, 2)).astype(np.float32),
        np.tile(np.sin(angle), (1, 2)).astype(np.float32),
    )


def bf16(table):
    return jnp.asarray(np.asarray(table, np.float32), jnp.bfloat16)


def left_table(direction):
    c, s = base_tables()
    return np.block([[c, direction * s], [-direction * s, c]])


def right_table(direction):
    c, s = base_tables()
    eye = np.eye(2)
    return np.block(
        [
            [np.kron(eye, c), np.kron(eye, -direction * s)],
            [np.kron(eye, direction * s), np.kron(eye, c)],
        ]
    )


def look_table():
    table = np.zeros((4, 2, 2, SPLIT, 2, 4, 2, SPLIT // LOOKS))
    for g in range(4):
        for c in range(2):
            for rb in range(2):
                for q in range(SPLIT):
                    table[g, c, rb, q, rb, g, c, q // LOOKS] = 1.0 / LOOKS
    return table.reshape(4 * 2 * 2 * SPLIT, 2 * 4 * 2 * SPLIT // LOOKS)


def patch_azimuth_table():
    c, s = base_tables()
    table = np.zeros((4, 4, 2, 16, 4, 2, 64))
    for p in range(4):
        part_c, part_s = c[16 * p : 16 * p + 16], s[16 * p : 16 * p + 16]
        for r in range(4):
            table[p, r, 0, :, r, 0] = part_c
            table[p, r, 1, :, r, 0] = part_s
            table[p, r, 0, :, r, 1] = -part_s
            table[p, r, 1, :, r, 1] = part_c
    return table.reshape(512, 512)


def patch_range_table():
    c, s = base_tables()
    return np.block([[c, s], [-s, c]])


def back_azimuth_table():
    c, s = base_tables()
    c, s = c[:, 16:48], s[:, 16:48]
    table = np.zeros((2, 4, 64, 2, 4, 32))
    for i in range(4):
        table[0, i, :, 0, i] = c
        table[1, i, :, 0, i] = -s
        table[0, i, :, 1, i] = s
        table[1, i, :, 1, i] = c
    return table.reshape(512, 256)


def back_range_table():
    c, s = base_tables()
    c, s = c[16:48], s[16:48]
    return np.block([[c, -s], [s, c]])


def dot(a, b):
    return jnp.dot(a, b, preferred_element_type=jnp.float32)


def lane_order():
    lane = np.arange(SPLIT)
    return 2 * (lane % (SPLIT // 2)) + lane // (SPLIT // 2)


def spectrum_side(table, axis):
    order = np.concatenate([SPLIT * half + lane_order() for half in range(4)])
    return np.take(table, order, axis=axis)


def cos_sin(angle):
    h = 0.5 * angle
    h2 = h * h
    sin_h = 1.0 / 6227020800.0
    for fact in (-39916800.0, 362880.0, -5040.0, 120.0, -6.0, 1.0):
        sin_h = sin_h * h2 + 1.0 / fact
    sin_h = sin_h * h
    cos_h = 1.0 / 479001600.0
    for fact in (-3628800.0, 40320.0, -720.0, 24.0, -2.0, 1.0):
        cos_h = cos_h * h2 + 1.0 / fact
    return 1.0 - 2.0 * sin_h * sin_h, 2.0 * sin_h * cos_h


def make_weights(g, band_ref, lines_ref, weight_ref, cos_ref, sin_ref):
    shape = (SPLIT, LANES)
    lane = lax.broadcasted_iota(jnp.int32, shape, 1)
    row = lax.broadcasted_iota(jnp.int32, shape, 0)
    half = SPLIT // 2
    k = row + SPLIT * (2 * (lane & (half - 1)) + ((lane & half) // half))
    total = SPLIT * SPLIT
    f = jnp.where(k < total // 2, k, k - total).astype(jnp.float32)
    ratio = f * (2.0 / total)
    band = jnp.where(lane < SPLIT, band_ref[g], band_ref[g + GROUPS]).astype(jnp.float32)
    s = band * (ratio * ratio - 0.5)
    n = jnp.floor(s + 0.5)
    y = s - n
    y2 = y * y
    pi = math.pi
    poly = -(pi**11) / 39916800.0
    for power, fact in ((9, 362880.0), (7, -5040.0), (5, 120.0), (3, -6.0), (1, 1.0)):
        poly = poly * y2 + (pi**power) / fact
    odd = n.astype(jnp.int32) & 1
    lobe = jnp.where(odd == 1, 1.0, -1.0) * (y * poly) * (1.0 / pi)
    cos_s, sin_s = cos_sin(s * (pi / 4.0))
    cos_s, sin_s = 0.5 * cos_s, 0.5 * sin_s
    for tap in range(TAPS):
        m = tap + 1 - SHIFT
        x = m - s
        sign = 1.0 if m % 2 == 0 else -1.0
        safe = jnp.where(x == 0.0, 1.0, x)
        sinc = jnp.where(x == 0.0, 1.0, (sign * lobe) / safe)
        window = 0.5 + math.cos(pi * m / 4.0) * cos_s + math.sin(pi * m / 4.0) * sin_s
        weight = jnp.where(jnp.abs(x) < SHIFT / 2.0, sinc * window, 0.0)
        weight_ref[g, tap] = jnp.concatenate([weight, weight], axis=1).astype(jnp.bfloat16)
    first = lines_ref[pl.ds(g, SPLIT // 2, stride=STRIP)]
    second = lines_ref[pl.ds(g + GROUPS, SPLIT // 2, stride=STRIP)]
    pieces = [first, pltpu.roll(first, SPLIT, 1), second, pltpu.roll(second, SPLIT, 1)]
    angle = jnp.concatenate(pieces, axis=0).T[:SPLIT]
    cos_ref[g], sin_ref[g] = cos_sin(angle)


def arrived_lines(wide_ref, i, sources, local, low):
    rows = []
    for c in range(2):
        for pair in range(wide_ref.shape[1]):
            one = wide_ref[c, pair, pl.ds(i, sources, stride=HALF)]
            two = wide_ref[c, pair, pl.ds(i + SHIFT, sources, stride=HALF)]
            rows.append(jnp.where(low[:sources], one, pltpu.roll(two, SPLIT, 1)))
            if local > 1:
                rows.append(jnp.where(low[:sources], pltpu.roll(one, SPLIT, 1), two))
    return jnp.concatenate(rows, axis=0).astype(jnp.bfloat16)


def scene_kernel(
    packed_ref, band_ref, phase_ref, table_ref, twiddle_ref,
    out_ref,
    raw_ref, spread_ref, recv_ref, lines_ref, wide_ref, weight_ref, cos_ref, sin_ref, ext_ref,
    rim_ref, up_ref, down_ref, before_ref, after_ref, focused_ref,
    own_ref, own_before_ref, own_after_ref, line_ref, grid_ref,
    send_sem, recv_sem, edge_send, edge_recv, look_send, look_recv,
    slabs, loads,
):
    scene = lax.axis_size("scene")
    me = lax.axis_index("scene")
    dates = raw_ref.shape[0]
    lines_held = raw_ref.shape[5]
    local = lines_held // SPLIT
    low = lax.broadcasted_iota(jnp.int32, (SPLIT, LANES), 1) < SPLIT
    lows = jnp.concatenate([low, low], axis=1)
    patches = SPLIT // 2

    left_ref, back_left_ref, range_ref, back_range_ref = (
        table_ref.at[rows, columns] for rows, columns in (
            (pl.ds(0, LANES), pl.ds(0, LANES)), (pl.ds(0, LANES), pl.ds(LANES, LANES)),
            (pl.ds(LANES, LANES), pl.ds(0, LANES)), (pl.ds(LANES, PATCH), pl.ds(LANES, LANES)),
        )
    )
    wide = 2 * LANES
    starts = np.cumsum([wide, wide, wide, 4 * wide, 2 * wide, 2 * wide]).tolist()
    right_ref, back_right_ref, look_ref, azimuth_one_ref, azimuth_two_ref, back_azimuth_ref = (
        table_ref.at[pl.ds(start, rows)]
        for start, rows in zip(starts, (wide, wide, 4 * wide, 2 * wide, 2 * wide, 2 * wide))
    )
    tc_ref, ts_ref = twiddle_ref.at[pl.ds(0, SPLIT)], twiddle_ref.at[pl.ds(SPLIT, SPLIT)]

    barrier = pltpu.get_barrier_semaphore()

    def greet(o, carry):
        pl.semaphore_signal(
            barrier, inc=1, device_id={"scene": lax.rem(me + o, scene)},
            device_id_type=pl.DeviceIdType.MESH,
        )
        return carry

    lax.fori_loop(1, scene, greet, 0)
    for load in slabs + loads:
        load.start()
    piece = packed_ref.shape[0] // (2 * SLABS)
    for n, slab in enumerate(slabs):
        slab.wait()
        for half in range(2):
            rows = pl.ds((2 * n + half) * piece, piece)
            spread_ref[rows] = packed_ref[rows].astype(jnp.float32)
    owners = LANES // STRIP
    tiles = scene // owners
    stride = 2 * tiles * dates

    def piece_of(ref, k, owner):
        return ref.at[k // 2, k % 2, owner]

    def strip_copy(k, peer):
        return pltpu.make_async_remote_copy(
            src_ref=piece_of(raw_ref, k, peer),
            dst_ref=piece_of(recv_ref, k, me),
            send_sem=send_sem.at[k],
            recv_sem=recv_sem.at[k],
            device_id={"scene": peer},
            device_id_type=pl.DeviceIdType.MESH,
        )

    def own_copy(k):
        return pltpu.make_async_copy(
            piece_of(raw_ref, k, me), piece_of(recv_ref, k, me), recv_sem.at[k]
        )

    def turn(d, tile):
        for c in range(2):
            start = (c * tiles + tile) * dates + d
            bins = spread_ref[pl.ds(start, lines_held, stride=stride)].T
            for n in range(owners):
                own = bins[n * STRIP : (n + 1) * STRIP]
                rim = jnp.concatenate([own[:SHIFT], own[STRIP - SHIFT :]], axis=0)
                core = own[SHIFT : STRIP - SHIFT]
                raw_ref[d, 0, tile * owners + n, c] = rim.astype(jnp.bfloat16)
                raw_ref[d, 1, tile * owners + n, c] = core.astype(jnp.bfloat16)

    def turn_and_send(d):
        def body(i, carry):
            tile = lax.rem(me // owners + tiles // 2 + i, tiles)
            turn(d, tile)

            @pl.when(i == 0)
            def _():
                if d == 0:
                    pl.semaphore_wait(barrier, scene - 1)

            for n in range(owners):
                peer = tile * owners + n

                @pl.when(peer != me)
                def _():
                    strip_copy(2 * d, peer).start()

            return carry

        lax.fori_loop(0, tiles, body, 0)
        own_copy(2 * d).start()

    def far(i):
        half = (i + 1) // 2
        return scene // 2 + half * (1 - 2 * lax.rem(i, 2))

    def send_all(k):
        def send(i, carry):
            strip_copy(k, lax.rem(me + far(i), scene)).start()
            return carry

        lax.fori_loop(0, scene - 1, send, 0)
        own_copy(k).start()

    def arrive_all(k):
        held = recv_ref.at[k // 2, k % 2]
        pltpu.make_async_copy(held, held, recv_sem.at[k]).wait()

    def sent_all(k):
        held = raw_ref.at[k // 2, k % 2, pl.ds(0, scene - 1)]
        pltpu.make_async_copy(held, held, send_sem.at[k]).wait()

    for d in range(dates):
        turn_and_send(d)

    for load in loads:
        load.wait()

    for part in range(SPLIT // 2):
        lines_ref[pl.ds(part * STRIP, STRIP)] = phase_ref[:, part * LANES : (part + 1) * LANES]

    def weigh(g, carry):
        make_weights(g, band_ref, lines_ref, weight_ref, cos_ref, sin_ref)
        return carry

    lax.fori_loop(0, GROUPS, weigh, 0)

    @pl.when(me == 0)
    def _():
        before_ref[...] = jnp.zeros(before_ref.shape, before_ref.dtype)
        own_before_ref[...] = jnp.zeros(own_before_ref.shape, own_before_ref.dtype)

    @pl.when(me == scene - 1)
    def _():
        after_ref[...] = jnp.zeros(after_ref.shape, after_ref.dtype)
        own_after_ref[...] = jnp.zeros(own_after_ref.shape, own_after_ref.dtype)

    line_ref[...] = jnp.zeros(line_ref.shape, jnp.float32)

    def neighbour(source, target, send, recv, step):
        return pltpu.make_async_remote_copy(
            src_ref=source, dst_ref=target, send_sem=send, recv_sem=recv,
            device_id={"scene": me + step}, device_id_type=pl.DeviceIdType.MESH,
        )

    def edge_copies(d):
        return (
            neighbour(
                up_ref.at[d, pl.ds(1, SHIFT - 1)], before_ref.at[d, pl.ds(1, SHIFT - 1)],
                edge_send.at[d, 0], edge_recv.at[d, 0], 1,
            ),
            neighbour(
                down_ref.at[d, pl.ds(0, SHIFT - 1)], after_ref.at[d, pl.ds(0, SHIFT - 1)],
                edge_send.at[d, 1], edge_recv.at[d, 1], -1,
            ),
        )

    def look_copies(big):
        return (
            neighbour(
                own_ref.at[HALO_CHUNKS + big], own_before_ref.at[big],
                look_send.at[0], look_recv.at[0], 1,
            ),
            neighbour(
                own_ref.at[big], own_after_ref.at[big],
                look_send.at[1], look_recv.at[1], -1,
            ),
        )

    def start_pair(copies):
        @pl.when(me < scene - 1)
        def _():
            copies[0].start()

        @pl.when(me > 0)
        def _():
            copies[1].start()

    def wait_pair(copies):
        @pl.when(me > 0)
        def _():
            copies[0].wait_recv()
            copies[1].wait_send()

        @pl.when(me < scene - 1)
        def _():
            copies[1].wait_recv()
            copies[0].wait_send()

    def widen(d, part):
        def body(source, carry):
            start = pl.multiple_of(source * HALF, HALF)
            for c in range(2):
                strip = recv_ref[d, part, source, c].astype(jnp.float32)
                for pair in range(wide_ref.shape[1]):
                    kept = strip[:, pair * LANES : (pair + 1) * LANES]
                    wide_ref[c, pair, pl.ds(start, HALF), : kept.shape[1]] = kept
            return carry

        lax.fori_loop(0, scene, body, 0)

    def transform(first, count):
        held = [arrived_lines(wide_ref, first + n, scene, local, low) for n in range(count)]
        mixed = dot(left_ref[...], jnp.concatenate(held, axis=1))
        tc, ts = tc_ref[...], ts_ref[...]
        segments = []
        for n in range(count):
            re, im = (mixed[k : k + SPLIT, n * LANES : (n + 1) * LANES] for k in (0, SPLIT))
            segments.append(jnp.concatenate([re * tc + im * ts, im * tc - re * ts], axis=1))
        stacked = jnp.concatenate(segments, axis=0).astype(jnp.bfloat16)
        spectra = dot(stacked, right_ref[...])
        return [spectra[n * SPLIT : (n + 1) * SPLIT] for n in range(count)]

    def turned(pair):
        parts = (pair[:, :LANES], pair[:, LANES:])
        return jnp.concatenate([pltpu.roll(part, SPLIT, 1) for part in parts], axis=1)

    def forward_rim(d):
        widen(d, 0)

        def body(step, carry):
            for n, rim in enumerate(transform(BATCH * step, BATCH)):
                i = BATCH * step + n
                flipped = turned(rim)
                rim_ref[d, i] = rim
                down = jnp.where(low, rim[:, :LANES], flipped[:, LANES:])
                up = jnp.where(low, flipped[:, :LANES], rim[:, LANES:])
                down_ref[d, i] = down.astype(jnp.bfloat16)
                up_ref[d, i] = up.astype(jnp.bfloat16)
            return carry

        lax.fori_loop(0, SHIFT // BATCH, body, 0, unroll=True)
        start_pair(edge_copies(d))

    def forward_core(d):
        widen(d, 1)
        wait_pair(edge_copies(d))

        def body(step, carry):
            for n, core in enumerate(transform(BATCH * step, BATCH)):
                i = BATCH * step + n
                before = before_ref[d, i].astype(jnp.float32)
                after = after_ref[d, i].astype(jnp.float32)
                before = jnp.concatenate([before, pltpu.roll(before, SPLIT, 1)], axis=1)
                after = jnp.concatenate([pltpu.roll(after, SPLIT, 1), after], axis=1)
                rim, flipped = rim_ref[d, i], turned(core)
                ext_ref[i] = jnp.where(lows, before, flipped).astype(jnp.bfloat16)
                ext_ref[SHIFT + i] = jnp.where(lows, rim, core).astype(jnp.bfloat16)
                ext_ref[2 * SHIFT + i] = jnp.where(lows, core, rim).astype(jnp.bfloat16)
                ext_ref[3 * SHIFT + i] = jnp.where(lows, flipped, after).astype(jnp.bfloat16)
            return carry

        lax.fori_loop(0, SHIFT // BATCH, body, 0, unroll=True)

    def migrate(big):
        totals = [[] for _ in range(4)]
        for top in range(0, SPLIT, 8):
            rows = slice(top, top + 8)
            data = [ext_ref[4 * big + n + 1, rows] for n in range(TAPS + 3)]
            for j in range(4):
                sums = []
                for first in range(2):
                    total = weight_ref[4 * big + j, first, rows] * data[j + first]
                    for tap in range(first + 2, TAPS, 2):
                        total += weight_ref[4 * big + j, tap, rows] * data[j + tap]
                    sums.append(total.astype(jnp.float32))
                totals[j].append(sums[0] + sums[1])
        return [jnp.concatenate(total, axis=0) for total in totals]

    def focus(big):
        compressed = []
        for j, migrated in enumerate(migrate(big)):
            re, im = migrated[:, :LANES], migrated[:, LANES:]
            cos_phase, sin_phase = cos_ref[4 * big + j], sin_ref[4 * big + j]
            parts = [re * cos_phase - im * sin_phase, im * cos_phase + re * sin_phase]
            compressed.append(jnp.concatenate(parts, axis=1).astype(jnp.bfloat16))
        first = dot(jnp.concatenate(compressed, axis=0), back_right_ref[...])
        tc, ts = tc_ref[...], ts_ref[...]
        segments = []
        for j in range(4):
            rows = first[j * SPLIT : (j + 1) * SPLIT]
            re, im = rows[:, :LANES], rows[:, LANES:]
            segments.append(jnp.concatenate([re * tc - im * ts, im * tc + re * ts], axis=0))
        stacked = jnp.concatenate(segments, axis=1).astype(jnp.bfloat16)
        second = dot(back_left_ref[...], stacked).astype(jnp.bfloat16)
        return [second[:, j * LANES : (j + 1) * LANES] for j in range(4)]

    def focus_first(big, carry):
        for j, focused in enumerate(focus(big)):
            focused_ref[4 * big + j] = focused
        return carry

    def focus_last(step, carry):
        products = []
        for n in range(2):
            big = 2 * step + n
            pieces = []
            for j, focused in enumerate(focus(big)):
                leading = focused.astype(jnp.float32)
                trailing = focused_ref[4 * big + j].astype(jnp.float32)
                lr, li = leading[:SPLIT], leading[SPLIT:]
                tr, ti = trailing[:SPLIT], trailing[SPLIT:]
                product = jnp.concatenate([lr * tr + li * ti, li * tr - lr * ti], axis=1)
                pieces.append(product.astype(jnp.bfloat16))
            products.append(jnp.concatenate(pieces, axis=1))
        looked = dot(jnp.concatenate(products, axis=0), look_ref[...]).astype(jnp.bfloat16)
        for n in range(2):
            big, rows = 2 * step + n, slice(n * SPLIT, (n + 1) * SPLIT)
            own_ref[big] = looked[rows, :LANES]
            own_ref[HALO_CHUNKS + big] = looked[rows, LANES:]
            start_pair(look_copies(big))
        return carry

    send_all(1)
    arrive_all(0)
    forward_rim(0)
    arrive_all(2)
    send_all(3)
    forward_rim(1)
    arrive_all(1)
    forward_core(0)
    lax.fori_loop(0, GROUPS // 4, focus_first, 0, unroll=2)
    arrive_all(3)
    forward_core(1)
    lax.fori_loop(0, GROUPS // 8, focus_last, 0)

    def lines_of(*firsts):
        rows = []
        for chunk in (first + j for first in firsts for j in range(HALO_CHUNKS)):
            parts = [line_ref[chunk, pl.ds(p, patches, stride=2)] for p in range(4)]
            rows.append(jnp.concatenate(parts, axis=1))
        lines = jnp.concatenate(rows, axis=0).astype(jnp.bfloat16)
        results = [dot(lines, ref[...]) for ref in (azimuth_one_ref, azimuth_two_ref)]
        for n, first in enumerate(firsts):
            for j in range(HALO_CHUNKS):
                for r in range(4):
                    part = results[r // 2][(n * HALO_CHUNKS + j) * patches :][:patches]
                    part = part[:, (r % 2) * LANES : (r % 2 + 1) * LANES]
                    grid_ref[pl.ds(((first + j) * 4 + r) * patches, patches)] = part

    for j in range(CHUNKS):
        line_ref[HALO_CHUNKS + j, pl.ds(1, SPLIT)] = own_ref[j].astype(jnp.float32)
    lines_of(HALO_CHUNKS, 2 * HALO_CHUNKS)
    for k in range(2 * dates):
        sent_all(k)
    wait_pair(
        (
            neighbour(own_before_ref, own_before_ref, look_send.at[0], look_recv.at[0], 1),
            neighbour(own_after_ref, own_after_ref, look_send.at[1], look_recv.at[1], -1),
        )
    )
    for j in range(HALO_CHUNKS):
        line_ref[j, pl.ds(1, SPLIT)] = own_before_ref[j].astype(jnp.float32)
        line_ref[HALO_CHUNKS + CHUNKS + j, pl.ds(1, SPLIT)] = own_after_ref[j].astype(jnp.float32)
    lines_of(0, HALO_CHUNKS + CHUNKS)
    lane = lax.broadcasted_iota(jnp.int32, (PATCH, LANES), 1)
    opening, closing = lane % PATCH == 0, lane % PATCH == PATCH - 1

    def filter_patches(step, carry):
        stacks = []
        for pair in range(2 * STEPS):
            one = grid_ref[pl.ds(4 * STEPS * step + 2 * pair, PATCH, stride=patches)]
            two = grid_ref[pl.ds(4 * STEPS * step + 2 * pair + 1, PATCH, stride=patches)]
            re = jnp.where(low, one, pltpu.roll(two, PATCH, 1))
            im = jnp.where(low, pltpu.roll(one, PATCH, 1), two)
            stacks.append(jnp.concatenate([re, im], axis=0).astype(jnp.bfloat16))
        spectra = dot(range_ref[...], jnp.concatenate(stacks, axis=1))
        kept_re, kept_im = [], []
        for pair in range(2 * STEPS):
            re = spectra[:PATCH, pair * LANES : (pair + 1) * LANES]
            im = spectra[PATCH:, pair * LANES : (pair + 1) * LANES]
            power = re * re + im * im + EPSILON
            magnitude = power * lax.rsqrt(power)
            rows = magnitude + pltpu.roll(magnitude, 1, 0) + pltpu.roll(magnitude, PATCH - 1, 0)
            left = jnp.where(opening, pltpu.roll(rows, PATCH + 1, 1), pltpu.roll(rows, 1, 1))
            right = jnp.where(closing, pltpu.roll(rows, PATCH - 1, 1), pltpu.roll(rows, LANES - 1, 1))
            column = jnp.sum(magnitude, axis=0, keepdims=True)
            first = jnp.sum(jnp.where(low[:1], column, 0.0), axis=1, keepdims=True)
            second = jnp.sum(jnp.where(low[:1], 0.0, column), axis=1, keepdims=True)
            level = jnp.where(low[:1], first, second) * (1.0 / (PATCH * PATCH)) + EPSILON
            gain = (rows + left + right) * ((1.0 / 9.0) / level)
            kept_re.append((re * gain).astype(jnp.bfloat16))
            kept_im.append((im * gain).astype(jnp.bfloat16))
        kept = [
            jnp.concatenate(kept_re[2 * n : 2 * n + 2] + kept_im[2 * n : 2 * n + 2], axis=1)
            for n in range(STEPS)
        ]
        back = dot(jnp.concatenate(kept, axis=0), back_azimuth_ref[...]).astype(jnp.bfloat16)
        stacked = []
        for n in range(STEPS):
            rows = back[n * PATCH : (n + 1) * PATCH]
            stacked.append(jnp.concatenate([rows[:, :LANES], rows[:, LANES:]], axis=0))
        result = dot(back_range_ref[...], jnp.concatenate(stacked, axis=1))
        width = STEPS * LANES
        start = pl.multiple_of(step * width, width)
        out_ref[:, pl.ds(start, width)] = result.astype(jnp.bfloat16)
        return carry

    lax.fori_loop(0, patches // (4 * STEPS), filter_patches, 0, unroll=1)


def loading_kernel(*refs):
    held, out_ref, kept, load_sem = refs[:TABLES], refs[TABLES], refs[TABLES + 1 : -1], refs[-1]
    rows = held[0].shape[0] // SLABS
    slabs = [
        pltpu.make_async_copy(
            held[0].at[pl.ds(n * rows, rows)], kept[0].at[pl.ds(n * rows, rows)], load_sem.at[n]
        )
        for n in range(SLABS)
    ]
    loads = [
        pltpu.make_async_copy(held[i], kept[i], load_sem.at[SLABS - 1 + i])
        for i in range(1, TABLES)
    ]
    scene_kernel(*kept[:TABLES], out_ref, *kept[TABLES:], slabs, loads)


def table_stack(left):
    unit = 1.0 / SPLIT
    back_range = np.zeros((LANES, LANES))
    back_range[:PATCH] = back_range_table() * unit
    azimuth = patch_azimuth_table()
    return np.concatenate(
        [
            np.concatenate([left, left_table(-1.0) * unit], axis=1),
            np.concatenate([patch_range_table() * unit, back_range], axis=1),
            spectrum_side(right_table(1.0), 1) * unit,
            spectrum_side(right_table(-1.0), 0),
            look_table(),
            azimuth[:, : 2 * LANES],
            azimuth[:, 2 * LANES :],
            back_azimuth_table(),
        ]
    )


def run_scene(raw, band, phase, left, scene, shape):
    dates, width = shape[1], shape[3]
    looks = SPLIT * SPLIT // LOOKS
    vmem = pl.BlockSpec(memory_space=pltpu.VMEM)
    plane = (GROUPS, SPLIT, LANES)
    edge = pltpu.VMEM((dates, SHIFT, SPLIT, LANES), jnp.bfloat16)
    looked_edge = pltpu.VMEM((HALO_CHUNKS, SPLIT, LANES), jnp.bfloat16)
    dma = pltpu.SemaphoreType.DMA
    twiddles = np.concatenate(twiddle_tables())
    tables = (raw, band, phase, bf16(table_stack(left)), jnp.asarray(twiddles))
    return pl.pallas_call(
        loading_kernel,
        in_specs=[pl.BlockSpec(memory_space=pl.ANY)] * TABLES,
        out_specs=vmem,
        out_shape=pltpu.VMEM((2 * STRIP, looks), jnp.bfloat16),
        scratch_shapes=[
            (pltpu.SMEM if table is band else pltpu.VMEM)(table.shape, table.dtype)
            for table in tables
        ]
        + [
            pltpu.VMEM((dates, 2, scene, 2, HALF, width), jnp.bfloat16),
            pltpu.VMEM(raw.shape, jnp.float32),
            pltpu.VMEM((dates, 2, scene, 2, HALF, width), jnp.bfloat16),
            pltpu.VMEM((STRIP * SPLIT // 2, LANES), jnp.float32),
            pltpu.VMEM((2, pl.cdiv(width, LANES), scene * HALF, LANES), jnp.float32),
            pltpu.VMEM((GROUPS, TAPS, SPLIT, 2 * LANES), jnp.bfloat16),
            pltpu.VMEM(plane, jnp.float32),
            pltpu.VMEM(plane, jnp.float32),
            pltpu.VMEM((GROUPS + 2 * SHIFT, SPLIT, 2 * LANES), jnp.bfloat16),
            pltpu.VMEM((dates, SHIFT, SPLIT, 2 * LANES), jnp.float32),
            edge, edge, edge, edge,
            pltpu.VMEM((GROUPS, 2 * SPLIT, LANES), jnp.bfloat16),
            pltpu.VMEM((CHUNKS, SPLIT, LANES), jnp.bfloat16),
            looked_edge,
            looked_edge,
            pltpu.VMEM((2 * CHUNKS, SPLIT + 8, LANES), jnp.float32),
            pltpu.VMEM((PATCH * SPLIT // 2, LANES), jnp.float32),
            dma((2 * dates,)), dma((2 * dates,)),
            dma((dates, 2)), dma((dates, 2)), dma((2,)), dma((2,)), dma((SLABS - 1 + TABLES,)),
        ],
        compiler_params=pltpu.CompilerParams(
            vmem_limit_bytes=VMEM_LIMIT, collective_id=0, has_side_effects=True
        ),
        name="scene",
    )(*[pltpu.with_memory_space_constraint(t, pltpu.HBM) for t in tables])


def on_device(raw_echoes, azimuth_phase, band_offset, partners):
    scene = lax.axis_size("scene")
    dates = raw_echoes.shape[2]
    local = raw_echoes.shape[0] // SPLIT
    pairs = partners.size
    assert dates == 2 and raw_echoes.shape[3] == scene * STRIP
    left = left_table(1.0).reshape(2 * SPLIT, 2, scene, local)
    left = left.transpose(0, 1, 3, 2).reshape(2 * SPLIT, 2 * SPLIT)
    lines, bins = raw_echoes.shape[0], raw_echoes.shape[3]
    raw = raw_echoes.reshape(lines, 2, dates, bins // LANES, LANES)
    raw = raw.transpose(0, 1, 3, 2, 4).reshape(-1, LANES)
    phase = azimuth_phase.T
    result = run_scene(
        raw, band_offset, phase, left, scene, (2, dates, bins, lines)
    )
    result = jnp.broadcast_to(result, (pairs,) + result.shape)
    return result.reshape(pairs, 2, STRIP, -1).transpose(0, 3, 1, 2)


def solution(mesh):
    return jax.shard_map(
        on_device,
        mesh=mesh,
        in_specs=(
            P("scene", None, "stack", None),
            P("stack", "scene"),
            P(("stack", "scene")),
            P("stack", None),
        ),
        out_specs=P("stack", None, None, "scene"),
        check_vma=False,
    )
```

```python
import math

import jax
import jax.numpy as jnp
import numpy as np
from jax import lax
from jax.experimental import pallas as pl
from jax.experimental.pallas import tpu as pltpu
from jax.sharding import PartitionSpec as P

SPLIT = 64
LOOKS = 4
PATCH = 64
SHIFT = 8
TAPS = 2 * SHIFT - 1
EPSILON = 1e-06
STRIP = 32
GROUPS = STRIP // 2
LANES = 2 * SPLIT
CHUNKS = STRIP // 4
HALO_CHUNKS = CHUNKS // 2
HALF = STRIP // 2
HALF_LANES = 32
UPS, DOWNS = SHIFT - 2, SHIFT - 3
STEPS = 8
TABLES = 5
SLABS = 4
VMEM_LIMIT = 40 * 1024 * 1024


def base_tables():
    k = np.arange(64)
    angle = 2.0 * np.pi * ((k[:, None] * k[None, :]) % 64) / 64.0
    return np.cos(angle), np.sin(angle)


def twiddle_tables():
    k = np.arange(SPLIT)
    angle = 2.0 * np.pi * ((k[:, None] * k[None, :]) % (SPLIT * SPLIT)) / (SPLIT * SPLIT)
    return (
        np.tile(np.cos(angle), (1, 2)).astype(np.float32),
        np.tile(np.sin(angle), (1, 2)).astype(np.float32),
    )


def bf16(table):
    return jnp.asarray(np.asarray(table, np.float32), jnp.bfloat16)


def left_table(direction):
    c, s = base_tables()
    return np.block([[c, direction * s], [-direction * s, c]])


def right_table(direction):
    c, s = base_tables()
    eye = np.eye(2)
    return np.block(
        [
            [np.kron(eye, c), np.kron(eye, -direction * s)],
            [np.kron(eye, direction * s), np.kron(eye, c)],
        ]
    )


def look_table():
    table = np.zeros((4, 2, 2, SPLIT, 2, 4, 2, SPLIT // LOOKS))
    for g in range(4):
        for c in range(2):
            for rb in range(2):
                for q in range(SPLIT):
                    table[g, c, rb, q, rb, g, c, q // LOOKS] = 1.0 / LOOKS
    return table.reshape(4 * 2 * 2 * SPLIT, 2 * 4 * 2 * SPLIT // LOOKS)


def patch_azimuth_table():
    c, s = base_tables()
    table = np.zeros((4, 4, 2, 16, 4, 2, 64))
    for p in range(4):
        part_c, part_s = c[16 * p : 16 * p + 16], s[16 * p : 16 * p + 16]
        for r in range(4):
            table[p, r, 0, :, r, 0] = part_c
            table[p, r, 1, :, r, 0] = part_s
            table[p, r, 0, :, r, 1] = -part_s
            table[p, r, 1, :, r, 1] = part_c
    return table.reshape(512, 512)


def patch_range_table():
    c, s = base_tables()
    return np.block([[c, s], [-s, c]])


def smooth_table():
    k = np.arange(PATCH)
    gap = (k[:, None] - k[None, :]) % PATCH
    near = ((gap <= 1) | (gap == PATCH - 1)).astype(np.float64)
    eye = np.eye(2)
    return np.concatenate([np.kron(eye, near), np.kron(eye, np.ones((PATCH, PATCH)))], axis=1)


def back_azimuth_table():
    c, s = base_tables()
    c, s = c[:, 16:48], s[:, 16:48]
    table = np.zeros((2, 4, 64, 2, 4, 32))
    for i in range(4):
        table[0, i, :, 0, i] = c
        table[1, i, :, 0, i] = -s
        table[0, i, :, 1, i] = s
        table[1, i, :, 1, i] = c
    return table.reshape(512, 256)


def back_range_table():
    c, s = base_tables()
    c, s = c[16:48], s[16:48]
    return np.block([[c, -s], [s, c]])


def dot(a, b):
    return jnp.dot(a, b, preferred_element_type=jnp.float32)


def lane_order():
    quarter = SPLIT // 4
    places = np.arange(SPLIT // 2)
    fast = places[quarter // 2 : 3 * quarter // 2]
    slow = np.concatenate([places[: quarter // 2], places[3 * quarter // 2 :]])
    return np.concatenate([2 * fast, 2 * fast + 1, 2 * slow, 2 * slow + 1])


def spectrum_side(table, axis):
    order = np.concatenate([SPLIT * half + lane_order() for half in range(4)])
    return np.take(table, order, axis=axis)


def cos_sin(angle):
    h = 0.5 * angle
    h2 = h * h
    sin_h = 1.0 / 6227020800.0
    for fact in (-39916800.0, 362880.0, -5040.0, 120.0, -6.0, 1.0):
        sin_h = sin_h * h2 + 1.0 / fact
    sin_h = sin_h * h
    cos_h = 1.0 / 479001600.0
    for fact in (-3628800.0, 40320.0, -720.0, 24.0, -2.0, 1.0):
        cos_h = cos_h * h2 + 1.0 / fact
    return 1.0 - 2.0 * sin_h * sin_h, 2.0 * sin_h * cos_h


def make_weights(g, band_ref, lines_ref, weight_ref, cos_ref, sin_ref):
    shape = (SPLIT, LANES)
    lane = lax.broadcasted_iota(jnp.int32, shape, 1)
    row = lax.broadcasted_iota(jnp.int32, shape, 0)
    quarter = SPLIT // 4
    place, odd = lane & (quarter - 1), (lane & quarter) // quarter
    slow = jnp.where(place < quarter // 2, place, place + quarter)
    place = jnp.where((lane & (2 * quarter)) != 0, slow, place + quarter // 2)
    k = row + SPLIT * (2 * place + odd)
    total = SPLIT * SPLIT
    f = jnp.where(k < total // 2, k, k - total).astype(jnp.float32)
    ratio = f * (2.0 / total)
    band = jnp.where(lane < SPLIT, band_ref[g], band_ref[g + GROUPS]).astype(jnp.float32)
    s = band * (ratio * ratio - 0.5)
    n = jnp.floor(s + 0.5)
    y = s - n
    y2 = y * y
    pi = math.pi
    poly = -(pi**11) / 39916800.0
    for power, fact in ((9, 362880.0), (7, -5040.0), (5, 120.0), (3, -6.0), (1, 1.0)):
        poly = poly * y2 + (pi**power) / fact
    odd = n.astype(jnp.int32) & 1
    lobe = jnp.where(odd == 1, 1.0, -1.0) * (y * poly) * (1.0 / pi)
    cos_s, sin_s = cos_sin(s * (pi / 4.0))
    cos_s, sin_s = 0.5 * cos_s, 0.5 * sin_s
    for tap in range(TAPS):
        m = tap + 1 - SHIFT
        x = m - s
        sign = 1.0 if m % 2 == 0 else -1.0
        safe = jnp.where(x == 0.0, 1.0, x)
        sinc = jnp.where(x == 0.0, 1.0, (sign * lobe) / safe)
        window = 0.5 + math.cos(pi * m / 4.0) * cos_s + math.sin(pi * m / 4.0) * sin_s
        weight = jnp.where(jnp.abs(x) < SHIFT / 2.0, sinc * window, 0.0)
        weight_ref[g, tap] = jnp.concatenate([weight, weight], axis=1).astype(jnp.bfloat16)
    first = lines_ref[pl.ds(g, SPLIT // 2, stride=STRIP)]
    second = lines_ref[pl.ds(g + GROUPS, SPLIT // 2, stride=STRIP)]
    cuts = (0, quarter // 2, 3 * quarter // 2, SPLIT // 2)
    pieces = []
    for even in (first, second):
        both = (even, pltpu.roll(even, SPLIT, 1))
        thirds = [[part[a:b] for a, b in zip(cuts, cuts[1:])] for part in both]
        pieces += [thirds[0][1], thirds[1][1]]
        pieces += [thirds[0][0], thirds[0][2], thirds[1][0], thirds[1][2]]
    angle = jnp.concatenate(pieces, axis=0).T[:SPLIT]
    cos_ref[g], sin_ref[g] = cos_sin(angle)


def arrived_lines(wide_ref, i, sources, local, low):
    rows = []
    for c in range(2):
        for pair in range(wide_ref.shape[1]):
            one = wide_ref[c, pair, pl.ds(i, sources, stride=HALF)]
            two = wide_ref[c, pair, pl.ds(i + SHIFT, sources, stride=HALF)]
            rows.append(jnp.where(low[:sources], one, pltpu.roll(two, SPLIT, 1)))
            if local > 1:
                rows.append(jnp.where(low[:sources], pltpu.roll(one, SPLIT, 1), two))
    return jnp.concatenate(rows, axis=0).astype(jnp.bfloat16)


def scene_kernel(
    packed_ref, band_ref, phase_ref, table_ref, twiddle_ref,
    out_ref,
    raw_ref, spread_ref, recv_ref, lines_ref, wide_ref, weight_ref, cos_ref, sin_ref, ext_ref,
    rim_ref, up_ref, down_ref, before_ref, after_ref, focused_ref,
    own_ref, own_before_ref, own_after_ref, line_ref, grid_ref,
    send_sem, recv_sem, edge_send, edge_recv, look_send, look_recv,
    slabs, loads,
):
    scene = lax.axis_size("scene")
    me = lax.axis_index("scene")
    dates = raw_ref.shape[0]
    lines_held = raw_ref.shape[5]
    local = lines_held // SPLIT
    low = lax.broadcasted_iota(jnp.int32, (SPLIT, LANES), 1) < SPLIT
    lows = jnp.concatenate([low, low], axis=1)
    fast = lax.broadcasted_iota(jnp.int32, (SPLIT, LANES), 1) % SPLIT < HALF_LANES
    patches = SPLIT // 2

    left_ref, back_left_ref, range_ref, back_range_ref = (
        table_ref.at[rows, columns] for rows, columns in (
            (pl.ds(0, LANES), pl.ds(0, LANES)), (pl.ds(0, LANES), pl.ds(LANES, LANES)),
            (pl.ds(LANES, LANES), pl.ds(0, LANES)), (pl.ds(LANES, PATCH), pl.ds(LANES, LANES)),
        )
    )
    wide = 2 * LANES
    starts = np.cumsum([wide, wide, wide, 4 * wide, 2 * wide, 2 * wide, 2 * wide]).tolist()
    (
        right_ref, back_right_ref, look_ref, azimuth_one_ref, azimuth_two_ref,
        back_azimuth_ref, smooth_ref,
    ) = (
        table_ref.at[pl.ds(start, rows)]
        for start, rows in zip(starts, (wide, wide, 4 * wide, 2 * wide, 2 * wide, 2 * wide, LANES))
    )
    tc_ref, ts_ref = twiddle_ref.at[pl.ds(0, SPLIT)], twiddle_ref.at[pl.ds(SPLIT, SPLIT)]

    barrier = pltpu.get_barrier_semaphore()

    def greet(o, carry):
        pl.semaphore_signal(
            barrier, inc=1, device_id={"scene": lax.rem(me + o, scene)},
            device_id_type=pl.DeviceIdType.MESH,
        )
        return carry

    lax.fori_loop(1, scene, greet, 0)
    for load in slabs + loads:
        load.start()
    piece = packed_ref.shape[0] // (2 * SLABS)
    for n, slab in enumerate(slabs):
        slab.wait()
        for half in range(2):
            rows = pl.ds((2 * n + half) * piece, piece)
            spread_ref[rows] = packed_ref[rows].astype(jnp.float32)
    owners = LANES // STRIP
    tiles = scene // owners
    stride = 2 * tiles * dates

    def piece_of(ref, k, owner):
        return ref.at[k // 2, k % 2, owner]

    def strip_copy(k, peer):
        return pltpu.make_async_remote_copy(
            src_ref=piece_of(raw_ref, k, peer),
            dst_ref=piece_of(recv_ref, k, me),
            send_sem=send_sem.at[k],
            recv_sem=recv_sem.at[k],
            device_id={"scene": peer},
            device_id_type=pl.DeviceIdType.MESH,
        )

    def own_copy(k):
        return pltpu.make_async_copy(
            piece_of(raw_ref, k, me), piece_of(recv_ref, k, me), recv_sem.at[k]
        )

    def turn(d, tile):
        for c in range(2):
            start = (c * tiles + tile) * dates + d
            bins = spread_ref[pl.ds(start, lines_held, stride=stride)].T
            for n in range(owners):
                own = bins[n * STRIP : (n + 1) * STRIP]
                rim = jnp.concatenate([own[:SHIFT], own[STRIP - SHIFT :]], axis=0)
                core = own[SHIFT : STRIP - SHIFT]
                raw_ref[d, 0, tile * owners + n, c] = rim.astype(jnp.bfloat16)
                raw_ref[d, 1, tile * owners + n, c] = core.astype(jnp.bfloat16)

    def turn_and_send(d):
        def body(i, carry):
            tile = lax.rem(me // owners + tiles // 2 + i, tiles)
            turn(d, tile)

            @pl.when(i == 0)
            def _():
                if d == 0:
                    pl.semaphore_wait(barrier, scene - 1)

            for n in range(owners):
                peer = tile * owners + n

                @pl.when(peer != me)
                def _():
                    strip_copy(2 * d, peer).start()

            return carry

        lax.fori_loop(0, tiles, body, 0)
        own_copy(2 * d).start()

    def far(i):
        half = (i + 1) // 2
        return scene // 2 + half * (1 - 2 * lax.rem(i, 2))

    def send_all(k):
        def send(i, carry):
            strip_copy(k, lax.rem(me + far(i), scene)).start()
            return carry

        lax.fori_loop(0, scene - 1, send, 0)
        own_copy(k).start()

    def arrive_all(k):
        held = recv_ref.at[k // 2, k % 2]
        pltpu.make_async_copy(held, held, recv_sem.at[k]).wait()

    def sent_all(k):
        held = raw_ref.at[k // 2, k % 2, pl.ds(0, scene - 1)]
        pltpu.make_async_copy(held, held, send_sem.at[k]).wait()

    for d in range(dates):
        turn_and_send(d)

    for load in loads:
        load.wait()

    for part in range(SPLIT // 2):
        lines_ref[pl.ds(part * STRIP, STRIP)] = phase_ref[:, part * LANES : (part + 1) * LANES]

    def weigh(g, carry):
        make_weights(g, band_ref, lines_ref, weight_ref, cos_ref, sin_ref)
        return carry

    lax.fori_loop(0, GROUPS, weigh, 0)

    @pl.when(me == 0)
    def _():
        before_ref[...] = jnp.zeros(before_ref.shape, before_ref.dtype)
        own_before_ref[...] = jnp.zeros(own_before_ref.shape, own_before_ref.dtype)

    @pl.when(me == scene - 1)
    def _():
        after_ref[...] = jnp.zeros(after_ref.shape, after_ref.dtype)
        own_after_ref[...] = jnp.zeros(own_after_ref.shape, own_after_ref.dtype)

    line_ref[...] = jnp.zeros(line_ref.shape, jnp.float32)

    def neighbour(source, target, send, recv, step):
        return pltpu.make_async_remote_copy(
            src_ref=source, dst_ref=target, send_sem=send, recv_sem=recv,
            device_id={"scene": me + step}, device_id_type=pl.DeviceIdType.MESH,
        )

    def edge_copies(d):
        return (
            neighbour(
                up_ref.at[d], before_ref.at[d], edge_send.at[d, 0], edge_recv.at[d, 0], 1,
            ),
            neighbour(
                down_ref.at[d], after_ref.at[d], edge_send.at[d, 1], edge_recv.at[d, 1], -1,
            ),
        )

    def look_copies(big):
        return (
            neighbour(
                own_ref.at[HALO_CHUNKS + big], own_before_ref.at[big],
                look_send.at[0], look_recv.at[0], 1,
            ),
            neighbour(
                own_ref.at[big], own_after_ref.at[big],
                look_send.at[1], look_recv.at[1], -1,
            ),
        )

    def start_pair(copies):
        @pl.when(me < scene - 1)
        def _():
            copies[0].start()

        @pl.when(me > 0)
        def _():
            copies[1].start()

    def wait_pair(copies):
        @pl.when(me > 0)
        def _():
            copies[0].wait_recv()
            copies[1].wait_send()

        @pl.when(me < scene - 1)
        def _():
            copies[1].wait_recv()
            copies[0].wait_send()

    def widen(d, part):
        def body(source, carry):
            start = pl.multiple_of(source * HALF, HALF)
            for c in range(2):
                strip = recv_ref[d, part, source, c].astype(jnp.float32)
                for pair in range(wide_ref.shape[1]):
                    kept = strip[:, pair * LANES : (pair + 1) * LANES]
                    wide_ref[c, pair, pl.ds(start, HALF), : kept.shape[1]] = kept
            return carry

        lax.fori_loop(0, scene, body, 0)

    def transform(first, count):
        held = [arrived_lines(wide_ref, first + n, scene, local, low) for n in range(count)]
        mixed = dot(left_ref[...], jnp.concatenate(held, axis=1))
        tc, ts = tc_ref[...], ts_ref[...]
        segments = []
        for n in range(count):
            re, im = (mixed[k : k + SPLIT, n * LANES : (n + 1) * LANES] for k in (0, SPLIT))
            segments.append(jnp.concatenate([re * tc + im * ts, im * tc - re * ts], axis=1))
        stacked = jnp.concatenate(segments, axis=0).astype(jnp.bfloat16)
        spectra = dot(stacked, right_ref[...])
        return [spectra[n * SPLIT : (n + 1) * SPLIT] for n in range(count)]

    def turned(pair):
        parts = (pair[:, :LANES], pair[:, LANES:])
        return jnp.concatenate([pltpu.roll(part, SPLIT, 1) for part in parts], axis=1)

    def forward_rim(d):
        widen(d, 0)

        ups, downs = [], []
        for i, rim in enumerate(transform(0, SHIFT)):
            flipped = turned(rim)
            rim_ref[d, i] = rim
            downs.append(jnp.where(low, rim[:, :LANES], flipped[:, LANES:]))
            ups.append(jnp.where(low, flipped[:, :LANES], rim[:, LANES:]))
        ups = [jnp.where(fast, pltpu.roll(ups[2], LANES - HALF_LANES, 1), ups[1])] + ups[3:]
        downs = downs[:3] + [
            jnp.where(fast, downs[i], pltpu.roll(downs[i + 1], HALF_LANES, 1)) for i in (3, 5)
        ]
        for n, up in enumerate(ups):
            up_ref[d, n] = up.astype(jnp.bfloat16)
        for n, down in enumerate(downs):
            down_ref[d, n] = down.astype(jnp.bfloat16)
        start_pair(edge_copies(d))

    def forward_core(d):
        widen(d, 1)
        wait_pair(edge_copies(d))

        befores = [before_ref[d, n].astype(jnp.float32) for n in range(UPS)]
        befores = [befores[0], befores[0], pltpu.roll(befores[0], HALF_LANES, 1)] + befores[1:]
        afters = [after_ref[d, n].astype(jnp.float32) for n in range(DOWNS)]
        afters = afters[:3] + [
            part for after in afters[3:]
            for part in (after, pltpu.roll(after, LANES - HALF_LANES, 1))
        ]
        afters.append(afters[-1])
        for i, core in enumerate(transform(0, SHIFT)):
            before = jnp.concatenate([befores[i], pltpu.roll(befores[i], SPLIT, 1)], axis=1)
            after = jnp.concatenate([pltpu.roll(afters[i], SPLIT, 1), afters[i]], axis=1)
            rim, flipped = rim_ref[d, i], turned(core)
            ext_ref[i] = jnp.where(lows, before, flipped).astype(jnp.bfloat16)
            ext_ref[SHIFT + i] = jnp.where(lows, rim, core).astype(jnp.bfloat16)
            ext_ref[2 * SHIFT + i] = jnp.where(lows, core, rim).astype(jnp.bfloat16)
            ext_ref[3 * SHIFT + i] = jnp.where(lows, flipped, after).astype(jnp.bfloat16)

    def migrate(big):
        totals = [[] for _ in range(4)]
        for top in range(0, SPLIT, 8):
            rows = slice(top, top + 8)
            data = [ext_ref[4 * big + n + 1, rows] for n in range(TAPS + 3)]
            for j in range(4):
                sums = []
                for first in range(2):
                    total = weight_ref[4 * big + j, first, rows] * data[j + first]
                    for tap in range(first + 2, TAPS, 2):
                        total += weight_ref[4 * big + j, tap, rows] * data[j + tap]
                    sums.append(total.astype(jnp.float32))
                totals[j].append(sums[0] + sums[1])
        return [jnp.concatenate(total, axis=0) for total in totals]

    def focus(big):
        compressed = []
        for j, migrated in enumerate(migrate(big)):
            re, im = migrated[:, :LANES], migrated[:, LANES:]
            cos_phase, sin_phase = cos_ref[4 * big + j], sin_ref[4 * big + j]
            parts = [re * cos_phase - im * sin_phase, im * cos_phase + re * sin_phase]
            compressed.append(jnp.concatenate(parts, axis=1).astype(jnp.bfloat16))
        first = dot(jnp.concatenate(compressed, axis=0), back_right_ref[...])
        tc, ts = tc_ref[...], ts_ref[...]
        segments = []
        for j in range(4):
            rows = first[j * SPLIT : (j + 1) * SPLIT]
            re, im = rows[:, :LANES], rows[:, LANES:]
            segments.append(jnp.concatenate([re * tc - im * ts, im * tc + re * ts], axis=0))
        stacked = jnp.concatenate(segments, axis=1).astype(jnp.bfloat16)
        second = dot(back_left_ref[...], stacked).astype(jnp.bfloat16)
        return [second[:, j * LANES : (j + 1) * LANES] for j in range(4)]

    def focus_first(big, carry):
        for j, focused in enumerate(focus(big)):
            focused_ref[4 * big + j] = focused
        return carry

    def focus_last(step, carry):
        products = []
        for n in range(2):
            big = 2 * step + n
            pieces = []
            for j, focused in enumerate(focus(big)):
                leading = focused.astype(jnp.float32)
                trailing = focused_ref[4 * big + j].astype(jnp.float32)
                lr, li = leading[:SPLIT], leading[SPLIT:]
                tr, ti = trailing[:SPLIT], trailing[SPLIT:]
                product = jnp.concatenate([lr * tr + li * ti, li * tr - lr * ti], axis=1)
                pieces.append(product.astype(jnp.bfloat16))
            products.append(jnp.concatenate(pieces, axis=1))
        looked = dot(jnp.concatenate(products, axis=0), look_ref[...]).astype(jnp.bfloat16)
        for n in range(2):
            big, rows = 2 * step + n, slice(n * SPLIT, (n + 1) * SPLIT)
            own_ref[big] = looked[rows, :LANES]
            own_ref[HALO_CHUNKS + big] = looked[rows, LANES:]
            start_pair(look_copies(big))
        return carry

    send_all(1)
    arrive_all(0)
    forward_rim(0)
    arrive_all(2)
    send_all(3)
    forward_rim(1)
    arrive_all(1)
    forward_core(0)
    lax.fori_loop(0, GROUPS // 4, focus_first, 0, unroll=2)
    arrive_all(3)
    forward_core(1)
    lax.fori_loop(0, GROUPS // 8, focus_last, 0)

    def lines_of(*firsts):
        rows = []
        for chunk in (first + j for first in firsts for j in range(HALO_CHUNKS)):
            parts = [line_ref[chunk, pl.ds(p, patches, stride=2)] for p in range(4)]
            rows.append(jnp.concatenate(parts, axis=1))
        lines = jnp.concatenate(rows, axis=0).astype(jnp.bfloat16)
        results = [dot(lines, ref[...]) for ref in (azimuth_one_ref, azimuth_two_ref)]
        for n, first in enumerate(firsts):
            for j in range(HALO_CHUNKS):
                for r in range(4):
                    part = results[r // 2][(n * HALO_CHUNKS + j) * patches :][:patches]
                    part = part[:, (r % 2) * LANES : (r % 2 + 1) * LANES]
                    grid_ref[pl.ds(((first + j) * 4 + r) * patches, patches)] = part

    for j in range(CHUNKS):
        line_ref[HALO_CHUNKS + j, pl.ds(1, SPLIT)] = own_ref[j].astype(jnp.float32)
    lines_of(HALO_CHUNKS, 2 * HALO_CHUNKS)
    for k in range(2 * dates):
        sent_all(k)
    wait_pair(
        (
            neighbour(own_before_ref, own_before_ref, look_send.at[0], look_recv.at[0], 1),
            neighbour(own_after_ref, own_after_ref, look_send.at[1], look_recv.at[1], -1),
        )
    )
    for j in range(HALO_CHUNKS):
        line_ref[j, pl.ds(1, SPLIT)] = own_before_ref[j].astype(jnp.float32)
        line_ref[HALO_CHUNKS + CHUNKS + j, pl.ds(1, SPLIT)] = own_after_ref[j].astype(jnp.float32)
    lines_of(0, HALO_CHUNKS + CHUNKS)
    def filter_patches(step, carry):
        stacks = []
        for pair in range(2 * STEPS):
            one = grid_ref[pl.ds(4 * STEPS * step + 2 * pair, PATCH, stride=patches)]
            two = grid_ref[pl.ds(4 * STEPS * step + 2 * pair + 1, PATCH, stride=patches)]
            re = jnp.where(low, one, pltpu.roll(two, PATCH, 1))
            im = jnp.where(low, pltpu.roll(one, PATCH, 1), two)
            stacks.append(jnp.concatenate([re, im], axis=0).astype(jnp.bfloat16))
        spectra = dot(range_ref[...], jnp.concatenate(stacks, axis=1))
        parts, sums = [], []
        for pair in range(2 * STEPS):
            re = spectra[:PATCH, pair * LANES : (pair + 1) * LANES]
            im = spectra[PATCH:, pair * LANES : (pair + 1) * LANES]
            power = re * re + im * im + EPSILON
            magnitude = power * lax.rsqrt(power)
            rows = magnitude + pltpu.roll(magnitude, 1, 0) + pltpu.roll(magnitude, PATCH - 1, 0)
            parts.append((re, im))
            sums.append(rows.astype(jnp.bfloat16))
        boxes = dot(jnp.concatenate(sums, axis=0), smooth_ref[...])
        kept_re, kept_im = [], []
        for pair, (re, im) in enumerate(parts):
            box = boxes[pair * PATCH : (pair + 1) * PATCH]
            total = jnp.sum(box[:, LANES:], axis=0, keepdims=True)
            level = total * (1.0 / (3 * PATCH * PATCH)) + EPSILON
            gain = box[:, :LANES] * ((1.0 / 9.0) / level)
            kept_re.append((re * gain).astype(jnp.bfloat16))
            kept_im.append((im * gain).astype(jnp.bfloat16))
        kept = [
            jnp.concatenate(kept_re[2 * n : 2 * n + 2] + kept_im[2 * n : 2 * n + 2], axis=1)
            for n in range(STEPS)
        ]
        back = dot(jnp.concatenate(kept, axis=0), back_azimuth_ref[...]).astype(jnp.bfloat16)
        stacked = []
        for n in range(STEPS):
            rows = back[n * PATCH : (n + 1) * PATCH]
            stacked.append(jnp.concatenate([rows[:, :LANES], rows[:, LANES:]], axis=0))
        result = dot(back_range_ref[...], jnp.concatenate(stacked, axis=1))
        width = STEPS * LANES
        start = pl.multiple_of(step * width, width)
        out_ref[:, pl.ds(start, width)] = result.astype(jnp.bfloat16)
        return carry

    lax.fori_loop(0, patches // (4 * STEPS), filter_patches, 0, unroll=1)


def loading_kernel(*refs):
    held, out_ref, kept, load_sem = refs[:TABLES], refs[TABLES], refs[TABLES + 1 : -1], refs[-1]
    rows = held[0].shape[0] // SLABS
    slabs = [
        pltpu.make_async_copy(
            held[0].at[pl.ds(n * rows, rows)], kept[0].at[pl.ds(n * rows, rows)], load_sem.at[n]
        )
        for n in range(SLABS)
    ]
    loads = [
        pltpu.make_async_copy(held[i], kept[i], load_sem.at[SLABS - 1 + i])
        for i in range(1, TABLES)
    ]
    scene_kernel(*kept[:TABLES], out_ref, *kept[TABLES:], slabs, loads)


def table_stack(left):
    unit = 1.0 / SPLIT
    back_range = np.zeros((LANES, LANES))
    back_range[:PATCH] = back_range_table() * unit
    azimuth = patch_azimuth_table()
    return np.concatenate(
        [
            np.concatenate([left, left_table(-1.0) * unit], axis=1),
            np.concatenate([patch_range_table() * unit, back_range], axis=1),
            spectrum_side(right_table(1.0), 1) * unit,
            spectrum_side(right_table(-1.0), 0),
            look_table(),
            azimuth[:, : 2 * LANES],
            azimuth[:, 2 * LANES :],
            back_azimuth_table(),
            smooth_table(),
        ]
    )


def run_scene(raw, band, phase, left, scene, shape):
    dates, width = shape[1], shape[3]
    looks = SPLIT * SPLIT // LOOKS
    vmem = pl.BlockSpec(memory_space=pltpu.VMEM)
    plane = (GROUPS, SPLIT, LANES)
    ups, downs = (pltpu.VMEM((dates, n, SPLIT, LANES), jnp.bfloat16) for n in (UPS, DOWNS))
    looked_edge = pltpu.VMEM((HALO_CHUNKS, SPLIT, LANES), jnp.bfloat16)
    dma = pltpu.SemaphoreType.DMA
    twiddles = np.concatenate(twiddle_tables())
    tables = (raw, band, phase, bf16(table_stack(left)), jnp.asarray(twiddles))
    return pl.pallas_call(
        loading_kernel,
        in_specs=[pl.BlockSpec(memory_space=pl.ANY)] * TABLES,
        out_specs=vmem,
        out_shape=pltpu.VMEM((2 * STRIP, looks), jnp.bfloat16),
        scratch_shapes=[
            (pltpu.SMEM if table is band else pltpu.VMEM)(table.shape, table.dtype)
            for table in tables
        ]
        + [
            pltpu.VMEM((dates, 2, scene, 2, HALF, width), jnp.bfloat16),
            pltpu.VMEM(raw.shape, jnp.float32),
            pltpu.VMEM((dates, 2, scene, 2, HALF, width), jnp.bfloat16),
            pltpu.VMEM((STRIP * SPLIT // 2, LANES), jnp.float32),
            pltpu.VMEM((2, pl.cdiv(width, LANES), scene * HALF, LANES), jnp.float32),
            pltpu.VMEM((GROUPS, TAPS, SPLIT, 2 * LANES), jnp.bfloat16),
            pltpu.VMEM(plane, jnp.float32),
            pltpu.VMEM(plane, jnp.float32),
            pltpu.VMEM((GROUPS + 2 * SHIFT, SPLIT, 2 * LANES), jnp.bfloat16),
            pltpu.VMEM((dates, SHIFT, SPLIT, 2 * LANES), jnp.float32),
            ups, downs, ups, downs,
            pltpu.VMEM((GROUPS, 2 * SPLIT, LANES), jnp.bfloat16),
            pltpu.VMEM((CHUNKS, SPLIT, LANES), jnp.bfloat16),
            looked_edge,
            looked_edge,
            pltpu.VMEM((2 * CHUNKS, SPLIT + 8, LANES), jnp.float32),
            pltpu.VMEM((PATCH * SPLIT // 2, LANES), jnp.float32),
            dma((2 * dates,)), dma((2 * dates,)),
            dma((dates, 2)), dma((dates, 2)), dma((2,)), dma((2,)), dma((SLABS - 1 + TABLES,)),
        ],
        compiler_params=pltpu.CompilerParams(
            vmem_limit_bytes=VMEM_LIMIT, collective_id=0, has_side_effects=True
        ),
        name="scene",
    )(*[pltpu.with_memory_space_constraint(t, pltpu.HBM) for t in tables])


def on_device(raw_echoes, azimuth_phase, band_offset, partners):
    scene = lax.axis_size("scene")
    dates = raw_echoes.shape[2]
    local = raw_echoes.shape[0] // SPLIT
    pairs = partners.size
    assert dates == 2 and raw_echoes.shape[3] == scene * STRIP
    left = left_table(1.0).reshape(2 * SPLIT, 2, scene, local)
    left = left.transpose(0, 1, 3, 2).reshape(2 * SPLIT, 2 * SPLIT)
    lines, bins = raw_echoes.shape[0], raw_echoes.shape[3]
    raw = raw_echoes.reshape(lines, 2, dates, bins // LANES, LANES)
    raw = raw.transpose(0, 1, 3, 2, 4).reshape(-1, LANES)
    phase = azimuth_phase.T
    result = run_scene(
        raw, band_offset, phase, left, scene, (2, dates, bins, lines)
    )
    result = jnp.broadcast_to(result, (pairs,) + result.shape)
    return result.reshape(pairs, 2, STRIP, -1).transpose(0, 3, 1, 2)


def solution(mesh):
    return jax.shard_map(
        on_device,
        mesh=mesh,
        in_specs=(
            P("scene", None, "stack", None),
            P("stack", "scene"),
            P(("stack", "scene")),
            P("stack", None),
        ),
        out_specs=P("stack", None, None, "scene"),
        check_vma=False,
    )
```

```python
import math

import jax
import jax.numpy as jnp
import numpy as np
from jax import lax
from jax.experimental import pallas as pl
from jax.experimental.pallas import tpu as pltpu
from jax.sharding import PartitionSpec as P

SPLIT = 64
LOOKS = 4
PATCH = 64
SHIFT = 8
TAPS = 2 * SHIFT - 1
EPSILON = 1e-06
STRIP = 32
GROUPS = STRIP // 2
LANES = 2 * SPLIT
CHUNKS = STRIP // 4
HALO_CHUNKS = CHUNKS // 2
HALF = STRIP // 2
HALF_LANES = 32
UPS, DOWNS = SHIFT - 2, SHIFT - 3
STEPS = 8
TABLES = 5
SLABS = 4
VMEM_LIMIT = 40 * 1024 * 1024


def base_tables():
    k = np.arange(64)
    angle = 2.0 * np.pi * ((k[:, None] * k[None, :]) % 64) / 64.0
    return np.cos(angle), np.sin(angle)


def twiddle_tables():
    k = np.arange(SPLIT)
    angle = 2.0 * np.pi * ((k[:, None] * k[None, :]) % (SPLIT * SPLIT)) / (SPLIT * SPLIT)
    return (
        np.tile(np.cos(angle), (1, 2)).astype(np.float32),
        np.tile(np.sin(angle), (1, 2)).astype(np.float32),
    )


def bf16(table):
    return jnp.asarray(np.asarray(table, np.float32), jnp.bfloat16)


def left_table(direction):
    c, s = base_tables()
    return np.block([[c, direction * s], [-direction * s, c]])


def right_table(direction):
    c, s = base_tables()
    eye = np.eye(2)
    return np.block(
        [
            [np.kron(eye, c), np.kron(eye, -direction * s)],
            [np.kron(eye, direction * s), np.kron(eye, c)],
        ]
    )


def look_table():
    table = np.zeros((4, 2, 2, SPLIT, 2, 4, 2, SPLIT // LOOKS))
    for g in range(4):
        for c in range(2):
            for rb in range(2):
                for q in range(SPLIT):
                    table[g, c, rb, q, rb, g, c, q // LOOKS] = 1.0 / LOOKS
    return table.reshape(4 * 2 * 2 * SPLIT, 2 * 4 * 2 * SPLIT // LOOKS)


def patch_azimuth_table():
    c, s = base_tables()
    table = np.zeros((4, 4, 2, 16, 4, 2, 64))
    for p in range(4):
        part_c, part_s = c[16 * p : 16 * p + 16], s[16 * p : 16 * p + 16]
        for r in range(4):
            table[p, r, 0, :, r, 0] = part_c
            table[p, r, 1, :, r, 0] = part_s
            table[p, r, 0, :, r, 1] = -part_s
            table[p, r, 1, :, r, 1] = part_c
    return table.reshape(512, 512)


def patch_range_table():
    c, s = base_tables()
    return np.block([[c, s], [-s, c]])


def smooth_table():
    k = np.arange(PATCH)
    gap = (k[:, None] - k[None, :]) % PATCH
    near = ((gap <= 1) | (gap == PATCH - 1)).astype(np.float64)
    eye = np.eye(2)
    return np.concatenate([np.kron(eye, near), np.kron(eye, np.ones((PATCH, PATCH)))], axis=1)


def back_azimuth_table():
    c, s = base_tables()
    c, s = c[:, 16:48], s[:, 16:48]
    table = np.zeros((2, 4, 64, 2, 4, 32))
    for i in range(4):
        table[0, i, :, 0, i] = c
        table[1, i, :, 0, i] = -s
        table[0, i, :, 1, i] = s
        table[1, i, :, 1, i] = c
    return table.reshape(512, 256)


def back_range_table():
    c, s = base_tables()
    c, s = c[16:48], s[16:48]
    return np.block([[c, -s], [s, c]])


def dot(a, b):
    return jnp.dot(a, b, preferred_element_type=jnp.float32)


def lane_order():
    quarter = SPLIT // 4
    places = np.arange(SPLIT // 2)
    fast = places[quarter // 2 : 3 * quarter // 2]
    slow = np.concatenate([places[: quarter // 2], places[3 * quarter // 2 :]])
    return np.concatenate([2 * fast, 2 * fast + 1, 2 * slow, 2 * slow + 1])


def spectrum_side(table, axis):
    order = np.concatenate([SPLIT * half + lane_order() for half in range(4)])
    return np.take(table, order, axis=axis)


def cos_sin(angle):
    h = 0.5 * angle
    h2 = h * h
    sin_h = 1.0 / 6227020800.0
    for fact in (-39916800.0, 362880.0, -5040.0, 120.0, -6.0, 1.0):
        sin_h = sin_h * h2 + 1.0 / fact
    sin_h = sin_h * h
    cos_h = 1.0 / 479001600.0
    for fact in (-3628800.0, 40320.0, -720.0, 24.0, -2.0, 1.0):
        cos_h = cos_h * h2 + 1.0 / fact
    return 1.0 - 2.0 * sin_h * sin_h, 2.0 * sin_h * cos_h


def make_weights(g, band_ref, lines_ref, weight_ref, cos_ref, sin_ref):
    shape = (SPLIT, LANES)
    lane = lax.broadcasted_iota(jnp.int32, shape, 1)
    row = lax.broadcasted_iota(jnp.int32, shape, 0)
    quarter = SPLIT // 4
    place, odd = lane & (quarter - 1), (lane & quarter) // quarter
    slow = jnp.where(place < quarter // 2, place, place + quarter)
    place = jnp.where((lane & (2 * quarter)) != 0, slow, place + quarter // 2)
    k = row + SPLIT * (2 * place + odd)
    total = SPLIT * SPLIT
    f = jnp.where(k < total // 2, k, k - total).astype(jnp.float32)
    ratio = f * (2.0 / total)
    band = jnp.where(lane < SPLIT, band_ref[g], band_ref[g + GROUPS]).astype(jnp.float32)
    s = band * (ratio * ratio - 0.5)
    n = jnp.floor(s + 0.5)
    y = s - n
    y2 = y * y
    pi = math.pi
    poly = -(pi**11) / 39916800.0
    for power, fact in ((9, 362880.0), (7, -5040.0), (5, 120.0), (3, -6.0), (1, 1.0)):
        poly = poly * y2 + (pi**power) / fact
    odd = n.astype(jnp.int32) & 1
    lobe = jnp.where(odd == 1, 1.0, -1.0) * (y * poly) * (1.0 / pi)
    cos_s, sin_s = cos_sin(s * (pi / 4.0))
    cos_s, sin_s = 0.5 * cos_s, 0.5 * sin_s
    for tap in range(TAPS):
        m = tap + 1 - SHIFT
        x = m - s
        sign = 1.0 if m % 2 == 0 else -1.0
        safe = jnp.where(x == 0.0, 1.0, x)
        sinc = jnp.where(x == 0.0, 1.0, (sign * lobe) / safe)
        window = 0.5 + math.cos(pi * m / 4.0) * cos_s + math.sin(pi * m / 4.0) * sin_s
        weight = jnp.where(jnp.abs(x) < SHIFT / 2.0, sinc * window, 0.0)
        weight_ref[g, tap] = jnp.concatenate([weight, weight], axis=1).astype(jnp.bfloat16)
    first = lines_ref[pl.ds(g, SPLIT // 2, stride=STRIP)]
    second = lines_ref[pl.ds(g + GROUPS, SPLIT // 2, stride=STRIP)]
    cuts = (0, quarter // 2, 3 * quarter // 2, SPLIT // 2)
    pieces = []
    for even in (first, second):
        both = (even, pltpu.roll(even, SPLIT, 1))
        thirds = [[part[a:b] for a, b in zip(cuts, cuts[1:])] for part in both]
        pieces += [thirds[0][1], thirds[1][1]]
        pieces += [thirds[0][0], thirds[0][2], thirds[1][0], thirds[1][2]]
    angle = jnp.concatenate(pieces, axis=0).T[:SPLIT]
    cos_ref[g], sin_ref[g] = cos_sin(angle)


def arrived_lines(wide_ref, i, sources, local, low):
    rows = []
    for c in range(2):
        for pair in range(wide_ref.shape[1]):
            one = wide_ref[c, pair, pl.ds(i, sources, stride=HALF)]
            two = wide_ref[c, pair, pl.ds(i + SHIFT, sources, stride=HALF)]
            rows.append(jnp.where(low[:sources], one, pltpu.roll(two, SPLIT, 1)))
            if local > 1:
                rows.append(jnp.where(low[:sources], pltpu.roll(one, SPLIT, 1), two))
    return jnp.concatenate(rows, axis=0).astype(jnp.bfloat16)


def scene_kernel(
    packed_ref, band_ref, phase_ref, table_ref, twiddle_ref,
    out_ref,
    raw_ref, spread_ref, recv_ref, lines_ref, wide_ref, weight_ref, cos_ref, sin_ref, ext_ref,
    rim_ref, up_ref, down_ref, before_ref, after_ref, focused_ref,
    own_ref, own_before_ref, own_after_ref, line_ref, grid_ref,
    send_sem, recv_sem, edge_send, edge_recv, look_send, look_recv,
    slabs, loads,
):
    scene = lax.axis_size("scene")
    me = lax.axis_index("scene")
    dates = raw_ref.shape[0]
    lines_held = raw_ref.shape[5]
    local = lines_held // SPLIT
    low = lax.broadcasted_iota(jnp.int32, (SPLIT, LANES), 1) < SPLIT
    lows = jnp.concatenate([low, low], axis=1)
    fast = lax.broadcasted_iota(jnp.int32, (SPLIT, LANES), 1) % SPLIT < HALF_LANES
    patches = SPLIT // 2

    left_ref, back_left_ref, range_ref, back_range_ref = (
        table_ref.at[rows, columns] for rows, columns in (
            (pl.ds(0, LANES), pl.ds(0, LANES)), (pl.ds(0, LANES), pl.ds(LANES, LANES)),
            (pl.ds(LANES, LANES), pl.ds(0, LANES)), (pl.ds(LANES, PATCH), pl.ds(LANES, LANES)),
        )
    )
    wide = 2 * LANES
    starts = np.cumsum([wide, wide, wide, 4 * wide, 2 * wide, 2 * wide, 2 * wide]).tolist()
    (
        right_ref, back_right_ref, look_ref, azimuth_one_ref, azimuth_two_ref,
        back_azimuth_ref, smooth_ref,
    ) = (
        table_ref.at[pl.ds(start, rows)]
        for start, rows in zip(starts, (wide, wide, 4 * wide, 2 * wide, 2 * wide, 2 * wide, LANES))
    )
    tc_ref, ts_ref = twiddle_ref.at[pl.ds(0, SPLIT)], twiddle_ref.at[pl.ds(SPLIT, SPLIT)]

    barrier = pltpu.get_barrier_semaphore()

    def greet(o, carry):
        pl.semaphore_signal(
            barrier, inc=1, device_id={"scene": lax.rem(me + o, scene)},
            device_id_type=pl.DeviceIdType.MESH,
        )
        return carry

    lax.fori_loop(1, scene, greet, 0)
    for load in slabs + loads:
        load.start()
    piece = packed_ref.shape[0] // (2 * SLABS)
    for n, slab in enumerate(slabs):
        slab.wait()
        for half in range(2):
            rows = pl.ds((2 * n + half) * piece, piece)
            spread_ref[rows] = packed_ref[rows].astype(jnp.float32)
    owners = LANES // STRIP
    tiles = scene // owners
    stride = 2 * tiles * dates

    def piece_of(ref, k, owner):
        return ref.at[k // 2, k % 2, owner]

    def strip_copy(k, peer):
        return pltpu.make_async_remote_copy(
            src_ref=piece_of(raw_ref, k, peer),
            dst_ref=piece_of(recv_ref, k, me),
            send_sem=send_sem.at[k],
            recv_sem=recv_sem.at[k],
            device_id={"scene": peer},
            device_id_type=pl.DeviceIdType.MESH,
        )

    def own_copy(k):
        return pltpu.make_async_copy(
            piece_of(raw_ref, k, me), piece_of(recv_ref, k, me), recv_sem.at[k]
        )

    def turn(d, tile):
        for c in range(2):
            start = (c * tiles + tile) * dates + d
            bins = spread_ref[pl.ds(start, lines_held, stride=stride)].T
            for n in range(owners):
                own = bins[n * STRIP : (n + 1) * STRIP]
                rim = jnp.concatenate([own[:SHIFT], own[STRIP - SHIFT :]], axis=0)
                core = own[SHIFT : STRIP - SHIFT]
                raw_ref[d, 0, tile * owners + n, c] = rim.astype(jnp.bfloat16)
                raw_ref[d, 1, tile * owners + n, c] = core.astype(jnp.bfloat16)

    def turn_and_send(d):
        def body(i, carry):
            tile = lax.rem(me // owners + tiles // 2 + i, tiles)
            turn(d, tile)

            @pl.when(i == 0)
            def _():
                if d == 0:
                    pl.semaphore_wait(barrier, scene - 1)

            for n in range(owners):
                peer = tile * owners + n

                @pl.when(peer != me)
                def _():
                    strip_copy(2 * d, peer).start()

            return carry

        lax.fori_loop(0, tiles, body, 0)
        own_copy(2 * d).start()

    def far(i):
        half = (i + 1) // 2
        return scene // 2 + half * (1 - 2 * lax.rem(i, 2))

    def send_all(k):
        def send(i, carry):
            strip_copy(k, lax.rem(me + far(i), scene)).start()
            return carry

        lax.fori_loop(0, scene - 1, send, 0)
        own_copy(k).start()

    def arrive_all(k):
        held = recv_ref.at[k // 2, k % 2]
        pltpu.make_async_copy(held, held, recv_sem.at[k]).wait()

    def sent_all(k):
        held = raw_ref.at[k // 2, k % 2, pl.ds(0, scene - 1)]
        pltpu.make_async_copy(held, held, send_sem.at[k]).wait()

    for d in range(dates):
        turn_and_send(d)

    for load in loads:
        load.wait()

    for part in range(SPLIT // 2):
        lines_ref[pl.ds(part * STRIP, STRIP)] = phase_ref[:, part * LANES : (part + 1) * LANES]

    def weigh(g, carry):
        make_weights(g, band_ref, lines_ref, weight_ref, cos_ref, sin_ref)
        return carry

    lax.fori_loop(0, GROUPS, weigh, 0)

    @pl.when(me == 0)
    def _():
        before_ref[...] = jnp.zeros(before_ref.shape, before_ref.dtype)
        own_before_ref[...] = jnp.zeros(own_before_ref.shape, own_before_ref.dtype)

    @pl.when(me == scene - 1)
    def _():
        after_ref[...] = jnp.zeros(after_ref.shape, after_ref.dtype)
        own_after_ref[...] = jnp.zeros(own_after_ref.shape, own_after_ref.dtype)

    line_ref[...] = jnp.zeros(line_ref.shape, jnp.float32)

    def neighbour(source, target, send, recv, step):
        return pltpu.make_async_remote_copy(
            src_ref=source, dst_ref=target, send_sem=send, recv_sem=recv,
            device_id={"scene": me + step}, device_id_type=pl.DeviceIdType.MESH,
        )

    def edge_copies(d):
        return (
            neighbour(
                up_ref.at[d], before_ref.at[d], edge_send.at[d, 0], edge_recv.at[d, 0], 1,
            ),
            neighbour(
                down_ref.at[d], after_ref.at[d], edge_send.at[d, 1], edge_recv.at[d, 1], -1,
            ),
        )

    def look_copies(big):
        return (
            neighbour(
                own_ref.at[HALO_CHUNKS + big], own_before_ref.at[big],
                look_send.at[0], look_recv.at[0], 1,
            ),
            neighbour(
                own_ref.at[big], own_after_ref.at[big],
                look_send.at[1], look_recv.at[1], -1,
            ),
        )

    def start_pair(copies):
        @pl.when(me < scene - 1)
        def _():
            copies[0].start()

        @pl.when(me > 0)
        def _():
            copies[1].start()

    def wait_pair(copies):
        @pl.when(me > 0)
        def _():
            copies[0].wait_recv()
            copies[1].wait_send()

        @pl.when(me < scene - 1)
        def _():
            copies[1].wait_recv()
            copies[0].wait_send()

    def widen(d, part):
        def body(source, carry):
            start = pl.multiple_of(source * HALF, HALF)
            for c in range(2):
                strip = recv_ref[d, part, source, c].astype(jnp.float32)
                for pair in range(wide_ref.shape[1]):
                    kept = strip[:, pair * LANES : (pair + 1) * LANES]
                    wide_ref[c, pair, pl.ds(start, HALF), : kept.shape[1]] = kept
            return carry

        lax.fori_loop(0, scene, body, 0)

    def transform(first, count):
        held = [arrived_lines(wide_ref, first + n, scene, local, low) for n in range(count)]
        mixed = dot(left_ref[...], jnp.concatenate(held, axis=1))
        tc, ts = tc_ref[...], ts_ref[...]
        segments = []
        for n in range(count):
            re, im = (mixed[k : k + SPLIT, n * LANES : (n + 1) * LANES] for k in (0, SPLIT))
            segments.append(jnp.concatenate([re * tc + im * ts, im * tc - re * ts], axis=1))
        stacked = jnp.concatenate(segments, axis=0).astype(jnp.bfloat16)
        spectra = dot(stacked, right_ref[...])
        return [spectra[n * SPLIT : (n + 1) * SPLIT] for n in range(count)]

    def turned(pair):
        parts = (pair[:, :LANES], pair[:, LANES:])
        return jnp.concatenate([pltpu.roll(part, SPLIT, 1) for part in parts], axis=1)

    def forward_rim(d):
        widen(d, 0)

        ups, downs = [], []
        for i, rim in enumerate(transform(0, SHIFT)):
            flipped = turned(rim)
            rim_ref[d, i] = rim
            downs.append(jnp.where(low, rim[:, :LANES], flipped[:, LANES:]))
            ups.append(jnp.where(low, flipped[:, :LANES], rim[:, LANES:]))
        ups = [jnp.where(fast, pltpu.roll(ups[2], LANES - HALF_LANES, 1), ups[1])] + ups[3:]
        downs = downs[:3] + [
            jnp.where(fast, downs[i], pltpu.roll(downs[i + 1], HALF_LANES, 1)) for i in (3, 5)
        ]
        for n, up in enumerate(ups):
            up_ref[d, n] = up.astype(jnp.bfloat16)
        for n, down in enumerate(downs):
            down_ref[d, n] = down.astype(jnp.bfloat16)
        start_pair(edge_copies(d))

    def forward_core(d):
        widen(d, 1)
        wait_pair(edge_copies(d))

        befores = [before_ref[d, n].astype(jnp.float32) for n in range(UPS)]
        befores = [befores[0], befores[0], pltpu.roll(befores[0], HALF_LANES, 1)] + befores[1:]
        afters = [after_ref[d, n].astype(jnp.float32) for n in range(DOWNS)]
        afters = afters[:3] + [
            part for after in afters[3:]
            for part in (after, pltpu.roll(after, LANES - HALF_LANES, 1))
        ]
        afters.append(afters[-1])
        for i, core in enumerate(transform(0, SHIFT)):
            before = jnp.concatenate([befores[i], pltpu.roll(befores[i], SPLIT, 1)], axis=1)
            after = jnp.concatenate([pltpu.roll(afters[i], SPLIT, 1), afters[i]], axis=1)
            rim, flipped = rim_ref[d, i], turned(core)
            ext_ref[i] = jnp.where(lows, before, flipped).astype(jnp.bfloat16)
            ext_ref[SHIFT + i] = jnp.where(lows, rim, core).astype(jnp.bfloat16)
            ext_ref[2 * SHIFT + i] = jnp.where(lows, core, rim).astype(jnp.bfloat16)
            ext_ref[3 * SHIFT + i] = jnp.where(lows, flipped, after).astype(jnp.bfloat16)

    def migrate(big):
        totals = [[] for _ in range(4)]
        for top in range(0, SPLIT, 8):
            rows = slice(top, top + 8)
            data = [ext_ref[4 * big + n + 1, rows] for n in range(TAPS + 3)]
            for j in range(4):
                sums = []
                for first in range(2):
                    total = weight_ref[4 * big + j, first, rows] * data[j + first]
                    for tap in range(first + 2, TAPS, 2):
                        total += weight_ref[4 * big + j, tap, rows] * data[j + tap]
                    sums.append(total.astype(jnp.float32))
                totals[j].append(sums[0] + sums[1])
        return [jnp.concatenate(total, axis=0) for total in totals]

    def focus(step):
        compressed = []
        for big in range(2):
            for j, migrated in enumerate(migrate(2 * step + big)):
                g = 8 * step + 4 * big + j
                re, im = migrated[:, :LANES], migrated[:, LANES:]
                cos_phase, sin_phase = cos_ref[g], sin_ref[g]
                parts = [re * cos_phase - im * sin_phase, im * cos_phase + re * sin_phase]
                compressed.append(jnp.concatenate(parts, axis=1).astype(jnp.bfloat16))
        first = dot(jnp.concatenate(compressed, axis=0), back_right_ref[...])
        tc, ts = tc_ref[...], ts_ref[...]
        segments = []
        for j in range(8):
            rows = first[j * SPLIT : (j + 1) * SPLIT]
            re, im = rows[:, :LANES], rows[:, LANES:]
            segments.append(jnp.concatenate([re * tc - im * ts, im * tc + re * ts], axis=0))
        stacked = jnp.concatenate(segments, axis=1).astype(jnp.bfloat16)
        second = dot(back_left_ref[...], stacked).astype(jnp.bfloat16)
        return [second[:, j * LANES : (j + 1) * LANES] for j in range(8)]

    def focus_first(step, carry):
        for j, focused in enumerate(focus(step)):
            focused_ref[8 * step + j] = focused
        return carry

    def focus_last(step, carry):
        pieces = []
        for j, focused in enumerate(focus(step)):
            leading = focused.astype(jnp.float32)
            trailing = focused_ref[8 * step + j].astype(jnp.float32)
            lr, li = leading[:SPLIT], leading[SPLIT:]
            tr, ti = trailing[:SPLIT], trailing[SPLIT:]
            product = jnp.concatenate([lr * tr + li * ti, li * tr - lr * ti], axis=1)
            pieces.append(product.astype(jnp.bfloat16))
        products = [jnp.concatenate(pieces[4 * n : 4 * n + 4], axis=1) for n in range(2)]
        looked = dot(jnp.concatenate(products, axis=0), look_ref[...]).astype(jnp.bfloat16)
        for n in range(2):
            big, rows = 2 * step + n, slice(n * SPLIT, (n + 1) * SPLIT)
            own_ref[big] = looked[rows, :LANES]
            own_ref[HALO_CHUNKS + big] = looked[rows, LANES:]
            start_pair(look_copies(big))
        return carry

    send_all(1)
    arrive_all(0)
    forward_rim(0)
    arrive_all(2)
    send_all(3)
    forward_rim(1)
    arrive_all(1)
    forward_core(0)
    lax.fori_loop(0, GROUPS // 8, focus_first, 0)
    arrive_all(3)
    forward_core(1)
    lax.fori_loop(0, GROUPS // 8, focus_last, 0)

    def lines_of(*firsts):
        rows = []
        for chunk in (first + j for first in firsts for j in range(HALO_CHUNKS)):
            parts = [line_ref[chunk, pl.ds(p, patches, stride=2)] for p in range(4)]
            rows.append(jnp.concatenate(parts, axis=1))
        lines = jnp.concatenate(rows, axis=0).astype(jnp.bfloat16)
        results = [dot(lines, ref[...]) for ref in (azimuth_one_ref, azimuth_two_ref)]
        for n, first in enumerate(firsts):
            for j in range(HALO_CHUNKS):
                for r in range(4):
                    part = results[r // 2][(n * HALO_CHUNKS + j) * patches :][:patches]
                    part = part[:, (r % 2) * LANES : (r % 2 + 1) * LANES]
                    grid_ref[pl.ds(((first + j) * 4 + r) * patches, patches)] = part

    for j in range(CHUNKS):
        line_ref[HALO_CHUNKS + j, pl.ds(1, SPLIT)] = own_ref[j].astype(jnp.float32)
    lines_of(HALO_CHUNKS, 2 * HALO_CHUNKS)
    for k in range(2 * dates):
        sent_all(k)
    wait_pair(
        (
            neighbour(own_before_ref, own_before_ref, look_send.at[0], look_recv.at[0], 1),
            neighbour(own_after_ref, own_after_ref, look_send.at[1], look_recv.at[1], -1),
        )
    )
    for j in range(HALO_CHUNKS):
        line_ref[j, pl.ds(1, SPLIT)] = own_before_ref[j].astype(jnp.float32)
        line_ref[HALO_CHUNKS + CHUNKS + j, pl.ds(1, SPLIT)] = own_after_ref[j].astype(jnp.float32)
    lines_of(0, HALO_CHUNKS + CHUNKS)
    def filter_patches(step, carry):
        stacks = []
        for pair in range(2 * STEPS):
            one = grid_ref[pl.ds(4 * STEPS * step + 2 * pair, PATCH, stride=patches)]
            two = grid_ref[pl.ds(4 * STEPS * step + 2 * pair + 1, PATCH, stride=patches)]
            re = jnp.where(low, one, pltpu.roll(two, PATCH, 1))
            im = jnp.where(low, pltpu.roll(one, PATCH, 1), two)
            stacks.append(jnp.concatenate([re, im], axis=0).astype(jnp.bfloat16))
        spectra = dot(range_ref[...], jnp.concatenate(stacks, axis=1))
        parts, sums = [], []
        for pair in range(2 * STEPS):
            re = spectra[:PATCH, pair * LANES : (pair + 1) * LANES]
            im = spectra[PATCH:, pair * LANES : (pair + 1) * LANES]
            power = re * re + im * im + EPSILON
            magnitude = power * lax.rsqrt(power)
            rows = magnitude + pltpu.roll(magnitude, 1, 0) + pltpu.roll(magnitude, PATCH - 1, 0)
            parts.append((re, im))
            sums.append(rows.astype(jnp.bfloat16))
        boxes = dot(jnp.concatenate(sums, axis=0), smooth_ref[...])
        kept_re, kept_im = [], []
        for pair, (re, im) in enumerate(parts):
            box = boxes[pair * PATCH : (pair + 1) * PATCH]
            total = jnp.sum(box[:, LANES:], axis=0, keepdims=True)
            level = total * (1.0 / (3 * PATCH * PATCH)) + EPSILON
            gain = box[:, :LANES] * ((1.0 / 9.0) / level)
            kept_re.append((re * gain).astype(jnp.bfloat16))
            kept_im.append((im * gain).astype(jnp.bfloat16))
        kept = [
            jnp.concatenate(kept_re[2 * n : 2 * n + 2] + kept_im[2 * n : 2 * n + 2], axis=1)
            for n in range(STEPS)
        ]
        back = dot(jnp.concatenate(kept, axis=0), back_azimuth_ref[...]).astype(jnp.bfloat16)
        stacked = []
        for n in range(STEPS):
            rows = back[n * PATCH : (n + 1) * PATCH]
            stacked.append(jnp.concatenate([rows[:, :LANES], rows[:, LANES:]], axis=0))
        result = dot(back_range_ref[...], jnp.concatenate(stacked, axis=1))
        width = STEPS * LANES
        start = pl.multiple_of(step * width, width)
        out_ref[:, pl.ds(start, width)] = result.astype(jnp.bfloat16)
        return carry

    lax.fori_loop(0, patches // (4 * STEPS), filter_patches, 0, unroll=1)


def loading_kernel(*refs):
    held, out_ref, kept, load_sem = refs[:TABLES], refs[TABLES], refs[TABLES + 1 : -1], refs[-1]
    rows = held[0].shape[0] // SLABS
    slabs = [
        pltpu.make_async_copy(
            held[0].at[pl.ds(n * rows, rows)], kept[0].at[pl.ds(n * rows, rows)], load_sem.at[n]
        )
        for n in range(SLABS)
    ]
    loads = [
        pltpu.make_async_copy(held[i], kept[i], load_sem.at[SLABS - 1 + i])
        for i in range(1, TABLES)
    ]
    scene_kernel(*kept[:TABLES], out_ref, *kept[TABLES:], slabs, loads)


def table_stack(left):
    unit = 1.0 / SPLIT
    back_range = np.zeros((LANES, LANES))
    back_range[:PATCH] = back_range_table() * unit
    azimuth = patch_azimuth_table()
    return np.concatenate(
        [
            np.concatenate([left, left_table(-1.0) * unit], axis=1),
            np.concatenate([patch_range_table() * unit, back_range], axis=1),
            spectrum_side(right_table(1.0), 1) * unit,
            spectrum_side(right_table(-1.0), 0),
            look_table(),
            azimuth[:, : 2 * LANES],
            azimuth[:, 2 * LANES :],
            back_azimuth_table(),
            smooth_table(),
        ]
    )


def run_scene(raw, band, phase, left, scene, shape):
    dates, width = shape[1], shape[3]
    looks = SPLIT * SPLIT // LOOKS
    vmem = pl.BlockSpec(memory_space=pltpu.VMEM)
    plane = (GROUPS, SPLIT, LANES)
    ups, downs = (pltpu.VMEM((dates, n, SPLIT, LANES), jnp.bfloat16) for n in (UPS, DOWNS))
    looked_edge = pltpu.VMEM((HALO_CHUNKS, SPLIT, LANES), jnp.bfloat16)
    dma = pltpu.SemaphoreType.DMA
    twiddles = np.concatenate(twiddle_tables())
    tables = (raw, band, phase, bf16(table_stack(left)), jnp.asarray(twiddles))
    return pl.pallas_call(
        loading_kernel,
        in_specs=[pl.BlockSpec(memory_space=pl.ANY)] * TABLES,
        out_specs=vmem,
        out_shape=pltpu.VMEM((2 * STRIP, looks), jnp.bfloat16),
        scratch_shapes=[
            (pltpu.SMEM if table is band else pltpu.VMEM)(table.shape, table.dtype)
            for table in tables
        ]
        + [
            pltpu.VMEM((dates, 2, scene, 2, HALF, width), jnp.bfloat16),
            pltpu.VMEM(raw.shape, jnp.float32),
            pltpu.VMEM((dates, 2, scene, 2, HALF, width), jnp.bfloat16),
            pltpu.VMEM((STRIP * SPLIT // 2, LANES), jnp.float32),
            pltpu.VMEM((2, pl.cdiv(width, LANES), scene * HALF, LANES), jnp.float32),
            pltpu.VMEM((GROUPS, TAPS, SPLIT, 2 * LANES), jnp.bfloat16),
            pltpu.VMEM(plane, jnp.float32),
            pltpu.VMEM(plane, jnp.float32),
            pltpu.VMEM((GROUPS + 2 * SHIFT, SPLIT, 2 * LANES), jnp.bfloat16),
            pltpu.VMEM((dates, SHIFT, SPLIT, 2 * LANES), jnp.float32),
            ups, downs, ups, downs,
            pltpu.VMEM((GROUPS, 2 * SPLIT, LANES), jnp.bfloat16),
            pltpu.VMEM((CHUNKS, SPLIT, LANES), jnp.bfloat16),
            looked_edge,
            looked_edge,
            pltpu.VMEM((2 * CHUNKS, SPLIT + 8, LANES), jnp.float32),
            pltpu.VMEM((PATCH * SPLIT // 2, LANES), jnp.float32),
            dma((2 * dates,)), dma((2 * dates,)),
            dma((dates, 2)), dma((dates, 2)), dma((2,)), dma((2,)), dma((SLABS - 1 + TABLES,)),
        ],
        compiler_params=pltpu.CompilerParams(
            vmem_limit_bytes=VMEM_LIMIT, collective_id=0, has_side_effects=True
        ),
        name="scene",
    )(*[pltpu.with_memory_space_constraint(t, pltpu.HBM) for t in tables])


def on_device(raw_echoes, azimuth_phase, band_offset, partners):
    scene = lax.axis_size("scene")
    dates = raw_echoes.shape[2]
    local = raw_echoes.shape[0] // SPLIT
    pairs = partners.size
    assert dates == 2 and raw_echoes.shape[3] == scene * STRIP
    left = left_table(1.0).reshape(2 * SPLIT, 2, scene, local)
    left = left.transpose(0, 1, 3, 2).reshape(2 * SPLIT, 2 * SPLIT)
    lines, bins = raw_echoes.shape[0], raw_echoes.shape[3]
    raw = raw_echoes.reshape(lines, 2, dates, bins // LANES, LANES)
    raw = raw.transpose(0, 1, 3, 2, 4).reshape(-1, LANES)
    phase = azimuth_phase.T
    result = run_scene(
        raw, band_offset, phase, left, scene, (2, dates, bins, lines)
    )
    result = jnp.broadcast_to(result, (pairs,) + result.shape)
    return result.reshape(pairs, 2, STRIP, -1).transpose(0, 3, 1, 2)


def solution(mesh):
    return jax.shard_map(
        on_device,
        mesh=mesh,
        in_specs=(
            P("scene", None, "stack", None),
            P("stack", "scene"),
            P(("stack", "scene")),
            P("stack", None),
        ),
        out_specs=P("stack", None, None, "scene"),
        check_vma=False,
    )
```

```python
import math

import jax
import jax.numpy as jnp
import numpy as np
from jax import lax
from jax.experimental import pallas as pl
from jax.experimental.pallas import tpu as pltpu
from jax.sharding import PartitionSpec as P

SPLIT = 64
LOOKS = 4
PATCH = 64
SHIFT = 8
TAPS = 2 * SHIFT - 1
EPSILON = 1e-06
STRIP = 32
GROUPS = STRIP // 2
LANES = 2 * SPLIT
CHUNKS = STRIP // 4
HALO_CHUNKS = CHUNKS // 2
HALF = STRIP // 2
HALF_LANES = 32
UPS, DOWNS = SHIFT - 2, SHIFT - 3
STEPS = 8
TABLES = 5
SLABS = 4
VMEM_LIMIT = 40 * 1024 * 1024


def base_tables():
    k = np.arange(64)
    angle = 2.0 * np.pi * ((k[:, None] * k[None, :]) % 64) / 64.0
    return np.cos(angle), np.sin(angle)


def twiddle_tables():
    k = np.arange(SPLIT)
    angle = 2.0 * np.pi * ((k[:, None] * k[None, :]) % (SPLIT * SPLIT)) / (SPLIT * SPLIT)
    return (
        np.tile(np.cos(angle), (1, 2)).astype(np.float32),
        np.tile(np.sin(angle), (1, 2)).astype(np.float32),
    )


def bf16(table):
    return jnp.asarray(np.asarray(table, np.float32), jnp.bfloat16)


def left_table(direction):
    c, s = base_tables()
    return np.block([[c, direction * s], [-direction * s, c]])


def right_table(direction):
    c, s = base_tables()
    eye = np.eye(2)
    return np.block(
        [
            [np.kron(eye, c), np.kron(eye, -direction * s)],
            [np.kron(eye, direction * s), np.kron(eye, c)],
        ]
    )


def look_table():
    table = np.zeros((4, 2, 2, SPLIT, 2, 4, 2, SPLIT // LOOKS))
    for g in range(4):
        for c in range(2):
            for rb in range(2):
                for q in range(SPLIT):
                    table[g, c, rb, q, rb, g, c, q // LOOKS] = 1.0 / LOOKS
    return table.reshape(4 * 2 * 2 * SPLIT, 2 * 4 * 2 * SPLIT // LOOKS)


def patch_azimuth_table():
    c, s = base_tables()
    table = np.zeros((4, 4, 2, 16, 4, 2, 64))
    for p in range(4):
        part_c, part_s = c[16 * p : 16 * p + 16], s[16 * p : 16 * p + 16]
        for r in range(4):
            table[p, r, 0, :, r, 0] = part_c
            table[p, r, 1, :, r, 0] = part_s
            table[p, r, 0, :, r, 1] = -part_s
            table[p, r, 1, :, r, 1] = part_c
    return table.reshape(512, 512)


def patch_range_table():
    c, s = base_tables()
    return np.block([[c, s], [-s, c]])


def smooth_table():
    k = np.arange(PATCH)
    gap = (k[:, None] - k[None, :]) % PATCH
    near = ((gap <= 1) | (gap == PATCH - 1)).astype(np.float64)
    eye = np.eye(2)
    return np.concatenate([np.kron(eye, near), np.kron(eye, np.ones((PATCH, PATCH)))], axis=1)


def back_azimuth_table():
    c, s = base_tables()
    c, s = c[:, 16:48], s[:, 16:48]
    table = np.zeros((2, 4, 64, 2, 4, 32))
    for i in range(4):
        table[0, i, :, 0, i] = c
        table[1, i, :, 0, i] = -s
        table[0, i, :, 1, i] = s
        table[1, i, :, 1, i] = c
    return table.reshape(512, 256)


def back_range_table():
    c, s = base_tables()
    c, s = c[16:48], s[16:48]
    return np.block([[c, -s], [s, c]])


def dot(a, b):
    return jnp.dot(a, b, preferred_element_type=jnp.float32)


def lane_order():
    quarter = SPLIT // 4
    places = np.arange(SPLIT // 2)
    fast = places[quarter // 2 : 3 * quarter // 2]
    slow = np.concatenate([places[: quarter // 2], places[3 * quarter // 2 :]])
    return np.concatenate([2 * fast, 2 * fast + 1, 2 * slow, 2 * slow + 1])


def spectrum_side(table, axis):
    order = np.concatenate([SPLIT * half + lane_order() for half in range(4)])
    return np.take(table, order, axis=axis)


def cos_sin(angle):
    h = 0.5 * angle
    h2 = h * h
    sin_h = 1.0 / 6227020800.0
    for fact in (-39916800.0, 362880.0, -5040.0, 120.0, -6.0, 1.0):
        sin_h = sin_h * h2 + 1.0 / fact
    sin_h = sin_h * h
    cos_h = 1.0 / 479001600.0
    for fact in (-3628800.0, 40320.0, -720.0, 24.0, -2.0, 1.0):
        cos_h = cos_h * h2 + 1.0 / fact
    return 1.0 - 2.0 * sin_h * sin_h, 2.0 * sin_h * cos_h


def make_weights(g, band_ref, lines_ref, weight_ref, cos_ref, sin_ref):
    shape = (SPLIT, LANES)
    lane = lax.broadcasted_iota(jnp.int32, shape, 1)
    row = lax.broadcasted_iota(jnp.int32, shape, 0)
    quarter = SPLIT // 4
    place, odd = lane & (quarter - 1), (lane & quarter) // quarter
    slow = jnp.where(place < quarter // 2, place, place + quarter)
    place = jnp.where((lane & (2 * quarter)) != 0, slow, place + quarter // 2)
    k = row + SPLIT * (2 * place + odd)
    total = SPLIT * SPLIT
    f = jnp.where(k < total // 2, k, k - total).astype(jnp.float32)
    ratio = f * (2.0 / total)
    band = jnp.where(lane < SPLIT, band_ref[g], band_ref[g + GROUPS]).astype(jnp.float32)
    s = band * (ratio * ratio - 0.5)
    n = jnp.floor(s + 0.5)
    y = s - n
    y2 = y * y
    pi = math.pi
    poly = -(pi**11) / 39916800.0
    for power, fact in ((9, 362880.0), (7, -5040.0), (5, 120.0), (3, -6.0), (1, 1.0)):
        poly = poly * y2 + (pi**power) / fact
    odd = n.astype(jnp.int32) & 1
    lobe = jnp.where(odd == 1, 1.0, -1.0) * (y * poly) * (1.0 / pi)
    cos_s, sin_s = cos_sin(s * (pi / 4.0))
    cos_s, sin_s = 0.5 * cos_s, 0.5 * sin_s
    for tap in range(TAPS):
        m = tap + 1 - SHIFT
        x = m - s
        sign = 1.0 if m % 2 == 0 else -1.0
        safe = jnp.where(x == 0.0, 1.0, x)
        sinc = jnp.where(x == 0.0, 1.0, (sign * lobe) / safe)
        window = 0.5 + math.cos(pi * m / 4.0) * cos_s + math.sin(pi * m / 4.0) * sin_s
        weight = jnp.where(jnp.abs(x) < SHIFT / 2.0, sinc * window, 0.0)
        weight_ref[g, tap] = jnp.concatenate([weight, weight], axis=1).astype(jnp.bfloat16)
    first = lines_ref[pl.ds(g, SPLIT // 2, stride=STRIP)]
    second = lines_ref[pl.ds(g + GROUPS, SPLIT // 2, stride=STRIP)]
    cuts = (0, quarter // 2, 3 * quarter // 2, SPLIT // 2)
    pieces = []
    for even in (first, second):
        both = (even, pltpu.roll(even, SPLIT, 1))
        thirds = [[part[a:b] for a, b in zip(cuts, cuts[1:])] for part in both]
        pieces += [thirds[0][1], thirds[1][1]]
        pieces += [thirds[0][0], thirds[0][2], thirds[1][0], thirds[1][2]]
    angle = jnp.concatenate(pieces, axis=0).T[:SPLIT]
    cos_ref[g], sin_ref[g] = cos_sin(angle)


def arrived_lines(wide_ref, i, sources, local, low):
    rows = []
    for c in range(2):
        for pair in range(wide_ref.shape[1]):
            one = wide_ref[c, pair, pl.ds(i, sources, stride=HALF)]
            two = wide_ref[c, pair, pl.ds(i + SHIFT, sources, stride=HALF)]
            rows.append(jnp.where(low[:sources], one, pltpu.roll(two, SPLIT, 1)))
            if local > 1:
                rows.append(jnp.where(low[:sources], pltpu.roll(one, SPLIT, 1), two))
    return jnp.concatenate(rows, axis=0).astype(jnp.bfloat16)


def scene_kernel(
    packed_ref, band_ref, phase_ref, table_ref, twiddle_ref,
    out_ref,
    raw_ref, spread_ref, recv_ref, lines_ref, wide_ref, weight_ref, cos_ref, sin_ref, ext_ref,
    rim_ref, up_ref, down_ref, before_ref, after_ref, focused_ref,
    own_ref, own_before_ref, own_after_ref, line_ref, grid_ref,
    send_sem, recv_sem, edge_send, edge_recv, look_send, look_recv,
    slabs, loads,
):
    scene = lax.axis_size("scene")
    me = lax.axis_index("scene")
    dates = raw_ref.shape[0]
    lines_held = raw_ref.shape[5]
    local = lines_held // SPLIT
    low = lax.broadcasted_iota(jnp.int32, (SPLIT, LANES), 1) < SPLIT
    lows = jnp.concatenate([low, low], axis=1)
    fast = lax.broadcasted_iota(jnp.int32, (SPLIT, LANES), 1) % SPLIT < HALF_LANES
    patches = SPLIT // 2

    left_ref, back_left_ref, range_ref, back_range_ref = (
        table_ref.at[rows, columns] for rows, columns in (
            (pl.ds(0, LANES), pl.ds(0, LANES)), (pl.ds(0, LANES), pl.ds(LANES, LANES)),
            (pl.ds(LANES, LANES), pl.ds(0, LANES)), (pl.ds(LANES, PATCH), pl.ds(LANES, LANES)),
        )
    )
    wide = 2 * LANES
    starts = np.cumsum([wide, wide, wide, 4 * wide, 2 * wide, 2 * wide, 2 * wide]).tolist()
    (
        right_ref, back_right_ref, look_ref, azimuth_one_ref, azimuth_two_ref,
        back_azimuth_ref, smooth_ref,
    ) = (
        table_ref.at[pl.ds(start, rows)]
        for start, rows in zip(starts, (wide, wide, 4 * wide, 2 * wide, 2 * wide, 2 * wide, LANES))
    )
    tc_ref, ts_ref = twiddle_ref.at[pl.ds(0, SPLIT)], twiddle_ref.at[pl.ds(SPLIT, SPLIT)]

    for slab in slabs:
        slab.start()
    barrier = pltpu.get_barrier_semaphore()

    def greet(o, carry):
        pl.semaphore_signal(
            barrier, inc=1, device_id={"scene": lax.rem(me + o, scene)},
            device_id_type=pl.DeviceIdType.MESH,
        )
        return carry

    lax.fori_loop(1, scene, greet, 0, unroll=True)
    piece = packed_ref.shape[0] // (2 * SLABS)
    for n, slab in enumerate(slabs):
        slab.wait()
        for half in range(2):
            rows = pl.ds((2 * n + half) * piece, piece)
            spread_ref[rows] = packed_ref[rows].astype(jnp.float32)
    for load in loads:
        load.start()
    owners = LANES // STRIP
    tiles = scene // owners
    stride = 2 * tiles * dates

    def piece_of(ref, k, owner):
        return ref.at[k // 2, k % 2, owner]

    def strip_copy(k, peer):
        return pltpu.make_async_remote_copy(
            src_ref=piece_of(raw_ref, k, peer),
            dst_ref=piece_of(recv_ref, k, me),
            send_sem=send_sem.at[k],
            recv_sem=recv_sem.at[k],
            device_id={"scene": peer},
            device_id_type=pl.DeviceIdType.MESH,
        )

    def own_copy(k):
        return pltpu.make_async_copy(
            piece_of(raw_ref, k, me), piece_of(recv_ref, k, me), recv_sem.at[k]
        )

    def turn(d, tile):
        for c in range(2):
            start = (c * tiles + tile) * dates + d
            bins = spread_ref[pl.ds(start, lines_held, stride=stride)].T
            for n in range(owners):
                own = bins[n * STRIP : (n + 1) * STRIP]
                rim = jnp.concatenate([own[:SHIFT], own[STRIP - SHIFT :]], axis=0)
                core = own[SHIFT : STRIP - SHIFT]
                raw_ref[d, 0, tile * owners + n, c] = rim.astype(jnp.bfloat16)
                raw_ref[d, 1, tile * owners + n, c] = core.astype(jnp.bfloat16)

    def turn_and_send(d):
        def body(i, carry):
            tile = lax.rem(me // owners + tiles // 2 + i, tiles)
            turn(d, tile)

            @pl.when(i == 0)
            def _():
                if d == 0:
                    pl.semaphore_wait(barrier, scene - 1)

            for n in range(owners):
                peer = tile * owners + n

                @pl.when(peer != me)
                def _():
                    strip_copy(2 * d, peer).start()

            return carry

        lax.fori_loop(0, tiles, body, 0)
        own_copy(2 * d).start()

    def far(i):
        half = (i + 1) // 2
        return scene // 2 + half * (1 - 2 * lax.rem(i, 2))

    def send_all(k):
        def send(i, carry):
            strip_copy(k, lax.rem(me + far(i), scene)).start()
            return carry

        lax.fori_loop(0, scene - 1, send, 0)
        own_copy(k).start()

    def arrive_all(k):
        held = recv_ref.at[k // 2, k % 2]
        pltpu.make_async_copy(held, held, recv_sem.at[k]).wait()

    def sent_all(k):
        held = raw_ref.at[k // 2, k % 2, pl.ds(0, scene - 1)]
        pltpu.make_async_copy(held, held, send_sem.at[k]).wait()

    for d in range(dates):
        turn_and_send(d)

    for load in loads:
        load.wait()

    for part in range(SPLIT // 2):
        lines_ref[pl.ds(part * STRIP, STRIP)] = phase_ref[:, part * LANES : (part + 1) * LANES]

    def weigh(g, carry):
        make_weights(g, band_ref, lines_ref, weight_ref, cos_ref, sin_ref)
        return carry

    lax.fori_loop(0, GROUPS, weigh, 0)

    @pl.when(me == 0)
    def _():
        before_ref[...] = jnp.zeros(before_ref.shape, before_ref.dtype)
        own_before_ref[...] = jnp.zeros(own_before_ref.shape, own_before_ref.dtype)

    @pl.when(me == scene - 1)
    def _():
        after_ref[...] = jnp.zeros(after_ref.shape, after_ref.dtype)
        own_after_ref[...] = jnp.zeros(own_after_ref.shape, own_after_ref.dtype)

    line_ref[...] = jnp.zeros(line_ref.shape, jnp.float32)

    def neighbour(source, target, send, recv, step):
        return pltpu.make_async_remote_copy(
            src_ref=source, dst_ref=target, send_sem=send, recv_sem=recv,
            device_id={"scene": me + step}, device_id_type=pl.DeviceIdType.MESH,
        )

    def edge_copies(d):
        return (
            neighbour(
                up_ref.at[d], before_ref.at[d], edge_send.at[d, 0], edge_recv.at[d, 0], 1,
            ),
            neighbour(
                down_ref.at[d], after_ref.at[d], edge_send.at[d, 1], edge_recv.at[d, 1], -1,
            ),
        )

    def look_copies(big):
        return (
            neighbour(
                own_ref.at[HALO_CHUNKS + big], own_before_ref.at[big],
                look_send.at[0], look_recv.at[0], 1,
            ),
            neighbour(
                own_ref.at[big], own_after_ref.at[big],
                look_send.at[1], look_recv.at[1], -1,
            ),
        )

    def start_pair(copies):
        @pl.when(me < scene - 1)
        def _():
            copies[0].start()

        @pl.when(me > 0)
        def _():
            copies[1].start()

    def wait_pair(copies):
        @pl.when(me > 0)
        def _():
            copies[0].wait_recv()
            copies[1].wait_send()

        @pl.when(me < scene - 1)
        def _():
            copies[1].wait_recv()
            copies[0].wait_send()

    def widen(d, part):
        def body(source, carry):
            start = pl.multiple_of(source * HALF, HALF)
            for c in range(2):
                strip = recv_ref[d, part, source, c].astype(jnp.float32)
                for pair in range(wide_ref.shape[1]):
                    kept = strip[:, pair * LANES : (pair + 1) * LANES]
                    wide_ref[c, pair, pl.ds(start, HALF), : kept.shape[1]] = kept
            return carry

        lax.fori_loop(0, scene, body, 0)

    def transform(first, count):
        held = [arrived_lines(wide_ref, first + n, scene, local, low) for n in range(count)]
        mixed = dot(left_ref[...], jnp.concatenate(held, axis=1))
        tc, ts = tc_ref[...], ts_ref[...]
        segments = []
        for n in range(count):
            re, im = (mixed[k : k + SPLIT, n * LANES : (n + 1) * LANES] for k in (0, SPLIT))
            segments.append(jnp.concatenate([re * tc + im * ts, im * tc - re * ts], axis=1))
        stacked = jnp.concatenate(segments, axis=0).astype(jnp.bfloat16)
        spectra = dot(stacked, right_ref[...])
        return [spectra[n * SPLIT : (n + 1) * SPLIT] for n in range(count)]

    def turned(pair):
        parts = (pair[:, :LANES], pair[:, LANES:])
        return jnp.concatenate([pltpu.roll(part, SPLIT, 1) for part in parts], axis=1)

    def forward_rim(d):
        widen(d, 0)

        ups, downs = [], []
        for i, rim in enumerate(transform(0, SHIFT)):
            flipped = turned(rim)
            rim_ref[d, i] = rim
            downs.append(jnp.where(low, rim[:, :LANES], flipped[:, LANES:]))
            ups.append(jnp.where(low, flipped[:, :LANES], rim[:, LANES:]))
        ups = [jnp.where(fast, pltpu.roll(ups[2], LANES - HALF_LANES, 1), ups[1])] + ups[3:]
        downs = downs[:3] + [
            jnp.where(fast, downs[i], pltpu.roll(downs[i + 1], HALF_LANES, 1)) for i in (3, 5)
        ]
        for n, up in enumerate(ups):
            up_ref[d, n] = up.astype(jnp.bfloat16)
        for n, down in enumerate(downs):
            down_ref[d, n] = down.astype(jnp.bfloat16)
        start_pair(edge_copies(d))

    def forward_core(d):
        widen(d, 1)
        wait_pair(edge_copies(d))

        befores = [before_ref[d, n].astype(jnp.float32) for n in range(UPS)]
        befores = [befores[0], befores[0], pltpu.roll(befores[0], HALF_LANES, 1)] + befores[1:]
        afters = [after_ref[d, n].astype(jnp.float32) for n in range(DOWNS)]
        afters = afters[:3] + [
            part for after in afters[3:]
            for part in (after, pltpu.roll(after, LANES - HALF_LANES, 1))
        ]
        afters.append(afters[-1])
        for i, core in enumerate(transform(0, SHIFT)):
            before = jnp.concatenate([befores[i], pltpu.roll(befores[i], SPLIT, 1)], axis=1)
            after = jnp.concatenate([pltpu.roll(afters[i], SPLIT, 1), afters[i]], axis=1)
            rim, flipped = rim_ref[d, i], turned(core)
            ext_ref[i] = jnp.where(lows, before, flipped).astype(jnp.bfloat16)
            ext_ref[SHIFT + i] = jnp.where(lows, rim, core).astype(jnp.bfloat16)
            ext_ref[2 * SHIFT + i] = jnp.where(lows, core, rim).astype(jnp.bfloat16)
            ext_ref[3 * SHIFT + i] = jnp.where(lows, flipped, after).astype(jnp.bfloat16)

    def migrate(big):
        totals = [[] for _ in range(4)]
        for top in range(0, SPLIT, 8):
            rows = slice(top, top + 8)
            data = [ext_ref[4 * big + n + 1, rows] for n in range(TAPS + 3)]
            for j in range(4):
                sums = []
                for first in range(2):
                    total = weight_ref[4 * big + j, first, rows] * data[j + first]
                    for tap in range(first + 2, TAPS, 2):
                        total += weight_ref[4 * big + j, tap, rows] * data[j + tap]
                    sums.append(total.astype(jnp.float32))
                totals[j].append(sums[0] + sums[1])
        return [jnp.concatenate(total, axis=0) for total in totals]

    def focus(step):
        compressed = []
        for big in range(2):
            for j, migrated in enumerate(migrate(2 * step + big)):
                g = 8 * step + 4 * big + j
                re, im = migrated[:, :LANES], migrated[:, LANES:]
                cos_phase, sin_phase = cos_ref[g], sin_ref[g]
                parts = [re * cos_phase - im * sin_phase, im * cos_phase + re * sin_phase]
                compressed.append(jnp.concatenate(parts, axis=1).astype(jnp.bfloat16))
        first = dot(jnp.concatenate(compressed, axis=0), back_right_ref[...])
        tc, ts = tc_ref[...], ts_ref[...]
        segments = []
        for j in range(8):
            rows = first[j * SPLIT : (j + 1) * SPLIT]
            re, im = rows[:, :LANES], rows[:, LANES:]
            segments.append(jnp.concatenate([re * tc - im * ts, im * tc + re * ts], axis=0))
        stacked = jnp.concatenate(segments, axis=1).astype(jnp.bfloat16)
        second = dot(back_left_ref[...], stacked).astype(jnp.bfloat16)
        return [second[:, j * LANES : (j + 1) * LANES] for j in range(8)]

    def focus_first(step, carry):
        for j, focused in enumerate(focus(step)):
            focused_ref[8 * step + j] = focused
        return carry

    def focus_last(step, carry):
        pieces = []
        for j, focused in enumerate(focus(step)):
            leading = focused.astype(jnp.float32)
            trailing = focused_ref[8 * step + j].astype(jnp.float32)
            lr, li = leading[:SPLIT], leading[SPLIT:]
            tr, ti = trailing[:SPLIT], trailing[SPLIT:]
            product = jnp.concatenate([lr * tr + li * ti, li * tr - lr * ti], axis=1)
            pieces.append(product.astype(jnp.bfloat16))
        products = [jnp.concatenate(pieces[4 * n : 4 * n + 4], axis=1) for n in range(2)]
        looked = dot(jnp.concatenate(products, axis=0), look_ref[...]).astype(jnp.bfloat16)
        for n in range(2):
            big, rows = 2 * step + n, slice(n * SPLIT, (n + 1) * SPLIT)
            own_ref[big] = looked[rows, :LANES]
            own_ref[HALO_CHUNKS + big] = looked[rows, LANES:]
            start_pair(look_copies(big))
        return carry

    send_all(1)
    arrive_all(0)
    forward_rim(0)
    arrive_all(2)
    send_all(3)
    forward_rim(1)
    arrive_all(1)
    forward_core(0)
    lax.fori_loop(0, GROUPS // 8, focus_first, 0)
    arrive_all(3)
    forward_core(1)
    lax.fori_loop(0, GROUPS // 8, focus_last, 0)

    def lines_of(*firsts):
        rows = []
        for chunk in (first + j for first in firsts for j in range(HALO_CHUNKS)):
            parts = [line_ref[chunk, pl.ds(p, patches, stride=2)] for p in range(4)]
            rows.append(jnp.concatenate(parts, axis=1))
        lines = jnp.concatenate(rows, axis=0).astype(jnp.bfloat16)
        results = [dot(lines, ref[...]) for ref in (azimuth_one_ref, azimuth_two_ref)]
        for n, first in enumerate(firsts):
            for j in range(HALO_CHUNKS):
                for r in range(4):
                    part = results[r // 2][(n * HALO_CHUNKS + j) * patches :][:patches]
                    part = part[:, (r % 2) * LANES : (r % 2 + 1) * LANES]
                    grid_ref[pl.ds(((first + j) * 4 + r) * patches, patches)] = part

    for j in range(CHUNKS):
        line_ref[HALO_CHUNKS + j, pl.ds(1, SPLIT)] = own_ref[j].astype(jnp.float32)
    lines_of(HALO_CHUNKS, 2 * HALO_CHUNKS)
    for k in range(2 * dates):
        sent_all(k)
    wait_pair(
        (
            neighbour(own_before_ref, own_before_ref, look_send.at[0], look_recv.at[0], 1),
            neighbour(own_after_ref, own_after_ref, look_send.at[1], look_recv.at[1], -1),
        )
    )
    for j in range(HALO_CHUNKS):
        line_ref[j, pl.ds(1, SPLIT)] = own_before_ref[j].astype(jnp.float32)
        line_ref[HALO_CHUNKS + CHUNKS + j, pl.ds(1, SPLIT)] = own_after_ref[j].astype(jnp.float32)
    lines_of(0, HALO_CHUNKS + CHUNKS)
    def filter_patches(step, carry):
        stacks = []
        for pair in range(2 * STEPS):
            one = grid_ref[pl.ds(4 * STEPS * step + 2 * pair, PATCH, stride=patches)]
            two = grid_ref[pl.ds(4 * STEPS * step + 2 * pair + 1, PATCH, stride=patches)]
            re = jnp.where(low, one, pltpu.roll(two, PATCH, 1))
            im = jnp.where(low, pltpu.roll(one, PATCH, 1), two)
            stacks.append(jnp.concatenate([re, im], axis=0).astype(jnp.bfloat16))
        spectra = dot(range_ref[...], jnp.concatenate(stacks, axis=1))
        parts, sums = [], []
        for pair in range(2 * STEPS):
            re = spectra[:PATCH, pair * LANES : (pair + 1) * LANES]
            im = spectra[PATCH:, pair * LANES : (pair + 1) * LANES]
            power = re * re + im * im + EPSILON
            magnitude = power * lax.rsqrt(power)
            rows = magnitude + pltpu.roll(magnitude, 1, 0) + pltpu.roll(magnitude, PATCH - 1, 0)
            parts.append((re, im))
            sums.append(rows.astype(jnp.bfloat16))
        boxes = dot(jnp.concatenate(sums, axis=0), smooth_ref[...])
        kept_re, kept_im = [], []
        for pair, (re, im) in enumerate(parts):
            box = boxes[pair * PATCH : (pair + 1) * PATCH]
            total = jnp.sum(box[:, LANES:], axis=0, keepdims=True)
            level = total * (1.0 / (3 * PATCH * PATCH)) + EPSILON
            gain = box[:, :LANES] * ((1.0 / 9.0) / level)
            kept_re.append((re * gain).astype(jnp.bfloat16))
            kept_im.append((im * gain).astype(jnp.bfloat16))
        kept = [
            jnp.concatenate(kept_re[2 * n : 2 * n + 2] + kept_im[2 * n : 2 * n + 2], axis=1)
            for n in range(STEPS)
        ]
        back = dot(jnp.concatenate(kept, axis=0), back_azimuth_ref[...]).astype(jnp.bfloat16)
        stacked = []
        for n in range(STEPS):
            rows = back[n * PATCH : (n + 1) * PATCH]
            stacked.append(jnp.concatenate([rows[:, :LANES], rows[:, LANES:]], axis=0))
        result = dot(back_range_ref[...], jnp.concatenate(stacked, axis=1))
        width = STEPS * LANES
        start = pl.multiple_of(step * width, width)
        out_ref[:, pl.ds(start, width)] = result.astype(jnp.bfloat16)
        return carry

    lax.fori_loop(0, patches // (4 * STEPS), filter_patches, 0, unroll=1)


def loading_kernel(*refs):
    held, out_ref, kept, load_sem = refs[:TABLES], refs[TABLES], refs[TABLES + 1 : -1], refs[-1]
    rows = held[0].shape[0] // SLABS
    slabs = [
        pltpu.make_async_copy(
            held[0].at[pl.ds(n * rows, rows)], kept[0].at[pl.ds(n * rows, rows)], load_sem.at[n]
        )
        for n in range(SLABS)
    ]
    loads = [
        pltpu.make_async_copy(held[i], kept[i], load_sem.at[SLABS - 1 + i])
        for i in range(1, TABLES)
    ]
    scene_kernel(*kept[:TABLES], out_ref, *kept[TABLES:], slabs, loads)


def table_stack(left):
    unit = 1.0 / SPLIT
    back_range = np.zeros((LANES, LANES))
    back_range[:PATCH] = back_range_table() * unit
    azimuth = patch_azimuth_table()
    return np.concatenate(
        [
            np.concatenate([left, left_table(-1.0) * unit], axis=1),
            np.concatenate([patch_range_table() * unit, back_range], axis=1),
            spectrum_side(right_table(1.0), 1) * unit,
            spectrum_side(right_table(-1.0), 0),
            look_table(),
            azimuth[:, : 2 * LANES],
            azimuth[:, 2 * LANES :],
            back_azimuth_table(),
            smooth_table(),
        ]
    )


def run_scene(raw, band, phase, left, scene, shape):
    dates, width = shape[1], shape[3]
    looks = SPLIT * SPLIT // LOOKS
    vmem = pl.BlockSpec(memory_space=pltpu.VMEM)
    plane = (GROUPS, SPLIT, LANES)
    ups, downs = (pltpu.VMEM((dates, n, SPLIT, LANES), jnp.bfloat16) for n in (UPS, DOWNS))
    looked_edge = pltpu.VMEM((HALO_CHUNKS, SPLIT, LANES), jnp.bfloat16)
    dma = pltpu.SemaphoreType.DMA
    twiddles = np.concatenate(twiddle_tables())
    tables = (raw, band, phase, bf16(table_stack(left)), jnp.asarray(twiddles))
    return pl.pallas_call(
        loading_kernel,
        in_specs=[pl.BlockSpec(memory_space=pl.ANY)] * TABLES,
        out_specs=vmem,
        out_shape=pltpu.VMEM((2 * STRIP, looks), jnp.bfloat16),
        scratch_shapes=[
            (pltpu.SMEM if table is band else pltpu.VMEM)(table.shape, table.dtype)
            for table in tables
        ]
        + [
            pltpu.VMEM((dates, 2, scene, 2, HALF, width), jnp.bfloat16),
            pltpu.VMEM(raw.shape, jnp.float32),
            pltpu.VMEM((dates, 2, scene, 2, HALF, width), jnp.bfloat16),
            pltpu.VMEM((STRIP * SPLIT // 2, LANES), jnp.float32),
            pltpu.VMEM((2, pl.cdiv(width, LANES), scene * HALF, LANES), jnp.float32),
            pltpu.VMEM((GROUPS, TAPS, SPLIT, 2 * LANES), jnp.bfloat16),
            pltpu.VMEM(plane, jnp.float32),
            pltpu.VMEM(plane, jnp.float32),
            pltpu.VMEM((GROUPS + 2 * SHIFT, SPLIT, 2 * LANES), jnp.bfloat16),
            pltpu.VMEM((dates, SHIFT, SPLIT, 2 * LANES), jnp.float32),
            ups, downs, ups, downs,
            pltpu.VMEM((GROUPS, 2 * SPLIT, LANES), jnp.bfloat16),
            pltpu.VMEM((CHUNKS, SPLIT, LANES), jnp.bfloat16),
            looked_edge,
            looked_edge,
            pltpu.VMEM((2 * CHUNKS, SPLIT + 8, LANES), jnp.float32),
            pltpu.VMEM((PATCH * SPLIT // 2, LANES), jnp.float32),
            dma((2 * dates,)), dma((2 * dates,)),
            dma((dates, 2)), dma((dates, 2)), dma((2,)), dma((2,)), dma((SLABS - 1 + TABLES,)),
        ],
        compiler_params=pltpu.CompilerParams(
            vmem_limit_bytes=VMEM_LIMIT, collective_id=0, has_side_effects=True
        ),
        name="scene",
    )(*[pltpu.with_memory_space_constraint(t, pltpu.HBM) for t in tables])


def on_device(raw_echoes, azimuth_phase, band_offset, partners):
    scene = lax.axis_size("scene")
    dates = raw_echoes.shape[2]
    local = raw_echoes.shape[0] // SPLIT
    pairs = partners.size
    assert dates == 2 and raw_echoes.shape[3] == scene * STRIP
    left = left_table(1.0).reshape(2 * SPLIT, 2, scene, local)
    left = left.transpose(0, 1, 3, 2).reshape(2 * SPLIT, 2 * SPLIT)
    lines, bins = raw_echoes.shape[0], raw_echoes.shape[3]
    raw = raw_echoes.reshape(lines, 2, dates, bins // LANES, LANES)
    raw = raw.transpose(0, 1, 3, 2, 4).reshape(-1, LANES)
    phase = azimuth_phase.T
    result = run_scene(
        raw, band_offset, phase, left, scene, (2, dates, bins, lines)
    )
    result = jnp.broadcast_to(result, (pairs,) + result.shape)
    return result.reshape(pairs, 2, STRIP, -1).transpose(0, 3, 1, 2)


def solution(mesh):
    return jax.shard_map(
        on_device,
        mesh=mesh,
        in_specs=(
            P("scene", None, "stack", None),
            P("stack", "scene"),
            P(("stack", "scene")),
            P("stack", None),
        ),
        out_specs=P("stack", None, None, "scene"),
        check_vma=False,
    )
```

```python
import math

import jax
import jax.numpy as jnp
import numpy as np
from jax import lax
from jax.experimental import pallas as pl
from jax.experimental.pallas import tpu as pltpu
from jax.sharding import PartitionSpec as P

SPLIT = 64
LOOKS = 4
PATCH = 64
SHIFT = 8
TAPS = 2 * SHIFT - 1
EPSILON = 1e-06
STRIP = 32
GROUPS = STRIP // 2
LANES = 2 * SPLIT
CHUNKS = STRIP // 4
HALO_CHUNKS = CHUNKS // 2
HALF = STRIP // 2
HALF_LANES = 32
UPS, DOWNS = SHIFT - 2, SHIFT - 3
STEPS = 8
TABLES = 5
SLABS = 4
VMEM_LIMIT = 40 * 1024 * 1024


def base_tables():
    k = np.arange(64)
    angle = 2.0 * np.pi * ((k[:, None] * k[None, :]) % 64) / 64.0
    return np.cos(angle), np.sin(angle)


def twiddle_tables():
    k = np.arange(SPLIT)
    angle = 2.0 * np.pi * ((k[:, None] * k[None, :]) % (SPLIT * SPLIT)) / (SPLIT * SPLIT)
    return (
        np.tile(np.cos(angle), (1, 2)).astype(np.float32),
        np.tile(np.sin(angle), (1, 2)).astype(np.float32),
    )


def bf16(table):
    return jnp.asarray(np.asarray(table, np.float32), jnp.bfloat16)


def left_table(direction):
    c, s = base_tables()
    return np.block([[c, direction * s], [-direction * s, c]])


def right_table(direction):
    c, s = base_tables()
    eye = np.eye(2)
    return np.block(
        [
            [np.kron(eye, c), np.kron(eye, -direction * s)],
            [np.kron(eye, direction * s), np.kron(eye, c)],
        ]
    )


def look_table():
    table = np.zeros((4, 2, 2, SPLIT, 2, 4, 2, SPLIT // LOOKS))
    for g in range(4):
        for c in range(2):
            for rb in range(2):
                for q in range(SPLIT):
                    table[g, c, rb, q, rb, g, c, q // LOOKS] = 1.0 / LOOKS
    return table.reshape(4 * 2 * 2 * SPLIT, 2 * 4 * 2 * SPLIT // LOOKS)


def patch_azimuth_table():
    c, s = base_tables()
    table = np.zeros((4, 4, 2, 16, 4, 2, 64))
    for p in range(4):
        part_c, part_s = c[16 * p : 16 * p + 16], s[16 * p : 16 * p + 16]
        for r in range(4):
            table[p, r, 0, :, r, 0] = part_c
            table[p, r, 1, :, r, 0] = part_s
            table[p, r, 0, :, r, 1] = -part_s
            table[p, r, 1, :, r, 1] = part_c
    return table.reshape(512, 512)


def patch_range_table():
    c, s = base_tables()
    return np.block([[c, s], [-s, c]])


def smooth_table():
    k = np.arange(PATCH)
    gap = (k[:, None] - k[None, :]) % PATCH
    near = ((gap <= 1) | (gap == PATCH - 1)).astype(np.float64)
    eye = np.eye(2)
    return np.concatenate([np.kron(eye, near), np.kron(eye, np.ones((PATCH, PATCH)))], axis=1)


def back_azimuth_table():
    c, s = base_tables()
    c, s = c[:, 16:48], s[:, 16:48]
    table = np.zeros((2, 4, 64, 2, 4, 32))
    for i in range(4):
        table[0, i, :, 0, i] = c
        table[1, i, :, 0, i] = -s
        table[0, i, :, 1, i] = s
        table[1, i, :, 1, i] = c
    return table.reshape(512, 256)


def back_range_table():
    c, s = base_tables()
    c, s = c[16:48], s[16:48]
    return np.block([[c, -s], [s, c]])


def dot(a, b):
    return jnp.dot(a, b, preferred_element_type=jnp.float32)


def lane_order():
    quarter = SPLIT // 4
    places = np.arange(SPLIT // 2)
    fast = places[quarter // 2 : 3 * quarter // 2]
    slow = np.concatenate([places[: quarter // 2], places[3 * quarter // 2 :]])
    return np.concatenate([2 * fast, 2 * fast + 1, 2 * slow, 2 * slow + 1])


def spectrum_side(table, axis):
    order = np.concatenate([SPLIT * half + lane_order() for half in range(4)])
    return np.take(table, order, axis=axis)


def cos_sin(angle):
    h = 0.5 * angle
    h2 = h * h
    sin_h = 1.0 / 6227020800.0
    for fact in (-39916800.0, 362880.0, -5040.0, 120.0, -6.0, 1.0):
        sin_h = sin_h * h2 + 1.0 / fact
    sin_h = sin_h * h
    cos_h = 1.0 / 479001600.0
    for fact in (-3628800.0, 40320.0, -720.0, 24.0, -2.0, 1.0):
        cos_h = cos_h * h2 + 1.0 / fact
    return 1.0 - 2.0 * sin_h * sin_h, 2.0 * sin_h * cos_h


def make_weights(g, band_ref, lines_ref, weight_ref, cos_ref, sin_ref):
    shape = (SPLIT, LANES)
    lane = lax.broadcasted_iota(jnp.int32, shape, 1)
    row = lax.broadcasted_iota(jnp.int32, shape, 0)
    quarter = SPLIT // 4
    place, odd = lane & (quarter - 1), (lane & quarter) // quarter
    slow = jnp.where(place < quarter // 2, place, place + quarter)
    place = jnp.where((lane & (2 * quarter)) != 0, slow, place + quarter // 2)
    k = row + SPLIT * (2 * place + odd)
    total = SPLIT * SPLIT
    f = jnp.where(k < total // 2, k, k - total).astype(jnp.float32)
    ratio = f * (2.0 / total)
    band = jnp.where(lane < SPLIT, band_ref[g], band_ref[g + GROUPS]).astype(jnp.float32)
    s = band * (ratio * ratio - 0.5)
    n = jnp.floor(s + 0.5)
    y = s - n
    y2 = y * y
    pi = math.pi
    poly = -(pi**11) / 39916800.0
    for power, fact in ((9, 362880.0), (7, -5040.0), (5, 120.0), (3, -6.0), (1, 1.0)):
        poly = poly * y2 + (pi**power) / fact
    odd = n.astype(jnp.int32) & 1
    lobe = jnp.where(odd == 1, 1.0, -1.0) * (y * poly) * (1.0 / pi)
    cos_s, sin_s = cos_sin(s * (pi / 4.0))
    cos_s, sin_s = 0.5 * cos_s, 0.5 * sin_s
    for tap in range(TAPS):
        m = tap + 1 - SHIFT
        x = m - s
        sign = 1.0 if m % 2 == 0 else -1.0
        safe = jnp.where(x == 0.0, 1.0, x)
        sinc = jnp.where(x == 0.0, 1.0, (sign * lobe) / safe)
        window = 0.5 + math.cos(pi * m / 4.0) * cos_s + math.sin(pi * m / 4.0) * sin_s
        weight = jnp.where(jnp.abs(x) < SHIFT / 2.0, sinc * window, 0.0)
        weight_ref[g, tap] = jnp.concatenate([weight, weight], axis=1).astype(jnp.bfloat16)
    first = lines_ref[pl.ds(g, SPLIT // 2, stride=STRIP)]
    second = lines_ref[pl.ds(g + GROUPS, SPLIT // 2, stride=STRIP)]
    cuts = (0, quarter // 2, 3 * quarter // 2, SPLIT // 2)
    pieces = []
    for even in (first, second):
        both = (even, pltpu.roll(even, SPLIT, 1))
        thirds = [[part[a:b] for a, b in zip(cuts, cuts[1:])] for part in both]
        pieces += [thirds[0][1], thirds[1][1]]
        pieces += [thirds[0][0], thirds[0][2], thirds[1][0], thirds[1][2]]
    angle = jnp.concatenate(pieces, axis=0).T[:SPLIT]
    cos_ref[g], sin_ref[g] = cos_sin(angle)


def arrived_lines(wide_ref, i, sources, local, low):
    rows = []
    for c in range(2):
        for pair in range(wide_ref.shape[1]):
            one = wide_ref[c, pair, pl.ds(i, sources, stride=HALF)]
            two = wide_ref[c, pair, pl.ds(i + SHIFT, sources, stride=HALF)]
            rows.append(jnp.where(low[:sources], one, pltpu.roll(two, SPLIT, 1)))
            if local > 1:
                rows.append(jnp.where(low[:sources], pltpu.roll(one, SPLIT, 1), two))
    return jnp.concatenate(rows, axis=0).astype(jnp.bfloat16)


def scene_kernel(
    packed_ref, band_ref, phase_ref, table_ref, twiddle_ref,
    out_ref,
    raw_ref, spread_ref, recv_ref, lines_ref, wide_ref, weight_ref, cos_ref, sin_ref, ext_ref,
    rim_ref, core_ref, up_ref, down_ref, before_ref, after_ref, focused_ref,
    own_ref, own_before_ref, own_after_ref, line_ref, grid_ref,
    send_sem, recv_sem, edge_send, edge_recv, look_send, look_recv,
    slabs, loads,
):
    scene = lax.axis_size("scene")
    me = lax.axis_index("scene")
    dates = raw_ref.shape[0]
    lines_held = raw_ref.shape[5]
    local = lines_held // SPLIT
    low = lax.broadcasted_iota(jnp.int32, (SPLIT, LANES), 1) < SPLIT
    lows = jnp.concatenate([low, low], axis=1)
    fast = lax.broadcasted_iota(jnp.int32, (SPLIT, LANES), 1) % SPLIT < HALF_LANES
    patches = SPLIT // 2

    left_ref, back_left_ref, range_ref, back_range_ref = (
        table_ref.at[rows, columns] for rows, columns in (
            (pl.ds(0, LANES), pl.ds(0, LANES)), (pl.ds(0, LANES), pl.ds(LANES, LANES)),
            (pl.ds(LANES, LANES), pl.ds(0, LANES)), (pl.ds(LANES, PATCH), pl.ds(LANES, LANES)),
        )
    )
    wide = 2 * LANES
    starts = np.cumsum([wide, wide, wide, 4 * wide, 2 * wide, 2 * wide, 2 * wide]).tolist()
    (
        right_ref, back_right_ref, look_ref, azimuth_one_ref, azimuth_two_ref,
        back_azimuth_ref, smooth_ref,
    ) = (
        table_ref.at[pl.ds(start, rows)]
        for start, rows in zip(starts, (wide, wide, 4 * wide, 2 * wide, 2 * wide, 2 * wide, LANES))
    )
    tc_ref, ts_ref = twiddle_ref.at[pl.ds(0, SPLIT)], twiddle_ref.at[pl.ds(SPLIT, SPLIT)]

    for slab in slabs:
        slab.start()
    barrier = pltpu.get_barrier_semaphore()

    def greet(o, carry):
        pl.semaphore_signal(
            barrier, inc=1, device_id={"scene": lax.rem(me + o, scene)},
            device_id_type=pl.DeviceIdType.MESH,
        )
        return carry

    lax.fori_loop(1, scene, greet, 0, unroll=True)
    piece = packed_ref.shape[0] // (2 * SLABS)
    for n, slab in enumerate(slabs):
        slab.wait()
        for half in range(2):
            rows = pl.ds((2 * n + half) * piece, piece)
            spread_ref[rows] = packed_ref[rows].astype(jnp.float32)
    for load in loads:
        load.start()
    owners = LANES // STRIP
    tiles = scene // owners
    stride = 2 * tiles * dates

    def piece_of(ref, k, owner):
        return ref.at[k // 2, k % 2, owner]

    def strip_copy(k, peer):
        return pltpu.make_async_remote_copy(
            src_ref=piece_of(raw_ref, k, peer),
            dst_ref=piece_of(recv_ref, k, me),
            send_sem=send_sem.at[k],
            recv_sem=recv_sem.at[k],
            device_id={"scene": peer},
            device_id_type=pl.DeviceIdType.MESH,
        )

    def own_copy(k):
        return pltpu.make_async_copy(
            piece_of(raw_ref, k, me), piece_of(recv_ref, k, me), recv_sem.at[k]
        )

    def turn(d, tile):
        for c in range(2):
            start = (c * tiles + tile) * dates + d
            bins = spread_ref[pl.ds(start, lines_held, stride=stride)].T
            for n in range(owners):
                own = bins[n * STRIP : (n + 1) * STRIP]
                rim = jnp.concatenate([own[:SHIFT], own[STRIP - SHIFT :]], axis=0)
                core = own[SHIFT : STRIP - SHIFT]
                raw_ref[d, 0, tile * owners + n, c] = rim.astype(jnp.bfloat16)
                raw_ref[d, 1, tile * owners + n, c] = core.astype(jnp.bfloat16)

    def turn_and_send(d):
        def body(i, carry):
            tile = lax.rem(me // owners + tiles // 2 + i, tiles)
            turn(d, tile)

            @pl.when(i == 0)
            def _():
                if d == 0:
                    pl.semaphore_wait(barrier, scene - 1)

            for n in range(owners):
                peer = tile * owners + n

                @pl.when(peer != me)
                def _():
                    strip_copy(2 * d, peer).start()

            return carry

        lax.fori_loop(0, tiles, body, 0)
        own_copy(2 * d).start()

    def far(i):
        half = (i + 1) // 2
        return scene // 2 + half * (1 - 2 * lax.rem(i, 2))

    def send_all(k):
        def send(i, carry):
            strip_copy(k, lax.rem(me + far(i), scene)).start()
            return carry

        lax.fori_loop(0, scene - 1, send, 0)
        own_copy(k).start()

    def arrive_all(k):
        held = recv_ref.at[k // 2, k % 2]
        pltpu.make_async_copy(held, held, recv_sem.at[k]).wait()

    def sent_all(k):
        held = raw_ref.at[k // 2, k % 2, pl.ds(0, scene - 1)]
        pltpu.make_async_copy(held, held, send_sem.at[k]).wait()

    for d in range(dates):
        turn_and_send(d)

    for load in loads:
        load.wait()

    for part in range(SPLIT // 2):
        lines_ref[pl.ds(part * STRIP, STRIP)] = phase_ref[:, part * LANES : (part + 1) * LANES]

    def weigh(g, carry):
        make_weights(g, band_ref, lines_ref, weight_ref, cos_ref, sin_ref)
        return carry

    lax.fori_loop(0, GROUPS, weigh, 0)

    @pl.when(me == 0)
    def _():
        before_ref[...] = jnp.zeros(before_ref.shape, before_ref.dtype)
        own_before_ref[...] = jnp.zeros(own_before_ref.shape, own_before_ref.dtype)

    @pl.when(me == scene - 1)
    def _():
        after_ref[...] = jnp.zeros(after_ref.shape, after_ref.dtype)
        own_after_ref[...] = jnp.zeros(own_after_ref.shape, own_after_ref.dtype)

    line_ref[...] = jnp.zeros(line_ref.shape, jnp.float32)

    def neighbour(source, target, send, recv, step):
        return pltpu.make_async_remote_copy(
            src_ref=source, dst_ref=target, send_sem=send, recv_sem=recv,
            device_id={"scene": me + step}, device_id_type=pl.DeviceIdType.MESH,
        )

    def edge_copies(d):
        return (
            neighbour(
                up_ref.at[d], before_ref.at[d], edge_send.at[d, 0], edge_recv.at[d, 0], 1,
            ),
            neighbour(
                down_ref.at[d], after_ref.at[d], edge_send.at[d, 1], edge_recv.at[d, 1], -1,
            ),
        )

    def look_copies(big):
        return (
            neighbour(
                own_ref.at[HALO_CHUNKS + big], own_before_ref.at[big],
                look_send.at[0], look_recv.at[0], 1,
            ),
            neighbour(
                own_ref.at[big], own_after_ref.at[big],
                look_send.at[1], look_recv.at[1], -1,
            ),
        )

    def start_pair(copies):
        @pl.when(me < scene - 1)
        def _():
            copies[0].start()

        @pl.when(me > 0)
        def _():
            copies[1].start()

    def wait_pair(copies):
        @pl.when(me > 0)
        def _():
            copies[0].wait_recv()
            copies[1].wait_send()

        @pl.when(me < scene - 1)
        def _():
            copies[1].wait_recv()
            copies[0].wait_send()

    def widen(d, part):
        def body(source, carry):
            start = pl.multiple_of(source * HALF, HALF)
            for c in range(2):
                strip = recv_ref[d, part, source, c].astype(jnp.float32)
                for pair in range(wide_ref.shape[1]):
                    kept = strip[:, pair * LANES : (pair + 1) * LANES]
                    wide_ref[c, pair, pl.ds(start, HALF), : kept.shape[1]] = kept
            return carry

        lax.fori_loop(0, scene, body, 0)

    def transform(first, count):
        held = [arrived_lines(wide_ref, first + n, scene, local, low) for n in range(count)]
        mixed = dot(left_ref[...], jnp.concatenate(held, axis=1))
        tc, ts = tc_ref[...], ts_ref[...]
        segments = []
        for n in range(count):
            re, im = (mixed[k : k + SPLIT, n * LANES : (n + 1) * LANES] for k in (0, SPLIT))
            segments.append(jnp.concatenate([re * tc + im * ts, im * tc - re * ts], axis=1))
        stacked = jnp.concatenate(segments, axis=0).astype(jnp.bfloat16)
        spectra = dot(stacked, right_ref[...])
        return [spectra[n * SPLIT : (n + 1) * SPLIT] for n in range(count)]

    def turned(pair):
        parts = (pair[:, :LANES], pair[:, LANES:])
        return jnp.concatenate([pltpu.roll(part, SPLIT, 1) for part in parts], axis=1)

    def forward_rim(d):
        widen(d, 0)

        ups, downs = [], []
        for i, rim in enumerate(transform(0, SHIFT)):
            flipped = turned(rim)
            rim_ref[d, i] = rim
            downs.append(jnp.where(low, rim[:, :LANES], flipped[:, LANES:]))
            ups.append(jnp.where(low, flipped[:, :LANES], rim[:, LANES:]))
        ups = [jnp.where(fast, pltpu.roll(ups[2], LANES - HALF_LANES, 1), ups[1])] + ups[3:]
        downs = downs[:3] + [
            jnp.where(fast, downs[i], pltpu.roll(downs[i + 1], HALF_LANES, 1)) for i in (3, 5)
        ]
        for n, up in enumerate(ups):
            up_ref[d, n] = up.astype(jnp.bfloat16)
        for n, down in enumerate(downs):
            down_ref[d, n] = down.astype(jnp.bfloat16)
        start_pair(edge_copies(d))

    def forward_core(d):
        widen(d, 1)
        if d == 0:
            for i, core in enumerate(transform(0, SHIFT)):
                core_ref[i] = core
        wait_pair(edge_copies(d))
        cores = [core_ref[i] for i in range(SHIFT)] if d == 0 else transform(0, SHIFT)
        befores = [before_ref[d, n].astype(jnp.float32) for n in range(UPS)]
        befores = [befores[0], befores[0], pltpu.roll(befores[0], HALF_LANES, 1)] + befores[1:]
        afters = [after_ref[d, n].astype(jnp.float32) for n in range(DOWNS)]
        afters = afters[:3] + [
            part for after in afters[3:]
            for part in (after, pltpu.roll(after, LANES - HALF_LANES, 1))
        ]
        afters.append(afters[-1])
        for i, core in enumerate(cores):
            before = jnp.concatenate([befores[i], pltpu.roll(befores[i], SPLIT, 1)], axis=1)
            after = jnp.concatenate([pltpu.roll(afters[i], SPLIT, 1), afters[i]], axis=1)
            rim, flipped = rim_ref[d, i], turned(core)
            ext_ref[i] = jnp.where(lows, before, flipped).astype(jnp.bfloat16)
            ext_ref[SHIFT + i] = jnp.where(lows, rim, core).astype(jnp.bfloat16)
            ext_ref[2 * SHIFT + i] = jnp.where(lows, core, rim).astype(jnp.bfloat16)
            ext_ref[3 * SHIFT + i] = jnp.where(lows, flipped, after).astype(jnp.bfloat16)

    def migrate(big):
        totals = [[] for _ in range(4)]
        for top in range(0, SPLIT, 8):
            rows = slice(top, top + 8)
            data = [ext_ref[4 * big + n + 1, rows] for n in range(TAPS + 3)]
            for j in range(4):
                sums = []
                for first in range(2):
                    total = weight_ref[4 * big + j, first, rows] * data[j + first]
                    for tap in range(first + 2, TAPS, 2):
                        total += weight_ref[4 * big + j, tap, rows] * data[j + tap]
                    sums.append(total.astype(jnp.float32))
                totals[j].append(sums[0] + sums[1])
        return [jnp.concatenate(total, axis=0) for total in totals]

    def focus(step):
        compressed = []
        for big in range(2):
            for j, migrated in enumerate(migrate(2 * step + big)):
                g = 8 * step + 4 * big + j
                re, im = migrated[:, :LANES], migrated[:, LANES:]
                cos_phase, sin_phase = cos_ref[g], sin_ref[g]
                parts = [re * cos_phase - im * sin_phase, im * cos_phase + re * sin_phase]
                compressed.append(jnp.concatenate(parts, axis=1).astype(jnp.bfloat16))
        first = dot(jnp.concatenate(compressed, axis=0), back_right_ref[...])
        tc, ts = tc_ref[...], ts_ref[...]
        segments = []
        for j in range(8):
            rows = first[j * SPLIT : (j + 1) * SPLIT]
            re, im = rows[:, :LANES], rows[:, LANES:]
            segments.append(jnp.concatenate([re * tc - im * ts, im * tc + re * ts], axis=0))
        stacked = jnp.concatenate(segments, axis=1).astype(jnp.bfloat16)
        second = dot(back_left_ref[...], stacked).astype(jnp.bfloat16)
        return [second[:, j * LANES : (j + 1) * LANES] for j in range(8)]

    def focus_first(step, carry):
        for j, focused in enumerate(focus(step)):
            focused_ref[8 * step + j] = focused
        return carry

    def focus_last(step, carry):
        pieces = []
        for j, focused in enumerate(focus(step)):
            leading = focused.astype(jnp.float32)
            trailing = focused_ref[8 * step + j].astype(jnp.float32)
            lr, li = leading[:SPLIT], leading[SPLIT:]
            tr, ti = trailing[:SPLIT], trailing[SPLIT:]
            product = jnp.concatenate([lr * tr + li * ti, li * tr - lr * ti], axis=1)
            pieces.append(product.astype(jnp.bfloat16))
        products = [jnp.concatenate(pieces[4 * n : 4 * n + 4], axis=1) for n in range(2)]
        looked = dot(jnp.concatenate(products, axis=0), look_ref[...]).astype(jnp.bfloat16)
        for n in range(2):
            big, rows = 2 * step + n, slice(n * SPLIT, (n + 1) * SPLIT)
            own_ref[big] = looked[rows, :LANES]
            own_ref[HALO_CHUNKS + big] = looked[rows, LANES:]
            start_pair(look_copies(big))
        return carry

    send_all(1)
    arrive_all(0)
    forward_rim(0)
    send_all(3)
    arrive_all(2)
    forward_rim(1)
    arrive_all(1)
    forward_core(0)
    lax.fori_loop(0, GROUPS // 8, focus_first, 0)
    arrive_all(3)
    forward_core(1)
    lax.fori_loop(0, GROUPS // 8, focus_last, 0)

    def lines_of(*firsts):
        rows = []
        for chunk in (first + j for first in firsts for j in range(HALO_CHUNKS)):
            parts = [line_ref[chunk, pl.ds(p, patches, stride=2)] for p in range(4)]
            rows.append(jnp.concatenate(parts, axis=1))
        lines = jnp.concatenate(rows, axis=0).astype(jnp.bfloat16)
        results = [dot(lines, ref[...]) for ref in (azimuth_one_ref, azimuth_two_ref)]
        for n, first in enumerate(firsts):
            for j in range(HALO_CHUNKS):
                for r in range(4):
                    part = results[r // 2][(n * HALO_CHUNKS + j) * patches :][:patches]
                    part = part[:, (r % 2) * LANES : (r % 2 + 1) * LANES]
                    grid_ref[pl.ds(((first + j) * 4 + r) * patches, patches)] = part

    for j in range(CHUNKS):
        line_ref[HALO_CHUNKS + j, pl.ds(1, SPLIT)] = own_ref[j].astype(jnp.float32)
    lines_of(HALO_CHUNKS, 2 * HALO_CHUNKS)
    for k in range(2 * dates):
        sent_all(k)
    wait_pair(
        (
            neighbour(own_before_ref, own_before_ref, look_send.at[0], look_recv.at[0], 1),
            neighbour(own_after_ref, own_after_ref, look_send.at[1], look_recv.at[1], -1),
        )
    )
    for j in range(HALO_CHUNKS):
        line_ref[j, pl.ds(1, SPLIT)] = own_before_ref[j].astype(jnp.float32)
        line_ref[HALO_CHUNKS + CHUNKS + j, pl.ds(1, SPLIT)] = own_after_ref[j].astype(jnp.float32)
    lines_of(0, HALO_CHUNKS + CHUNKS)
    def filter_patches(step, carry):
        stacks = []
        for pair in range(2 * STEPS):
            one = grid_ref[pl.ds(4 * STEPS * step + 2 * pair, PATCH, stride=patches)]
            two = grid_ref[pl.ds(4 * STEPS * step + 2 * pair + 1, PATCH, stride=patches)]
            re = jnp.where(low, one, pltpu.roll(two, PATCH, 1))
            im = jnp.where(low, pltpu.roll(one, PATCH, 1), two)
            stacks.append(jnp.concatenate([re, im], axis=0).astype(jnp.bfloat16))
        spectra = dot(range_ref[...], jnp.concatenate(stacks, axis=1))
        parts, sums = [], []
        for pair in range(2 * STEPS):
            re = spectra[:PATCH, pair * LANES : (pair + 1) * LANES]
            im = spectra[PATCH:, pair * LANES : (pair + 1) * LANES]
            power = re * re + im * im + EPSILON
            magnitude = power * lax.rsqrt(power)
            rows = magnitude + pltpu.roll(magnitude, 1, 0) + pltpu.roll(magnitude, PATCH - 1, 0)
            parts.append((re, im))
            sums.append(rows.astype(jnp.bfloat16))
        boxes = dot(jnp.concatenate(sums, axis=0), smooth_ref[...])
        kept_re, kept_im = [], []
        for pair, (re, im) in enumerate(parts):
            box = boxes[pair * PATCH : (pair + 1) * PATCH]
            total = jnp.sum(box[:, LANES:], axis=0, keepdims=True)
            level = total * (1.0 / (3 * PATCH * PATCH)) + EPSILON
            gain = box[:, :LANES] * ((1.0 / 9.0) / level)
            kept_re.append((re * gain).astype(jnp.bfloat16))
            kept_im.append((im * gain).astype(jnp.bfloat16))
        kept = [
            jnp.concatenate(kept_re[2 * n : 2 * n + 2] + kept_im[2 * n : 2 * n + 2], axis=1)
            for n in range(STEPS)
        ]
        back = dot(jnp.concatenate(kept, axis=0), back_azimuth_ref[...]).astype(jnp.bfloat16)
        stacked = []
        for n in range(STEPS):
            rows = back[n * PATCH : (n + 1) * PATCH]
            stacked.append(jnp.concatenate([rows[:, :LANES], rows[:, LANES:]], axis=0))
        result = dot(back_range_ref[...], jnp.concatenate(stacked, axis=1))
        width = STEPS * LANES
        start = pl.multiple_of(step * width, width)
        out_ref[:, pl.ds(start, width)] = result.astype(jnp.bfloat16)
        return carry

    lax.fori_loop(0, patches // (4 * STEPS), filter_patches, 0, unroll=1)


def loading_kernel(*refs):
    held, out_ref, kept, load_sem = refs[:TABLES], refs[TABLES], refs[TABLES + 1 : -1], refs[-1]
    rows = held[0].shape[0] // SLABS
    slabs = [
        pltpu.make_async_copy(
            held[0].at[pl.ds(n * rows, rows)], kept[0].at[pl.ds(n * rows, rows)], load_sem.at[n]
        )
        for n in range(SLABS)
    ]
    loads = [
        pltpu.make_async_copy(held[i], kept[i], load_sem.at[SLABS - 1 + i])
        for i in range(1, TABLES)
    ]
    scene_kernel(*kept[:TABLES], out_ref, *kept[TABLES:], slabs, loads)


def table_stack(left):
    unit = 1.0 / SPLIT
    back_range = np.zeros((LANES, LANES))
    back_range[:PATCH] = back_range_table() * unit
    azimuth = patch_azimuth_table()
    return np.concatenate(
        [
            np.concatenate([left, left_table(-1.0) * unit], axis=1),
            np.concatenate([patch_range_table() * unit, back_range], axis=1),
            spectrum_side(right_table(1.0), 1) * unit,
            spectrum_side(right_table(-1.0), 0),
            look_table(),
            azimuth[:, : 2 * LANES],
            azimuth[:, 2 * LANES :],
            back_azimuth_table(),
            smooth_table(),
        ]
    )


def run_scene(raw, band, phase, left, scene, shape):
    dates, width = shape[1], shape[3]
    looks = SPLIT * SPLIT // LOOKS
    vmem = pl.BlockSpec(memory_space=pltpu.VMEM)
    plane = (GROUPS, SPLIT, LANES)
    ups, downs = (pltpu.VMEM((dates, n, SPLIT, LANES), jnp.bfloat16) for n in (UPS, DOWNS))
    looked_edge = pltpu.VMEM((HALO_CHUNKS, SPLIT, LANES), jnp.bfloat16)
    dma = pltpu.SemaphoreType.DMA
    twiddles = np.concatenate(twiddle_tables())
    tables = (raw, band, phase, bf16(table_stack(left)), jnp.asarray(twiddles))
    return pl.pallas_call(
        loading_kernel,
        in_specs=[pl.BlockSpec(memory_space=pl.ANY)] * TABLES,
        out_specs=vmem,
        out_shape=pltpu.VMEM((2 * STRIP, looks), jnp.bfloat16),
        scratch_shapes=[
            (pltpu.SMEM if table is band else pltpu.VMEM)(table.shape, table.dtype)
            for table in tables
        ]
        + [
            pltpu.VMEM((dates, 2, scene, 2, HALF, width), jnp.bfloat16),
            pltpu.VMEM(raw.shape, jnp.float32),
            pltpu.VMEM((dates, 2, scene, 2, HALF, width), jnp.bfloat16),
            pltpu.VMEM((STRIP * SPLIT // 2, LANES), jnp.float32),
            pltpu.VMEM((2, pl.cdiv(width, LANES), scene * HALF, LANES), jnp.float32),
            pltpu.VMEM((GROUPS, TAPS, SPLIT, 2 * LANES), jnp.bfloat16),
            pltpu.VMEM(plane, jnp.float32),
            pltpu.VMEM(plane, jnp.float32),
            pltpu.VMEM((GROUPS + 2 * SHIFT, SPLIT, 2 * LANES), jnp.bfloat16),
            pltpu.VMEM((dates, SHIFT, SPLIT, 2 * LANES), jnp.float32),
            pltpu.VMEM((SHIFT, SPLIT, 2 * LANES), jnp.float32),
            ups, downs, ups, downs,
            pltpu.VMEM((GROUPS, 2 * SPLIT, LANES), jnp.bfloat16),
            pltpu.VMEM((CHUNKS, SPLIT, LANES), jnp.bfloat16),
            looked_edge,
            looked_edge,
            pltpu.VMEM((2 * CHUNKS, SPLIT + 8, LANES), jnp.float32),
            pltpu.VMEM((PATCH * SPLIT // 2, LANES), jnp.float32),
            dma((2 * dates,)), dma((2 * dates,)),
            dma((dates, 2)), dma((dates, 2)), dma((2,)), dma((2,)), dma((SLABS - 1 + TABLES,)),
        ],
        compiler_params=pltpu.CompilerParams(
            vmem_limit_bytes=VMEM_LIMIT, collective_id=0, has_side_effects=True
        ),
        name="scene",
    )(*[pltpu.with_memory_space_constraint(t, pltpu.HBM) for t in tables])


def on_device(raw_echoes, azimuth_phase, band_offset, partners):
    scene = lax.axis_size("scene")
    dates = raw_echoes.shape[2]
    local = raw_echoes.shape[0] // SPLIT
    pairs = partners.size
    assert dates == 2 and raw_echoes.shape[3] == scene * STRIP
    left = left_table(1.0).reshape(2 * SPLIT, 2, scene, local)
    left = left.transpose(0, 1, 3, 2).reshape(2 * SPLIT, 2 * SPLIT)
    lines, bins = raw_echoes.shape[0], raw_echoes.shape[3]
    raw = raw_echoes.reshape(lines, 2, dates, bins // LANES, LANES)
    raw = raw.transpose(0, 1, 3, 2, 4).reshape(-1, LANES)
    phase = azimuth_phase.T
    result = run_scene(
        raw, band_offset, phase, left, scene, (2, dates, bins, lines)
    )
    result = jnp.broadcast_to(result, (pairs,) + result.shape)
    return result.reshape(pairs, 2, STRIP, -1).transpose(0, 3, 1, 2)


def solution(mesh):
    return jax.shard_map(
        on_device,
        mesh=mesh,
        in_specs=(
            P("scene", None, "stack", None),
            P("stack", "scene"),
            P(("stack", "scene")),
            P("stack", None),
        ),
        out_specs=P("stack", None, None, "scene"),
        check_vma=False,
    )
```
